32 devices in a mesh: rows: 16 (over z, x, core), cols: 2 (over y).
Axes of the slice: x: 2, y: 2, z: 4, core: 2. Of those that a mesh axis runs over, the one named last changes fastest.
Arguments:
- unfolding: float32 [8192, 4096], P('rows', 'cols'), may hold values from -6 to 6
- pattern: int32 [32, 2], P('cols'), may hold values from 0 to 1, as said below
- sign_bits: int32 [4096, 2], P('cols'), may hold values from 0 to 1
Outputs:
- core_scaled: float32 [8192, 256], P('rows')
- next_unfolding: float32 [2048, 512], P('rows', 'cols')
The draws below stay inside these ranges and needn't reach their ends.
Inputs may be any that keep to these rules, and one draw needn't show every extreme that they name: Every row and every column of pattern holds at least one 1, and some entry is 0.
All inputs are finite; a program needn't handle non-finite values.
Results may differ from the reference program's by a relative error of at most 0.00017.
Values sent between devices are 32-bit elements; how exact they have to be, the bound alone decides.
No kernel may reach another device: no remote copies, remote signals or barrier semaphores. Data moves between devices by JAX's collectives and lax.ppermute only.
A program may use at most 64 MiB of HBM per device.

```python
import math
import jax
import jax.numpy as jnp
from jax import lax

RANK = 256
BLK = 128
MODE = 8
ROWS = 8192
COLS = 4096
REST = 512


def draw_pattern(key, part):
    row_blocks = COLS // BLK
    col_blocks = RANK // BLK
    coin_key = jax.random.fold_in(key, 11)
    pick_key = jax.random.fold_in(key, 23)
    coins = (jax.random.randint(coin_key, (row_blocks, col_blocks), 0, 4) == 0).astype(jnp.int32)
    picked = jax.random.randint(pick_key, (row_blocks, 1), 0, col_blocks)
    block_index = lax.broadcasted_iota(jnp.int32, (row_blocks, col_blocks), 0)
    column_index = lax.broadcasted_iota(jnp.int32, (row_blocks, col_blocks), 1)
    chosen = (picked == column_index).astype(jnp.int32)
    leading = ((block_index < col_blocks) & (block_index == column_index)).astype(jnp.int32)
    filled = jnp.maximum(jnp.maximum(coins, chosen), leading)
    last_row = jnp.where(row_blocks - 1 < col_blocks, leading, chosen)
    final = jnp.where(block_index == row_blocks - 1, last_row, filled)
    return final.astype(jnp.int32)


def with_ends(result, key, smallest, largest):
    dims = result.shape
    spot = [jax.random.randint(jax.random.fold_in(key, axis), (), 0, dims[axis]) for axis in range(len(dims))]
    result = result.at[tuple(spot)].set(smallest)
    longest = dims.index(max(dims))
    spot[longest] = (spot[longest] + 1) % dims[longest]
    return result.at[tuple(spot)].set(largest)


def levels(stream_key, shape, split, least, top_value):
    def one(axis_at, parts):
        draws = jax.random.uniform(jax.random.fold_in(jax.random.fold_in(stream_key, 6), axis_at), (parts,), jnp.float32, least / len(split), top_value / len(split))
        return jnp.repeat(jnp.exp(draws), shape[axis_at] // parts).reshape((-1,) + (1,) * (len(shape) - axis_at - 1))

    factor_of = one(*split[0])
    for cut in split[1:]:
        factor_of = factor_of * one(*cut)
    return factor_of


def scatter_about(own_key, extent, width, bound, cuts=(), held_as=jnp.bfloat16):
    array = width * jax.random.normal(own_key, extent, jnp.float32)
    if cuts:
        array = array * levels(own_key, extent, cuts, -0.22, 0.18)
    return jnp.clip(array, -bound, bound).astype(held_as)


def setup_inputs(seed: int = 0) -> dict:
    key_list = jax.random.split(jax.random.key(seed), 4)
    unfolding = scatter_about(key_list[0], (ROWS, COLS), 1.0, 6.0, ((0, 16), (1, 2)), jnp.float32)
    pattern = draw_pattern(jax.random.fold_in(key_list[3], 71), 0)
    sign_bits = with_ends(jax.random.randint(key_list[2], (COLS, RANK // BLK), 0, 2), jax.random.fold_in(key_list[2], 1), 0, 1).astype(jnp.int32)
    return {"unfolding": unfolding, "pattern": pattern, "sign_bits": sign_bits}


def hadamard_table(table_size):
    row_index = lax.broadcasted_iota(jnp.int32, (table_size, table_size), 0)
    col_index = lax.broadcasted_iota(jnp.int32, (table_size, table_size), 1)
    parity = jnp.zeros((table_size, table_size), jnp.int32)
    for bit_level in range(table_size.bit_length() - 1):
        bit_value = 1 << bit_level
        parity = parity + row_index // bit_value % 2 * (col_index // bit_value % 2)
    return (1 - 2 * (parity % 2)).astype(jnp.float32)

def sketch_matrix(pattern, sign_bits, block_size):
    blocks = sign_bits.shape[1]
    rows_here = sign_bits.shape[0]
    hadamard = hadamard_table(block_size)
    factor = jnp.repeat(pattern, block_size, axis=0) * (2 * sign_bits - 1)
    tiled_table = jnp.tile(hadamard, (rows_here // block_size, 1))
    expanded = factor.astype(jnp.float32)[:, :, None] * tiled_table[:, None, :]
    return expanded.reshape(rows_here, blocks * block_size)

def reference(unfolding, pattern, sign_bits):
    highest = lax.Precision.HIGHEST
    sketch_map = sketch_matrix(pattern, sign_bits, BLK)
    sketch = jnp.dot(unfolding, sketch_map, precision=highest)
    gram_matrix = jnp.dot(sketch.T, sketch, precision=highest)
    gram_matrix = gram_matrix + float(ROWS) * jnp.eye(RANK, dtype=jnp.float32)
    lower_factor = jnp.linalg.cholesky(gram_matrix)
    basis_rows = lax.linalg.triangular_solve(lower_factor, sketch, left_side=False, lower=True, transpose_a=True)
    core_scaled = basis_rows * math.sqrt(ROWS)
    remainder = jnp.dot(basis_rows.T, unfolding, precision=highest)
    next_unfolding = remainder.reshape(RANK * MODE, REST)
    return (core_scaled, next_unfolding)
```

```python
import math

import jax
import jax.numpy as jnp
import numpy as np
from jax import lax
from jax.experimental import pallas as pl
from jax.experimental.pallas import tpu as pltpu
from jax.sharding import PartitionSpec as P

RANK = 256
BLK = 128
MODE = 8
PANEL = 16
HIGHEST = lax.Precision.HIGHEST
F32 = jnp.float32
BF16 = jnp.bfloat16
VMEM = pl.BlockSpec(memory_space=pltpu.VMEM)
SMEM = pl.BlockSpec(memory_space=pltpu.SMEM)


def hadamard_table(table_size):
    index = np.arange(table_size)
    parity = np.zeros((table_size, table_size), np.int64)
    for bit_level in range(table_size.bit_length() - 1):
        parity += ((index[:, None] & index[None, :]) >> bit_level) & 1
    return jnp.asarray(1 - 2 * (parity % 2), F32)


def shape(*dims, dtype=F32):
    return jax.ShapeDtypeStruct(dims, dtype)


def split(value):
    high = value.astype(BF16)
    return high, (value - high.astype(F32)).astype(BF16)


def dot(left, right):
    return jnp.dot(left, right, preferred_element_type=F32)


def sketch_kernel(pattern_ref, block_ref, sign_ref, table_ref, out_ref):
    rows = block_ref.shape[0]
    col_blocks = sign_ref.shape[0]
    row_blocks = block_ref.shape[1] // BLK
    sums = []
    for k in range(col_blocks):
        total = jnp.zeros((rows, BLK), F32)
        for j in range(row_blocks):
            cols = slice(j * BLK, (j + 1) * BLK)
            factor = (2 * sign_ref[k : k + 1, cols] - 1) * pattern_ref[j, k]
            total = total + block_ref[:, cols] * factor.astype(F32)
        sums.append(total)
    mixed = jnp.dot(jnp.concatenate(sums, 0), table_ref[...], precision=HIGHEST)
    for k in range(col_blocks):
        out_ref[:, k * BLK : (k + 1) * BLK] = mixed[k * rows : (k + 1) * rows]


def sketch_band(unfolding, pattern, sign_rows, table, band, bands):
    rows, cols = unfolding.shape
    step = 64
    steps = rows // bands // step
    return pl.pallas_call(
        sketch_kernel,
        grid=(steps,),
        in_specs=[
            SMEM,
            pl.BlockSpec((step, cols), lambda i: (band * steps + i, 0)),
            pl.BlockSpec(sign_rows.shape, lambda i: (0, 0)),
            pl.BlockSpec((BLK, BLK), lambda i: (0, 0)),
        ],
        out_specs=pl.BlockSpec((step, RANK), lambda i: (i, 0)),
        out_shape=shape(rows // bands, RANK),
        name="sketch_band",
    )(pattern, unfolding, sign_rows, table)


def gram_kernel(ids_ref, own_a, own_b, got_a, got_b, sketch_ref, high_ref, low_ref, keep_ref, send_ref, packed):
    band = own_a.shape[0]
    sketch_ref[:band, :] = own_a[...] + got_a[...]
    sketch_ref[band:, :] = own_b[...] + got_b[...]
    sketch = sketch_ref[...]
    turned = sketch.T
    high, low = split(turned)
    high_ref[...] = high
    low_ref[...] = low
    top = jnp.dot(turned[:BLK], sketch, precision=HIGHEST)
    packed[:BLK] = top[:, :BLK]
    packed[BLK : 2 * BLK] = top[:, BLK:]
    packed[2 * BLK :] = jnp.dot(turned[BLK:], sketch[:, BLK:], precision=HIGHEST)
    half = packed.shape[0] // 2
    core = ids_ref[0]
    keep_ref[...] = packed[pl.ds(pl.multiple_of(core * half, half), half), :]
    send_ref[...] = packed[pl.ds(pl.multiple_of((1 - core) * half, half), half), :]


def gram_parts(ids, own, got):
    rows = own[0].shape[0] * 2
    return pl.pallas_call(
        gram_kernel,
        in_specs=[SMEM] + [VMEM] * 4,
        out_specs=[VMEM] * 5,
        out_shape=[
            shape(rows, RANK),
            shape(RANK, rows, dtype=BF16),
            shape(RANK, rows, dtype=BF16),
            shape(192, BLK),
            shape(192, BLK),
        ],
        scratch_shapes=[pltpu.VMEM((384, BLK), F32)],
        name="gram_parts",
    )(ids, *own, *got)


def project_kernel(ids_ref, high_ref, low_ref, block_ref, out_ref):
    a_high, a_low = split(block_ref[...])
    total = dot(high_ref[...], a_high) + dot(high_ref[...], a_low) + dot(low_ref[...], a_high)
    flip = ids_ref[1]
    out_ref[flip, 0] = total[:, :BLK]
    out_ref[1 - flip, 0] = total[:, BLK:]


def project(ids, high, low, unfolding, side):
    rows = unfolding.shape[0]

    def block(t, ids):
        return 0, (t ^ ids[2]) * 2 + (ids[3] ^ side)

    return pl.pallas_call(
        project_kernel,
        grid_spec=pltpu.PrefetchScalarGridSpec(
            num_scalar_prefetch=1,
            grid=(4,),
            in_specs=[
                pl.BlockSpec((RANK, rows), lambda t, ids: (0, 0)),
                pl.BlockSpec((RANK, rows), lambda t, ids: (0, 0)),
                pl.BlockSpec((rows, 2 * BLK), block),
            ],
            out_specs=pl.BlockSpec((2, 1, RANK, BLK), lambda t, ids: (0, t, 0, 0)),
        ),
        out_shape=shape(2, 4, RANK, BLK),
        name="project",
    )(ids, high, low, unfolding)


def factor_panel(parts, start):
    diagonal = parts[0][:, start : start + PANEL]
    columns = [jnp.broadcast_to(diagonal[:, k : k + 1], (PANEL, BLK)) for k in range(PANEL)]
    rows = lax.broadcasted_iota(jnp.int32, (PANEL, BLK), 0)
    pivots = jnp.ones((PANEL, BLK), F32)
    for j in range(PANEL):
        pivot = jnp.broadcast_to(columns[j][j : j + 1, :], (PANEL, BLK))
        multiplier = jnp.where(rows > j, columns[j] / pivot, 0.0)
        for k in range(j + 1, PANEL):
            columns[k] = columns[k] - multiplier * columns[k][j : j + 1, :]
        parts = [part - multiplier * part[j : j + 1, :] for part in parts]
        pivots = jnp.where(rows == j, pivot, pivots)
    scale = lax.rsqrt(pivots)
    return [part * scale for part in parts]


def factor_block(work):
    for panel in range(BLK // PANEL):
        start = panel * PANEL
        stop = start + PANEL
        parts = [work[start:stop, c * BLK : (c + 1) * BLK] for c in range(3)]
        parts = factor_panel(parts, start)
        for c in range(3):
            work[start:stop, c * BLK : (c + 1) * BLK] = parts[c]
        if stop < BLK:
            left = parts[0].T[stop:]
            work[stop:, :] = work[stop:, :] - jnp.dot(left, jnp.concatenate(parts, 1), precision=HIGHEST)


def factor_kernel(total_rows, ids_ref, own_ref, got_ref, out_ref, work, packed):
    half = own_ref.shape[0]
    core = ids_ref[0]
    packed[pl.ds(pl.multiple_of(core * half, half), half), :] = own_ref[...]
    packed[pl.ds(pl.multiple_of((1 - core) * half, half), half), :] = got_ref[...]
    row = lax.broadcasted_iota(jnp.int32, (BLK, BLK), 0)
    col = lax.broadcasted_iota(jnp.int32, (BLK, BLK), 1)
    eye = (row == col).astype(F32)
    work[:, :BLK] = packed[:BLK] + float(total_rows) * eye
    work[:, BLK : 2 * BLK] = packed[BLK : 2 * BLK]
    work[:, 2 * BLK :] = eye
    factor_block(work)
    out_ref[:BLK, :BLK] = work[:, 2 * BLK :]
    out_ref[:BLK, BLK:] = jnp.zeros((BLK, BLK), F32)
    above = work[:, BLK : 2 * BLK]
    product = jnp.dot(above.T, work[:, BLK:], precision=HIGHEST)
    work[:, :BLK] = packed[2 * BLK :] + float(total_rows) * eye - product[:, :BLK]
    work[:, BLK : 2 * BLK] = -product[:, BLK:]
    work[:, 2 * BLK :] = eye
    factor_block(work)
    out_ref[BLK:, :] = work[:, BLK:]


def inverse_factor(ids, own, got, total_rows):
    def body(*refs):
        factor_kernel(total_rows, *refs)

    return pl.pallas_call(
        body,
        in_specs=[SMEM, VMEM, VMEM],
        out_specs=VMEM,
        out_shape=shape(RANK, RANK),
        scratch_shapes=[pltpu.VMEM((BLK, 3 * BLK), F32), pltpu.VMEM((3 * BLK, BLK), F32)],
        name="inverse_factor",
    )(ids, own, got)


def core_kernel(scale, sketch_ref, inverse_ref, out_ref):
    s_high, s_low = split(sketch_ref[...])
    t_high, t_low = split(inverse_ref[...].T)
    total = dot(s_high, t_high) + dot(s_high, t_low) + dot(s_low, t_high)
    out_ref[...] = total * scale


def scaled_core(sketch, inverse, scale):
    def body(*refs):
        core_kernel(scale, *refs)

    return pl.pallas_call(
        body,
        in_specs=[VMEM, VMEM],
        out_specs=VMEM,
        out_shape=shape(*sketch.shape),
        name="scaled_core",
    )(sketch, inverse)


def remainder_kernel(ids_ref, inverse_ref, p0, p1, p2, p3, o0, o1, o2, o3, work):
    work[...] = jnp.dot(inverse_ref[...], (p0[...] + p1[...]) + (p2[...] + p3[...]), precision=HIGHEST)
    device = ids_ref[4]
    for m, out in enumerate((o0, o1, o2, o3)):
        for t in range(4):
            rank_block = (4 * t + m) ^ device
            out[t] = work[pl.ds(pl.multiple_of(rank_block * 16, 16), 16), :]


def remainder_pieces(ids, inverse, pieces):
    return pl.pallas_call(
        remainder_kernel,
        in_specs=[SMEM] + [VMEM] * 5,
        out_specs=[VMEM] * 4,
        out_shape=[shape(4, 16, BLK)] * 4,
        scratch_shapes=[pltpu.VMEM((RANK, BLK), F32)],
        name="remainder_pieces",
    )(ids, inverse, *pieces)


def arrange_kernel(ids_ref, r0, r1, r2, r3, s1, s2, s3, out_ref, work):
    core, right, deep, y = ids_ref[0], ids_ref[1], ids_ref[2], ids_ref[5]
    firsts = (r0, r1, r2, r3)
    later = (None, s1, s2, s3)
    for t in range(4):
        for m in range(4):
            mode = (y ^ core ^ (m & 1)) * 4 + (deep ^ t)
            work[mode, right ^ (m >> 1)] = firsts[m][0] if t == 0 else later[t][m]
    for mode in range(MODE):
        for c in range(2):
            out_ref[:, mode, c * BLK : (c + 1) * BLK] = work[mode, c]


def arrange(ids, firsts, later):
    out = pl.pallas_call(
        arrange_kernel,
        in_specs=[SMEM] + [VMEM] * 7,
        out_specs=VMEM,
        out_shape=shape(16, MODE, 2 * BLK),
        scratch_shapes=[pltpu.VMEM((MODE, 2, 16, BLK), F32)],
        name="arrange",
    )(ids, *firsts, *later)
    return out.reshape(16 * MODE, 2 * BLK)


def rows_permute(value, mask):
    size = lax.axis_size("rows")
    return lax.ppermute(value, "rows", [(i, i ^ mask) for i in range(size)])


def local(unfolding, pattern, sign_bits):
    total_rows = unfolding.shape[0] * lax.axis_size("rows")
    row = lax.axis_index("rows")
    y = lax.axis_index("cols")
    core = row & 1
    ids = jnp.stack([core, (row >> 1) & 1, row >> 2, core ^ y, row, y]).astype(jnp.int32)
    table = hadamard_table(BLK)
    sign_rows = sign_bits.T
    swap = [(0, 1), (1, 0)]
    own, got = [], []
    for band in range(2):
        part = sketch_band(unfolding, pattern, sign_rows, table, band, 2)
        own.append(part)
        got.append(lax.ppermute(part, "cols", swap))
    sketch, high, low, gram_keep, gram_send = gram_parts(ids, own, got)
    gram = gram_keep + rows_permute(gram_send, 1)
    give = project(ids, high, low, unfolding, 1)
    keep = project(ids, high, low, unfolding, 0)
    for mask in (2, 4, 8):
        gram = gram + rows_permute(gram, mask)
    gram_other = rows_permute(gram, 1)
    summed = keep + rows_permute(give, 1)
    summed = summed[0] + rows_permute(summed[1], 2)
    pieces = [summed[0]] + [rows_permute(summed[t], 4 * t) for t in (1, 2, 3)]
    inverse = inverse_factor(ids, gram, gram_other, total_rows)
    parts = remainder_pieces(ids, inverse, pieces)
    core_scaled = scaled_core(sketch, inverse, math.sqrt(total_rows))
    firsts = []
    for m in range(4):
        pairs = [(2 * i + j, 2 * (i ^ m) + (j ^ (i & 1))) for i in range(16) for j in range(2)]
        firsts.append(lax.ppermute(parts[m], ("rows", "cols"), pairs))
    later = []
    for t in (1, 2, 3):
        later.append(rows_permute(jnp.stack([first[t] for first in firsts]), 4 * t))
    return core_scaled, arrange(ids, firsts, later)


def sketch_matrix(pattern, sign_bits, block_size):
    blocks = sign_bits.shape[1]
    rows_here = sign_bits.shape[0]
    factor = jnp.repeat(pattern, block_size, axis=0) * (2 * sign_bits - 1)
    tiled_table = jnp.tile(hadamard_table(block_size), (rows_here // block_size, 1))
    expanded = factor.astype(F32)[:, :, None] * tiled_table[:, None, :]
    return expanded.reshape(rows_here, blocks * block_size)


def inner_rows(left_side, right_side):
    return lax.dot_general(left_side, right_side, (((0,), (0,)), ((), ())), precision=HIGHEST)


def local_any(unfolding, pattern, sign_bits):
    sketch_map = sketch_matrix(pattern, sign_bits, BLK)
    row_devices = lax.axis_size("rows")
    col_devices = lax.axis_size("cols")
    total_rows = unfolding.shape[0] * row_devices
    sketch = lax.psum(jnp.dot(unfolding, sketch_map, precision=HIGHEST), "cols")
    gram_matrix = lax.psum(inner_rows(sketch, sketch), "rows")
    gram_matrix = gram_matrix + float(total_rows) * jnp.eye(RANK, dtype=F32)
    lower_factor = jnp.linalg.cholesky(gram_matrix)
    basis_rows = lax.linalg.triangular_solve(lower_factor, sketch, left_side=False, lower=True, transpose_a=True)
    mode_local = MODE // col_devices
    rest_cols = unfolding.shape[1] // mode_local
    rank_share = RANK // row_devices
    reduced = lax.psum_scatter(inner_rows(basis_rows, unfolding), "rows", scatter_dimension=0, tiled=True)
    grouped = reduced.reshape(rank_share, mode_local, rest_cols)
    regrouped = lax.all_to_all(grouped, "cols", split_axis=2, concat_axis=1, tiled=True)
    return basis_rows * math.sqrt(total_rows), regrouped.reshape(rank_share * MODE, regrouped.shape[2])


def solution(mesh):
    in_specs = (P("rows", "cols"), P("cols", None), P("cols", None))
    out_specs = (P("rows", None), P("rows", "cols"))
    body = local if (mesh.shape["rows"], mesh.shape["cols"]) == (16, 2) else local_any
    return jax.shard_map(body, mesh=mesh, in_specs=in_specs, out_specs=out_specs, check_vma=False)
```

```python
import math

import jax
import jax.numpy as jnp
from jax import lax
from jax.experimental import pallas as pl
from jax.experimental.pallas import tpu as pltpu
from jax.sharding import PartitionSpec as P

RANK = 256
BLK = 128
MODE = 8
PANEL = 16
HIGHEST = lax.Precision.HIGHEST
F32 = jnp.float32
BF16 = jnp.bfloat16
VMEM = pl.BlockSpec(memory_space=pltpu.VMEM)
HBM = pl.BlockSpec(memory_space=pltpu.HBM)


def hadamard_table(table_size):
    row_index = lax.broadcasted_iota(jnp.int32, (table_size, table_size), 0)
    col_index = lax.broadcasted_iota(jnp.int32, (table_size, table_size), 1)
    both = row_index & col_index
    parity = jnp.zeros((table_size, table_size), jnp.int32)
    for bit_level in range(table_size.bit_length() - 1):
        parity = parity ^ (both >> bit_level)
    return (1 - 2 * (parity & 1)).astype(F32)


def on_chip(*dims, dtype=F32):
    return pltpu.VMEM(dims, dtype)


def held(*values):
    return [pltpu.with_memory_space_constraint(value, pltpu.VMEM) for value in values]


LIMIT = pltpu.CompilerParams(vmem_limit_bytes=8 << 20)


def cost(flops, size):
    return pl.CostEstimate(flops=flops, bytes_accessed=size, transcendentals=0)


def split(value):
    high = value.astype(BF16)
    return high, (value - high.astype(F32)).astype(BF16)


def dot(left, right):
    return jnp.dot(left, right, preferred_element_type=F32)


def sketch_kernel(first_row, pattern_ref, whole_ref, sign_ref, out_ref, band_ref, sems, signs, pattern):
    steps = sems.shape[0] - 2
    rows = band_ref.shape[0]
    step = rows // steps
    copies = [
        pltpu.make_async_copy(pattern_ref, pattern, sems.at[steps]),
        pltpu.make_async_copy(sign_ref, signs, sems.at[steps + 1]),
    ]
    for i in range(steps):
        here = pl.ds(first_row + i * step, step)
        copies.append(pltpu.make_async_copy(whole_ref.at[here], band_ref.at[pl.ds(i * step, step)], sems.at[i]))
    for copy in copies:
        copy.start()
    table = hadamard_table(BLK).astype(BF16)
    copies[0].wait()
    copies[1].wait()
    col_blocks = signs.shape[0]
    row_blocks = band_ref.shape[1] // BLK
    factors = []
    for k in range(col_blocks):
        signed = (2 * signs[k : k + 1, :] - 1).astype(F32)
        factors.append([signed[:, j * BLK : (j + 1) * BLK] * pattern[k, j].astype(F32) for j in range(row_blocks)])
    for i in range(steps):
        copies[2 + i].wait()
        here = slice(i * step, (i + 1) * step)
        for k in range(col_blocks):
            total = jnp.zeros((step, BLK), F32)
            for j in range(row_blocks):
                total = total + band_ref[here, j * BLK : (j + 1) * BLK] * factors[k][j]
            high, rest = split(total)
            low = (total - high.astype(F32) - rest.astype(F32)).astype(BF16)
            out_ref[here, k * BLK : (k + 1) * BLK] = dot(high, table) + dot(rest, table) + dot(low, table)


def sketch_band(unfolding, pattern_rows, sign_rows, band, bands):
    rows, cols = unfolding.shape
    rows //= bands

    def body(*refs):
        sketch_kernel(band * rows, *refs)

    return pl.pallas_call(
        body,
        in_specs=[HBM] * 3,
        out_specs=[VMEM] * 2,
        out_shape=[on_chip(rows, RANK), on_chip(rows, cols)],
        scratch_shapes=[
            pltpu.SemaphoreType.DMA((6,)),
            pltpu.VMEM(sign_rows.shape, jnp.int32),
            pltpu.SMEM(pattern_rows.shape, jnp.int32),
        ],
        cost_estimate=cost(rows * cols * 4, rows * cols * 4),
        compiler_params=LIMIT,
        name="sketch_band",
    )(*[pltpu.with_memory_space_constraint(x, pltpu.HBM) for x in (pattern_rows, unfolding, sign_rows)])


def gram_kernel(own_ref, got_ref, before_ref, sketch_ref, high_ref, low_ref, packed_ref, keep_ref, send_ref):
    sketch = own_ref[...] + got_ref[...]
    sketch_ref[...] = sketch
    turned = sketch.T
    high, low = split(turned)
    high_ref[...] = high
    low_ref[...] = low
    top = jnp.dot(turned[:BLK], sketch, precision=HIGHEST)
    low_corner = jnp.dot(turned[BLK:], sketch[:, BLK:], precision=HIGHEST)
    parts = [top[:, :BLK], top[:, BLK:], low_corner]
    for i, part in enumerate(parts):
        here = slice(i * BLK, (i + 1) * BLK)
        packed_ref[here] = part if before_ref is None else part + before_ref[here]
    if keep_ref is not None:
        half = keep_ref.shape[0]
        core = lax.axis_index("rows") & 1
        keep_ref[...] = packed_ref[pl.ds(pl.multiple_of(core * half, half), half), :]
        send_ref[...] = packed_ref[pl.ds(pl.multiple_of((1 - core) * half, half), half), :]


def gram_band(own, got, before):
    rows = own.shape[0]
    first = before is None
    operands = held(own, got) if first else held(own, got, before)
    packed = (3 * BLK, BLK)
    half = (3 * BLK // 2, BLK)

    def body(*refs):
        if first:
            gram_kernel(*refs[:2], None, *refs[2:], None, None)
        else:
            gram_kernel(*refs[:6], refs[8], *refs[6:8])

    return pl.pallas_call(
        body,
        in_specs=[VMEM] * len(operands),
        out_specs=[VMEM] * (4 if first else 5),
        out_shape=[
            on_chip(rows, RANK),
            on_chip(RANK, rows, dtype=BF16),
            on_chip(RANK, rows, dtype=BF16),
            *([on_chip(*packed)] if first else [on_chip(*half)] * 2),
        ],
        scratch_shapes=[] if first else [pltpu.VMEM(packed, F32)],
        cost_estimate=cost(rows * RANK * RANK * 12, rows * RANK * 8),
        compiler_params=LIMIT,
        name="gram_band",
    )(*operands)


def project_kernel(high_ref, low_ref, band_ref, before_ref, send_ref, keep_ref):
    row = lax.axis_index("rows")
    side_here = (row & 1) ^ lax.axis_index("cols")
    flip = (row >> 1) & 1
    for side, out_ref in ((1, send_ref), (0, keep_ref)):
        for t in range(4):
            block = (t ^ (row >> 2)) * 2 + (side_here ^ side)
            a_high, a_low = split(band_ref[:, pl.ds(pl.multiple_of(block * 2 * BLK, 2 * BLK), 2 * BLK)])
            total = dot(high_ref[...], a_high) + dot(high_ref[...], a_low) + dot(low_ref[...], a_high)
            for h in range(2):
                part = total[:, h * BLK : (h + 1) * BLK]
                place = flip if h == 0 else 1 - flip
                if before_ref is not None:
                    part = part + before_ref[1 - side][place, t]
                out_ref[place, t] = part


def project_band(high, low, band, before, after):
    rows, cols = band.shape
    operands = held(high, low, band, *(before or ()), *after)

    def body(*refs):
        project_kernel(*refs[:3], refs[3:5] if before else None, *refs[-2:])

    return pl.pallas_call(
        body,
        in_specs=[VMEM] * len(operands),
        out_specs=[VMEM] * 2,
        out_shape=[on_chip(2, 4, RANK, BLK)] * 2,
        cost_estimate=cost(rows * cols * RANK * 6, rows * cols * 4),
        compiler_params=LIMIT,
        name="project_band",
    )(*operands)


def add_parts_kernel(left_ref, right_ref, *outs):
    count = left_ref.shape[0] // len(outs)
    for i, out in enumerate(outs):
        if len(out.shape) < len(left_ref.shape):
            out[...] = left_ref[i] + right_ref[i]
        else:
            out[...] = left_ref[i * count : (i + 1) * count] + right_ref[i * count : (i + 1) * count]


def add_parts(left, right, parts, after=()):
    dims = left.shape
    out = dims[1:] if dims[0] == parts else (dims[0] // parts, *dims[1:])
    size = math.prod(dims)

    def body(*refs):
        add_parts_kernel(*refs[:2], *refs[-parts:])

    return pl.pallas_call(
        body,
        in_specs=[VMEM] * (2 + len(after)),
        out_specs=[VMEM] * parts,
        out_shape=[on_chip(*out)] * parts,
        cost_estimate=cost(size, size),
        compiler_params=LIMIT,
        name="add_parts",
    )(*held(left, right, *after))


def factor_panel(parts, start):
    diagonal = parts[0][:, start : start + PANEL]
    columns = [jnp.broadcast_to(diagonal[:, k : k + 1], (PANEL, BLK)) for k in range(PANEL)]
    rows = lax.broadcasted_iota(jnp.int32, (PANEL, BLK), 0)
    pivots = jnp.ones((PANEL, BLK), F32)
    for j in range(PANEL):
        pivot = jnp.broadcast_to(columns[j][j : j + 1, :], (PANEL, BLK))
        multiplier = jnp.where(rows > j, columns[j] / pivot, 0.0)
        for k in range(j + 1, PANEL):
            columns[k] = columns[k] - multiplier * columns[k][j : j + 1, :]
        parts = [part - multiplier * part[j : j + 1, :] for part in parts]
        pivots = jnp.where(rows == j, pivot, pivots)
    scale = lax.rsqrt(pivots)
    return [part * scale for part in parts]


def factor_block(work):
    for panel in range(BLK // PANEL):
        start = panel * PANEL
        stop = start + PANEL
        parts = [work[start:stop, c * BLK : (c + 1) * BLK] for c in range(3)]
        parts = factor_panel(parts, start)
        for c in range(3):
            work[start:stop, c * BLK : (c + 1) * BLK] = parts[c]
        if stop < BLK:
            left = parts[0].T[stop:]
            work[stop:, :] = work[stop:, :] - jnp.dot(left, jnp.concatenate(parts, 1), precision=HIGHEST)


def factor_kernel(total_rows, own_ref, got_ref, out_ref, work, packed):
    half = own_ref.shape[0]
    core = lax.axis_index("rows") & 1
    packed[pl.ds(pl.multiple_of(core * half, half), half), :] = own_ref[...]
    packed[pl.ds(pl.multiple_of((1 - core) * half, half), half), :] = got_ref[...]
    row = lax.broadcasted_iota(jnp.int32, (BLK, BLK), 0)
    col = lax.broadcasted_iota(jnp.int32, (BLK, BLK), 1)
    eye = (row == col).astype(F32)
    work[:, :BLK] = packed[:BLK] + float(total_rows) * eye
    work[:, BLK : 2 * BLK] = packed[BLK : 2 * BLK]
    work[:, 2 * BLK :] = eye
    factor_block(work)
    out_ref[:BLK, :BLK] = work[:, 2 * BLK :]
    out_ref[:BLK, BLK:] = jnp.zeros((BLK, BLK), F32)
    above = work[:, BLK : 2 * BLK]
    product = jnp.dot(above.T, work[:, BLK:], precision=HIGHEST)
    work[:, :BLK] = packed[2 * BLK :] + float(total_rows) * eye - product[:, :BLK]
    work[:, BLK : 2 * BLK] = -product[:, BLK:]
    work[:, 2 * BLK :] = eye
    factor_block(work)
    out_ref[BLK:, :] = work[:, BLK:]


def inverse_factor(own, got, total_rows):
    def body(*refs):
        factor_kernel(total_rows, *refs)

    return pl.pallas_call(
        body,
        in_specs=[VMEM, VMEM],
        out_specs=VMEM,
        out_shape=on_chip(RANK, RANK),
        scratch_shapes=[pltpu.VMEM((BLK, 3 * BLK), F32), pltpu.VMEM((3 * BLK, BLK), F32)],
        cost_estimate=cost(10_000_000_000, RANK * RANK * 8),
        compiler_params=LIMIT,
        name="inverse_factor",
    )(*held(own, got))


def core_kernel(scale, first_ref, second_ref, inverse_ref, out_ref):
    t_high, t_low = split(inverse_ref[...].T)
    band = first_ref.shape[0]
    for i, ref in enumerate((first_ref, second_ref)):
        s_high, s_low = split(ref[...])
        total = dot(s_high, t_high) + dot(s_high, t_low) + dot(s_low, t_high)
        out_ref[i * band : (i + 1) * band] = total * scale


def scaled_core(sketches, inverse, scale):
    rows = 2 * sketches[0].shape[0]

    def body(*refs):
        core_kernel(scale, *refs)

    return pl.pallas_call(
        body,
        in_specs=[VMEM] * 3,
        out_specs=VMEM,
        out_shape=jax.ShapeDtypeStruct((rows, RANK), F32),
        cost_estimate=cost(rows * RANK * RANK * 6, rows * RANK * 8),
        compiler_params=LIMIT,
        name="scaled_core",
    )(*held(*sketches, inverse))


def remainder_kernel(inverse_ref, p0, p1, p2, p3, o0, o1, o2, o3, work):
    work[...] = jnp.dot(inverse_ref[...], (p0[...] + p1[...]) + (p2[...] + p3[...]), precision=HIGHEST)
    device = lax.axis_index("rows")
    for m, out in enumerate((o0, o1, o2, o3)):
        for t in range(4):
            rank_block = (4 * t + m) ^ device
            out[t] = work[pl.ds(pl.multiple_of(rank_block * 16, 16), 16), :]


def remainder_pieces(inverse, pieces):
    return pl.pallas_call(
        remainder_kernel,
        in_specs=[VMEM] * 5,
        out_specs=[VMEM] * 4,
        out_shape=[on_chip(4, 16, BLK)] * 4,
        scratch_shapes=[pltpu.VMEM((RANK, BLK), F32)],
        cost_estimate=cost(RANK * RANK * BLK * 12, RANK * BLK * 8),
        compiler_params=LIMIT,
        name="remainder_pieces",
    )(*held(inverse, *pieces))


def collect_kernel(r0, r1, r2, r3, o1, o2, o3):
    for t, out in ((1, o1), (2, o2), (3, o3)):
        for m, piece in enumerate((r0, r1, r2, r3)):
            out[m] = piece[t]


def collect(firsts):
    return pl.pallas_call(
        collect_kernel,
        in_specs=[VMEM] * 4,
        out_specs=[VMEM] * 3,
        out_shape=[on_chip(4, 16, BLK)] * 3,
        cost_estimate=cost(0, 16 * BLK * 64),
        compiler_params=LIMIT,
        name="collect",
    )(*held(*firsts))


def arrange_kernel(r0, r1, r2, r3, s1, s2, s3, out_ref, work):
    row = lax.axis_index("rows")
    core, right, deep, y = row & 1, (row >> 1) & 1, row >> 2, lax.axis_index("cols")
    firsts = (r0, r1, r2, r3)
    later = (None, s1, s2, s3)
    for t in range(4):
        for m in range(4):
            mode = (y ^ core ^ (m & 1)) * 4 + (deep ^ t)
            work[mode, right ^ (m >> 1)] = firsts[m][0] if t == 0 else later[t][m]
    for mode in range(MODE):
        for c in range(2):
            out_ref[:, mode, c * BLK : (c + 1) * BLK] = work[mode, c]


def arrange(firsts, later):
    out = pl.pallas_call(
        arrange_kernel,
        in_specs=[VMEM] * 7,
        out_specs=VMEM,
        out_shape=jax.ShapeDtypeStruct((16, MODE, 2 * BLK), F32),
        scratch_shapes=[pltpu.VMEM((MODE, 2, 16, BLK), F32)],
        cost_estimate=cost(0, 16 * BLK * 64),
        compiler_params=LIMIT,
        name="arrange",
    )(*held(*firsts, *later))
    return out.reshape(16 * MODE, 2 * BLK)


def rows_permute(value, mask):
    size = lax.axis_size("rows")
    return lax.ppermute(value, "rows", [(i, i ^ mask) for i in range(size)])


def local(unfolding, pattern, sign_bits):
    total_rows = unfolding.shape[0] * lax.axis_size("rows")
    own, got, bands = [], [], []
    for band in range(2):
        part, rows_here = sketch_band(unfolding, pattern.T, sign_bits.T, band, 2)
        own.append(part)
        bands.append(rows_here)
        got.append(lax.ppermute(part, "cols", [(0, 1), (1, 0)]))
    first, high, low, packed = gram_band(own[0], got[0], None)
    sides = project_band(high, low, bands[0], None, ())
    second, high, low, gram_keep, gram_send = gram_band(own[1], got[1], packed)
    gram, = add_parts(gram_keep, rows_permute(gram_send, 1), 1)
    give, keep = project_band(high, low, bands[1], sides, (gram,))
    gram, = add_parts(gram, rows_permute(gram, 4), 1)
    keep, give = add_parts(keep, rows_permute(give, 1), 2, (gram,))
    for mask in (8, 2):
        gram, = add_parts(gram, rows_permute(gram, mask), 1)
    gram_other = rows_permute(gram, 1)
    pieces = add_parts(keep, rows_permute(give, 2), 4)
    pieces = [pieces[0]] + [rows_permute(pieces[t], 4 * t) for t in (1, 2, 3)]
    inverse = inverse_factor(gram, gram_other, total_rows)
    parts = remainder_pieces(inverse, pieces)
    core_scaled = scaled_core((first, second), inverse, math.sqrt(total_rows))
    firsts = []
    for m in range(4):
        pairs = [(2 * i + j, 2 * (i ^ m) + (j ^ (i & 1))) for i in range(16) for j in range(2)]
        firsts.append(lax.ppermute(parts[m], ("rows", "cols"), pairs))
    later = [rows_permute(part, 4 * t) for t, part in zip((1, 2, 3), collect(firsts))]
    return core_scaled, arrange(firsts, later)


def sketch_matrix(pattern, sign_bits, block_size):
    blocks = sign_bits.shape[1]
    rows_here = sign_bits.shape[0]
    factor = jnp.repeat(pattern, block_size, axis=0) * (2 * sign_bits - 1)
    tiled_table = jnp.tile(hadamard_table(block_size), (rows_here // block_size, 1))
    expanded = factor.astype(F32)[:, :, None] * tiled_table[:, None, :]
    return expanded.reshape(rows_here, blocks * block_size)


def inner_rows(left_side, right_side):
    return lax.dot_general(left_side, right_side, (((0,), (0,)), ((), ())), precision=HIGHEST)


def local_any(unfolding, pattern, sign_bits):
    sketch_map = sketch_matrix(pattern, sign_bits, BLK)
    row_devices = lax.axis_size("rows")
    col_devices = lax.axis_size("cols")
    total_rows = unfolding.shape[0] * row_devices
    sketch = lax.psum(jnp.dot(unfolding, sketch_map, precision=HIGHEST), "cols")
    gram_matrix = lax.psum(inner_rows(sketch, sketch), "rows")
    gram_matrix = gram_matrix + float(total_rows) * jnp.eye(RANK, dtype=F32)
    lower_factor = jnp.linalg.cholesky(gram_matrix)
    basis_rows = lax.linalg.triangular_solve(lower_factor, sketch, left_side=False, lower=True, transpose_a=True)
    mode_local = MODE // col_devices
    rest_cols = unfolding.shape[1] // mode_local
    rank_share = RANK // row_devices
    reduced = lax.psum_scatter(inner_rows(basis_rows, unfolding), "rows", scatter_dimension=0, tiled=True)
    grouped = reduced.reshape(rank_share, mode_local, rest_cols)
    regrouped = lax.all_to_all(grouped, "cols", split_axis=2, concat_axis=1, tiled=True)
    return basis_rows * math.sqrt(total_rows), regrouped.reshape(rank_share * MODE, regrouped.shape[2])


def solution(mesh):
    in_specs = (P("rows", "cols"), P("cols", None), P("cols", None))
    out_specs = (P("rows", None), P("rows", "cols"))
    body = local if (mesh.shape["rows"], mesh.shape["cols"]) == (16, 2) else local_any
    return jax.shard_map(body, mesh=mesh, in_specs=in_specs, out_specs=out_specs, check_vma=False)
```

```python
import math

import jax
import jax.numpy as jnp
from jax import lax
from jax.experimental import pallas as pl
from jax.experimental.pallas import tpu as pltpu
from jax.sharding import PartitionSpec as P

RANK = 256
BLK = 128
MODE = 8
PANEL = 16
HIGHEST = lax.Precision.HIGHEST
F32 = jnp.float32
BF16 = jnp.bfloat16
VMEM = pl.BlockSpec(memory_space=pltpu.VMEM)
HBM = pl.BlockSpec(memory_space=pltpu.HBM)


def hadamard_table(table_size):
    row_index = lax.broadcasted_iota(jnp.int32, (table_size, table_size), 0)
    col_index = lax.broadcasted_iota(jnp.int32, (table_size, table_size), 1)
    both = row_index & col_index
    parity = jnp.zeros((table_size, table_size), jnp.int32)
    for bit_level in range(table_size.bit_length() - 1):
        parity = parity ^ (both >> bit_level)
    return (1 - 2 * (parity & 1)).astype(F32)


def on_chip(*dims, dtype=F32):
    return pltpu.VMEM(dims, dtype)


def held(*values):
    return [pltpu.with_memory_space_constraint(value, pltpu.VMEM) for value in values]


LIMIT = pltpu.CompilerParams(vmem_limit_bytes=8 << 20)


def cost(flops, size):
    return pl.CostEstimate(flops=flops, bytes_accessed=size, transcendentals=0)


def split(value):
    high = value.astype(BF16)
    return high, (value - high.astype(F32)).astype(BF16)


def dot(left, right):
    return jnp.dot(left, right, preferred_element_type=F32)


def sketch_kernel(first_row, pattern_ref, whole_ref, sign_ref, out_ref, band_ref, sems, signs, pattern):
    steps = sems.shape[0] - 2
    rows = band_ref.shape[0]
    step = rows // steps
    copies = [
        pltpu.make_async_copy(pattern_ref, pattern, sems.at[steps]),
        pltpu.make_async_copy(sign_ref, signs, sems.at[steps + 1]),
    ]
    for i in range(steps):
        here = pl.ds(first_row + i * step, step)
        copies.append(pltpu.make_async_copy(whole_ref.at[here], band_ref.at[pl.ds(i * step, step)], sems.at[i]))
    for copy in copies:
        copy.start()
    table = hadamard_table(BLK).astype(BF16)
    copies[0].wait()
    copies[1].wait()
    col_blocks = signs.shape[0]
    row_blocks = band_ref.shape[1] // BLK
    factors = []
    for k in range(col_blocks):
        signed = (2 * signs[k : k + 1, :] - 1).astype(F32)
        factors.append([signed[:, j * BLK : (j + 1) * BLK] * pattern[k, j].astype(F32) for j in range(row_blocks)])
    for i in range(steps):
        copies[2 + i].wait()
        here = slice(i * step, (i + 1) * step)
        for k in range(col_blocks):
            total = jnp.zeros((step, BLK), F32)
            for j in range(row_blocks):
                total = total + band_ref[here, j * BLK : (j + 1) * BLK] * factors[k][j]
            high, rest = split(total)
            low = (total - high.astype(F32) - rest.astype(F32)).astype(BF16)
            out_ref[here, k * BLK : (k + 1) * BLK] = dot(high, table) + dot(rest, table) + dot(low, table)


def sketch_band(unfolding, pattern_rows, sign_rows, band, bands):
    rows, cols = unfolding.shape
    rows //= bands

    def body(*refs):
        sketch_kernel(band * rows, *refs)

    return pl.pallas_call(
        body,
        in_specs=[HBM] * 3,
        out_specs=[VMEM] * 2,
        out_shape=[on_chip(rows, RANK), on_chip(rows, cols)],
        scratch_shapes=[
            pltpu.SemaphoreType.DMA((6,)),
            pltpu.VMEM(sign_rows.shape, jnp.int32),
            pltpu.SMEM(pattern_rows.shape, jnp.int32),
        ],
        cost_estimate=cost(rows * cols * 4, rows * cols * 4),
        compiler_params=LIMIT,
        name="sketch_band",
    )(*[pltpu.with_memory_space_constraint(x, pltpu.HBM) for x in (pattern_rows, unfolding, sign_rows)])


def gram_kernel(own_ref, got_ref, before_ref, sketch_ref, high_ref, low_ref, packed_ref, keep_ref, send_ref):
    sketch = own_ref[...] + got_ref[...]
    sketch_ref[...] = sketch
    turned = sketch.T
    high, low = split(turned)
    high_ref[...] = high
    low_ref[...] = low
    top = jnp.dot(turned[:BLK], sketch, precision=HIGHEST)
    low_corner = jnp.dot(turned[BLK:], sketch[:, BLK:], precision=HIGHEST)
    parts = [top[:, :BLK], top[:, BLK:], low_corner]
    for i, part in enumerate(parts):
        here = slice(i * BLK, (i + 1) * BLK)
        packed_ref[here] = part if before_ref is None else part + before_ref[here]
    if keep_ref is not None:
        half = keep_ref.shape[0]
        core = lax.axis_index("rows") & 1
        keep_ref[...] = packed_ref[pl.ds(pl.multiple_of(core * half, half), half), :]
        send_ref[...] = packed_ref[pl.ds(pl.multiple_of((1 - core) * half, half), half), :]


def gram_band(own, got, before, after=()):
    rows = own.shape[0]
    first = before is None
    operands = held(own, got) if first else held(own, got, before, *after)
    packed = (3 * BLK, BLK)
    half = (3 * BLK // 2, BLK)

    def body(*refs):
        if first:
            gram_kernel(*refs[:2], None, *refs[2:], None, None)
        else:
            gram_kernel(*refs[:3], *refs[-6:-3], refs[-1], *refs[-3:-1])

    return pl.pallas_call(
        body,
        in_specs=[VMEM] * len(operands),
        out_specs=[VMEM] * (4 if first else 5),
        out_shape=[
            on_chip(rows, RANK),
            on_chip(RANK, rows, dtype=BF16),
            on_chip(RANK, rows, dtype=BF16),
            *([on_chip(*packed)] if first else [on_chip(*half)] * 2),
        ],
        scratch_shapes=[] if first else [pltpu.VMEM(packed, F32)],
        cost_estimate=cost(rows * RANK * RANK * 12, rows * RANK * 8),
        compiler_params=LIMIT,
        name="gram_band",
    )(*operands)


def project_kernel(high_ref, low_ref, band_ref, before_ref, send_ref, keep_ref):
    row = lax.axis_index("rows")
    core, flip, near, far = row & 1, (row >> 1) & 1, (row >> 2) & 1, row >> 3
    for side, out_ref in ((1, send_ref), (0, keep_ref)):
        for t in range(4):
            block = (far ^ (t >> 1)) * 4 + (core ^ side) * 2 + (near ^ (t & 1))
            a_high, a_low = split(band_ref[:, pl.ds(pl.multiple_of(block * 2 * BLK, 2 * BLK), 2 * BLK)])
            total = dot(high_ref[...], a_high) + dot(high_ref[...], a_low) + dot(low_ref[...], a_high)
            for h in range(2):
                part = total[:, h * BLK : (h + 1) * BLK]
                place = flip if h == 0 else 1 - flip
                if before_ref is not None:
                    part = part + before_ref[1 - side][place, t]
                out_ref[place, t] = part


def project_band(high, low, band, before, after):
    rows, cols = band.shape
    operands = held(high, low, band, *(before or ()), *after)

    def body(*refs):
        project_kernel(*refs[:3], refs[3:5] if before else None, *refs[-2:])

    return pl.pallas_call(
        body,
        in_specs=[VMEM] * len(operands),
        out_specs=[VMEM] * 2,
        out_shape=[on_chip(2, 4, RANK, BLK)] * 2,
        cost_estimate=cost(rows * cols * RANK * 6, rows * cols * 4),
        compiler_params=LIMIT,
        name="project_band",
    )(*operands)


def add_parts_kernel(left_ref, right_ref, *outs):
    count = left_ref.shape[0] // len(outs)
    for i, out in enumerate(outs):
        if len(out.shape) < len(left_ref.shape):
            out[...] = left_ref[i] + right_ref[i]
        else:
            out[...] = left_ref[i * count : (i + 1) * count] + right_ref[i * count : (i + 1) * count]


def add_parts(left, right, parts, after=()):
    dims = left.shape
    out = dims[1:] if dims[0] == parts else (dims[0] // parts, *dims[1:])
    size = math.prod(dims)

    def body(*refs):
        add_parts_kernel(*refs[:2], *refs[-parts:])

    return pl.pallas_call(
        body,
        in_specs=[VMEM] * (2 + len(after)),
        out_specs=[VMEM] * parts,
        out_shape=[on_chip(*out)] * parts,
        cost_estimate=cost(size, size),
        compiler_params=LIMIT,
        name="add_parts",
    )(*held(left, right, *after))


def factor_panel(parts, start):
    diagonal = parts[0][:, start : start + PANEL]
    columns = [jnp.broadcast_to(diagonal[:, k : k + 1], (PANEL, BLK)) for k in range(PANEL)]
    rows = lax.broadcasted_iota(jnp.int32, (PANEL, BLK), 0)
    pivots = jnp.ones((PANEL, BLK), F32)
    for j in range(PANEL):
        pivot = jnp.broadcast_to(columns[j][j : j + 1, :], (PANEL, BLK))
        multiplier = jnp.where(rows > j, columns[j] / pivot, 0.0)
        for k in range(j + 1, PANEL):
            columns[k] = columns[k] - multiplier * columns[k][j : j + 1, :]
        parts = [part - multiplier * part[j : j + 1, :] for part in parts]
        pivots = jnp.where(rows == j, pivot, pivots)
    scale = lax.rsqrt(pivots)
    return [part * scale for part in parts]


def factor_block(work):
    for panel in range(BLK // PANEL):
        start = panel * PANEL
        stop = start + PANEL
        parts = [work[start:stop, c * BLK : (c + 1) * BLK] for c in range(3)]
        parts = factor_panel(parts, start)
        for c in range(3):
            work[start:stop, c * BLK : (c + 1) * BLK] = parts[c]
        if stop < BLK:
            left = parts[0].T[stop:]
            work[stop:, :] = work[stop:, :] - jnp.dot(left, jnp.concatenate(parts, 1), precision=HIGHEST)


def factor_kernel(total_rows, own_ref, got_ref, out_ref, work, packed):
    half = own_ref.shape[0]
    core = lax.axis_index("rows") & 1
    packed[pl.ds(pl.multiple_of(core * half, half), half), :] = own_ref[...]
    packed[pl.ds(pl.multiple_of((1 - core) * half, half), half), :] = got_ref[...]
    row = lax.broadcasted_iota(jnp.int32, (BLK, BLK), 0)
    col = lax.broadcasted_iota(jnp.int32, (BLK, BLK), 1)
    eye = (row == col).astype(F32)
    work[:, :BLK] = packed[:BLK] + float(total_rows) * eye
    work[:, BLK : 2 * BLK] = packed[BLK : 2 * BLK]
    work[:, 2 * BLK :] = eye
    factor_block(work)
    out_ref[:BLK, :BLK] = work[:, 2 * BLK :]
    out_ref[:BLK, BLK:] = jnp.zeros((BLK, BLK), F32)
    above = work[:, BLK : 2 * BLK]
    product = jnp.dot(above.T, work[:, BLK:], precision=HIGHEST)
    work[:, :BLK] = packed[2 * BLK :] + float(total_rows) * eye - product[:, :BLK]
    work[:, BLK : 2 * BLK] = -product[:, BLK:]
    work[:, 2 * BLK :] = eye
    factor_block(work)
    out_ref[BLK:, :] = work[:, BLK:]


def inverse_factor(own, got, total_rows, after):
    def body(*refs):
        factor_kernel(total_rows, *refs[:2], *refs[-3:])

    return pl.pallas_call(
        body,
        in_specs=[VMEM] * (2 + len(after)),
        out_specs=VMEM,
        out_shape=on_chip(RANK, RANK),
        scratch_shapes=[pltpu.VMEM((BLK, 3 * BLK), F32), pltpu.VMEM((3 * BLK, BLK), F32)],
        cost_estimate=cost(10_000_000_000, RANK * RANK * 8),
        compiler_params=LIMIT,
        name="inverse_factor",
    )(*held(own, got, *after))


def core_kernel(scale, first_ref, second_ref, inverse_ref, out_ref):
    t_high, t_low = split(inverse_ref[...].T)
    band = first_ref.shape[0]
    for i, ref in enumerate((first_ref, second_ref)):
        s_high, s_low = split(ref[...])
        total = dot(s_high, t_high) + dot(s_high, t_low) + dot(s_low, t_high)
        out_ref[i * band : (i + 1) * band] = total * scale


def scaled_core(sketches, inverse, scale):
    rows = 2 * sketches[0].shape[0]

    def body(*refs):
        core_kernel(scale, *refs)

    return pl.pallas_call(
        body,
        in_specs=[VMEM] * 3,
        out_specs=VMEM,
        out_shape=jax.ShapeDtypeStruct((rows, RANK), F32),
        cost_estimate=cost(rows * RANK * RANK * 6, rows * RANK * 8),
        compiler_params=LIMIT,
        name="scaled_core",
    )(*held(*sketches, inverse))


def remainder_kernel(inverse_ref, p0, p1, p2, p3, o0, o1, o2, o3, work):
    work[...] = jnp.dot(inverse_ref[...], (p0[...] + p1[...]) + (p2[...] + p3[...]), precision=HIGHEST)
    device = lax.axis_index("rows")
    for m, out in enumerate((o0, o1, o2, o3)):
        for t in range(4):
            rank_block = (4 * t + m) ^ device
            out[t] = work[pl.ds(pl.multiple_of(rank_block * 16, 16), 16), :]


def remainder_pieces(inverse, pieces):
    return pl.pallas_call(
        remainder_kernel,
        in_specs=[VMEM] * 5,
        out_specs=[VMEM] * 4,
        out_shape=[on_chip(4, 16, BLK)] * 4,
        scratch_shapes=[pltpu.VMEM((RANK, BLK), F32)],
        cost_estimate=cost(RANK * RANK * BLK * 12, RANK * BLK * 8),
        compiler_params=LIMIT,
        name="remainder_pieces",
    )(*held(inverse, *pieces))


def collect_kernel(r0, r1, r2, r3, o1, o2, o3):
    for t, out in ((1, o1), (2, o2), (3, o3)):
        for m, piece in enumerate((r0, r1, r2, r3)):
            out[m] = piece[t]


def collect(firsts):
    return pl.pallas_call(
        collect_kernel,
        in_specs=[VMEM] * 4,
        out_specs=[VMEM] * 3,
        out_shape=[on_chip(4, 16, BLK)] * 3,
        cost_estimate=cost(0, 16 * BLK * 64),
        compiler_params=LIMIT,
        name="collect",
    )(*held(*firsts))


def arrange_kernel(r0, r1, r2, r3, s1, s2, s3, out_ref, work):
    row = lax.axis_index("rows")
    core, right, deep = row & 1, (row >> 1) & 1, row >> 2
    firsts = (r0, r1, r2, r3)
    later = (None, s1, s2, s3)
    for t in range(4):
        for m in range(4):
            there = deep ^ t
            mode = (there & 1) * 4 + (there >> 1) * 2 + (core ^ (m & 1))
            work[mode, right ^ (m >> 1)] = firsts[m][0] if t == 0 else later[t][m]
    for mode in range(MODE):
        for c in range(2):
            out_ref[:, mode, c * BLK : (c + 1) * BLK] = work[mode, c]


def arrange(firsts, later):
    out = pl.pallas_call(
        arrange_kernel,
        in_specs=[VMEM] * 7,
        out_specs=VMEM,
        out_shape=jax.ShapeDtypeStruct((16, MODE, 2 * BLK), F32),
        scratch_shapes=[pltpu.VMEM((MODE, 2, 16, BLK), F32)],
        cost_estimate=cost(0, 16 * BLK * 64),
        compiler_params=LIMIT,
        name="arrange",
    )(*held(*firsts, *later))
    return out.reshape(16 * MODE, 2 * BLK)


def rows_permute(value, mask):
    size = lax.axis_size("rows")
    return lax.ppermute(value, "rows", [(i, i ^ mask) for i in range(size)])


def local(unfolding, pattern, sign_bits):
    total_rows = unfolding.shape[0] * lax.axis_size("rows")
    own, got, bands = [], [], []
    for band in range(2):
        part, rows_here = sketch_band(unfolding, pattern.T, sign_bits.T, band, 2)
        own.append(part)
        bands.append(rows_here)
        got.append(lax.ppermute(part, "cols", [(0, 1), (1, 0)]))
    first, high, low, packed = gram_band(own[0], got[0], None)
    sides = project_band(high, low, bands[0], None, ())
    second, high, low, gram_keep, gram_send = gram_band(own[1], got[1], packed, sides)
    gram_got = rows_permute(gram_send, 1)
    give, keep = project_band(high, low, bands[1], sides, ())
    gram, = add_parts(gram_keep, gram_got, 1, (keep,))
    keep, give = add_parts(keep, rows_permute(give, 1), 2)
    gram, = add_parts(gram, rows_permute(gram, 4), 1, (give,))
    for mask in (8, 2):
        gram, = add_parts(gram, rows_permute(gram, mask), 1)
    gram_other = rows_permute(gram, 1)
    pieces = add_parts(keep, rows_permute(give, 2), 4)
    inverse = inverse_factor(gram, gram_other, total_rows, pieces)
    gathered = []
    for k in range(4):
        pairs = []
        for i in range(16):
            for y in range(2):
                to = (i & 3) | (y << 2) | ((i & 8) ^ ((k >> 1) << 3))
                pairs.append((2 * i + y, 2 * to + (((i >> 2) & 1) ^ (k & 1))))
        gathered.append(lax.ppermute(pieces[k], ("rows", "cols"), pairs))
    parts = remainder_pieces(inverse, gathered)
    core_scaled = scaled_core((first, second), inverse, math.sqrt(total_rows))
    firsts = [parts[0]] + [rows_permute(parts[m], m) for m in (1, 2, 3)]
    later = [rows_permute(part, 4 * t) for t, part in zip((1, 2, 3), collect(firsts))]
    return core_scaled, arrange(firsts, later)


def sketch_matrix(pattern, sign_bits, block_size):
    blocks = sign_bits.shape[1]
    rows_here = sign_bits.shape[0]
    factor = jnp.repeat(pattern, block_size, axis=0) * (2 * sign_bits - 1)
    tiled_table = jnp.tile(hadamard_table(block_size), (rows_here // block_size, 1))
    expanded = factor.astype(F32)[:, :, None] * tiled_table[:, None, :]
    return expanded.reshape(rows_here, blocks * block_size)


def inner_rows(left_side, right_side):
    return lax.dot_general(left_side, right_side, (((0,), (0,)), ((), ())), precision=HIGHEST)


def local_any(unfolding, pattern, sign_bits):
    sketch_map = sketch_matrix(pattern, sign_bits, BLK)
    row_devices = lax.axis_size("rows")
    col_devices = lax.axis_size("cols")
    total_rows = unfolding.shape[0] * row_devices
    sketch = lax.psum(jnp.dot(unfolding, sketch_map, precision=HIGHEST), "cols")
    gram_matrix = lax.psum(inner_rows(sketch, sketch), "rows")
    gram_matrix = gram_matrix + float(total_rows) * jnp.eye(RANK, dtype=F32)
    lower_factor = jnp.linalg.cholesky(gram_matrix)
    basis_rows = lax.linalg.triangular_solve(lower_factor, sketch, left_side=False, lower=True, transpose_a=True)
    mode_local = MODE // col_devices
    rest_cols = unfolding.shape[1] // mode_local
    rank_share = RANK // row_devices
    reduced = lax.psum_scatter(inner_rows(basis_rows, unfolding), "rows", scatter_dimension=0, tiled=True)
    grouped = reduced.reshape(rank_share, mode_local, rest_cols)
    regrouped = lax.all_to_all(grouped, "cols", split_axis=2, concat_axis=1, tiled=True)
    return basis_rows * math.sqrt(total_rows), regrouped.reshape(rank_share * MODE, regrouped.shape[2])


def solution(mesh):
    in_specs = (P("rows", "cols"), P("cols", None), P("cols", None))
    out_specs = (P("rows", None), P("rows", "cols"))
    body = local if (mesh.shape["rows"], mesh.shape["cols"]) == (16, 2) else local_any
    return jax.shard_map(body, mesh=mesh, in_specs=in_specs, out_specs=out_specs, check_vma=False)
```

```python
import math

import jax
import jax.numpy as jnp
from jax import lax
from jax.experimental import pallas as pl
from jax.experimental.pallas import tpu as pltpu
from jax.sharding import PartitionSpec as P

RANK = 256
BLK = 128
MODE = 8
PANEL = 16
HIGHEST = lax.Precision.HIGHEST
F32 = jnp.float32
BF16 = jnp.bfloat16
VMEM = pl.BlockSpec(memory_space=pltpu.VMEM)
HBM = pl.BlockSpec(memory_space=pltpu.HBM)


def hadamard_table(table_size):
    row_index = lax.broadcasted_iota(jnp.int32, (table_size, table_size), 0)
    col_index = lax.broadcasted_iota(jnp.int32, (table_size, table_size), 1)
    both = row_index & col_index
    parity = jnp.zeros((table_size, table_size), jnp.int32)
    for bit_level in range(table_size.bit_length() - 1):
        parity = parity ^ (both >> bit_level)
    return (1 - 2 * (parity & 1)).astype(F32)


def on_chip(*dims, dtype=F32):
    return pltpu.VMEM(dims, dtype)


def held(*values):
    return [pltpu.with_memory_space_constraint(value, pltpu.VMEM) for value in values]


LIMIT = pltpu.CompilerParams(vmem_limit_bytes=8 << 20)


def cost(flops, size):
    return pl.CostEstimate(flops=flops, bytes_accessed=size, transcendentals=0)


def split(value):
    high = value.astype(BF16)
    return high, (value - high.astype(F32)).astype(BF16)


def dot(left, right):
    return jnp.dot(left, right, preferred_element_type=F32)


def sketch_kernel(first_row, pattern_ref, whole_ref, sign_ref, out_ref, band_ref, sems, signs, pattern):
    steps = sems.shape[0] - 2
    rows = band_ref.shape[0]
    step = rows // steps
    copies = [
        pltpu.make_async_copy(pattern_ref, pattern, sems.at[steps]),
        pltpu.make_async_copy(sign_ref, signs, sems.at[steps + 1]),
    ]
    for i in range(steps):
        here = pl.ds(first_row + i * step, step)
        copies.append(pltpu.make_async_copy(whole_ref.at[here], band_ref.at[pl.ds(i * step, step)], sems.at[i]))
    for copy in copies:
        copy.start()
    table = hadamard_table(BLK).astype(BF16)
    copies[0].wait()
    copies[1].wait()
    col_blocks = signs.shape[0]
    row_blocks = band_ref.shape[1] // BLK
    factors = []
    for k in range(col_blocks):
        signed = (2 * signs[k : k + 1, :] - 1).astype(F32)
        factors.append([signed[:, j * BLK : (j + 1) * BLK] * pattern[k, j].astype(F32) for j in range(row_blocks)])
    for i in range(steps):
        copies[2 + i].wait()
        here = slice(i * step, (i + 1) * step)
        for k in range(col_blocks):
            total = jnp.zeros((step, BLK), F32)
            for j in range(row_blocks):
                total = total + band_ref[here, j * BLK : (j + 1) * BLK] * factors[k][j]
            high, rest = split(total)
            low = (total - high.astype(F32) - rest.astype(F32)).astype(BF16)
            out_ref[here, k * BLK : (k + 1) * BLK] = dot(high, table) + dot(rest, table) + dot(low, table)


def sketch_band(unfolding, pattern_rows, sign_rows, band, bands):
    rows, cols = unfolding.shape
    rows //= bands

    def body(*refs):
        sketch_kernel(band * rows, *refs)

    return pl.pallas_call(
        body,
        in_specs=[HBM] * 3,
        out_specs=[VMEM] * 2,
        out_shape=[on_chip(rows, RANK), on_chip(rows, cols)],
        scratch_shapes=[
            pltpu.SemaphoreType.DMA((6,)),
            pltpu.VMEM(sign_rows.shape, jnp.int32),
            pltpu.SMEM(pattern_rows.shape, jnp.int32),
        ],
        cost_estimate=cost(rows * cols * 4, rows * cols * 4),
        compiler_params=LIMIT,
        name="sketch_band",
    )(*[pltpu.with_memory_space_constraint(x, pltpu.HBM) for x in (pattern_rows, unfolding, sign_rows)])


def gram_kernel(own_ref, got_ref, before_ref, sketch_ref, high_ref, low_ref, packed_ref, keep_ref, send_ref):
    sketch = own_ref[...] + got_ref[...]
    sketch_ref[...] = sketch
    turned = sketch.T
    high, low = split(turned)
    high_ref[...] = high
    low_ref[...] = low
    top = jnp.dot(turned[:BLK], sketch, precision=HIGHEST)
    low_corner = jnp.dot(turned[BLK:], sketch[:, BLK:], precision=HIGHEST)
    parts = [top[:, :BLK], top[:, BLK:], low_corner]
    for i, part in enumerate(parts):
        here = slice(i * BLK, (i + 1) * BLK)
        packed_ref[here] = part if before_ref is None else part + before_ref[here]
    if keep_ref is not None:
        half = keep_ref.shape[0]
        core = lax.axis_index("rows") & 1
        keep_ref[...] = packed_ref[pl.ds(pl.multiple_of(core * half, half), half), :]
        send_ref[...] = packed_ref[pl.ds(pl.multiple_of((1 - core) * half, half), half), :]


def gram_band(own, got, before, after=()):
    rows = own.shape[0]
    first = before is None
    operands = held(own, got) if first else held(own, got, before, *after)
    packed = (3 * BLK, BLK)
    half = (3 * BLK // 2, BLK)

    def body(*refs):
        if first:
            gram_kernel(*refs[:2], None, *refs[2:], None, None)
        else:
            gram_kernel(*refs[:3], *refs[-6:-3], refs[-1], *refs[-3:-1])

    return pl.pallas_call(
        body,
        in_specs=[VMEM] * len(operands),
        out_specs=[VMEM] * (4 if first else 5),
        out_shape=[
            on_chip(rows, RANK),
            on_chip(RANK, rows, dtype=BF16),
            on_chip(RANK, rows, dtype=BF16),
            *([on_chip(*packed)] if first else [on_chip(*half)] * 2),
        ],
        scratch_shapes=[] if first else [pltpu.VMEM(packed, F32)],
        cost_estimate=cost(rows * RANK * RANK * 12, rows * RANK * 8),
        compiler_params=LIMIT,
        name="gram_band",
    )(*operands)


def project_kernel(high_ref, low_ref, band_ref, before_ref, send_ref, keep_ref):
    row = lax.axis_index("rows")
    core, flip, near, far = row & 1, (row >> 1) & 1, (row >> 2) & 1, row >> 3
    for side, out_ref in ((1, send_ref), (0, keep_ref)):
        for t in range(4):
            block = (far ^ (t >> 1)) * 4 + (core ^ side) * 2 + (near ^ (t & 1))
            a_high, a_low = split(band_ref[:, pl.ds(pl.multiple_of(block * 2 * BLK, 2 * BLK), 2 * BLK)])
            total = dot(high_ref[...], a_high) + dot(high_ref[...], a_low) + dot(low_ref[...], a_high)
            for h in range(2):
                part = total[:, h * BLK : (h + 1) * BLK]
                place = flip if h == 0 else 1 - flip
                if before_ref is not None:
                    part = part + before_ref[1 - side][place, t]
                out_ref[place, t] = part


def project_band(high, low, band, before, after):
    rows, cols = band.shape
    operands = held(high, low, band, *(before or ()), *after)

    def body(*refs):
        project_kernel(*refs[:3], refs[3:5] if before else None, *refs[-2:])

    return pl.pallas_call(
        body,
        in_specs=[VMEM] * len(operands),
        out_specs=[VMEM] * 2,
        out_shape=[on_chip(2, 4, RANK, BLK)] * 2,
        cost_estimate=cost(rows * cols * RANK * 6, rows * cols * 4),
        compiler_params=LIMIT,
        name="project_band",
    )(*operands)


def add_parts_kernel(left_ref, right_ref, *outs):
    count = left_ref.shape[0] // len(outs)
    for i, out in enumerate(outs):
        if len(out.shape) < len(left_ref.shape):
            out[...] = left_ref[i] + right_ref[i]
        else:
            out[...] = left_ref[i * count : (i + 1) * count] + right_ref[i * count : (i + 1) * count]


def add_parts(left, right, parts, after=()):
    dims = left.shape
    out = dims[1:] if dims[0] == parts else (dims[0] // parts, *dims[1:])
    size = math.prod(dims)

    def body(*refs):
        add_parts_kernel(*refs[:2], *refs[-parts:])

    return pl.pallas_call(
        body,
        in_specs=[VMEM] * (2 + len(after)),
        out_specs=[VMEM] * parts,
        out_shape=[on_chip(*out)] * parts,
        cost_estimate=cost(size, size),
        compiler_params=LIMIT,
        name="add_parts",
    )(*held(left, right, *after))


def factor_panel(parts, start):
    diagonal = parts[0][:, start : start + PANEL]
    columns = [jnp.broadcast_to(diagonal[:, k : k + 1], (PANEL, BLK)) for k in range(PANEL)]
    rows = lax.broadcasted_iota(jnp.int32, (PANEL, BLK), 0)
    pivots = jnp.ones((PANEL, BLK), F32)
    for j in range(PANEL):
        pivot = jnp.broadcast_to(columns[j][j : j + 1, :], (PANEL, BLK))
        multiplier = jnp.where(rows > j, columns[j] / pivot, 0.0)
        for k in range(j + 1, PANEL):
            columns[k] = columns[k] - multiplier * columns[k][j : j + 1, :]
        parts = [part - multiplier * part[j : j + 1, :] for part in parts]
        pivots = jnp.where(rows == j, pivot, pivots)
    scale = lax.rsqrt(pivots)
    return [part * scale for part in parts]


def factor_block(work):
    for panel in range(BLK // PANEL):
        start = panel * PANEL
        stop = start + PANEL
        parts = [work[start:stop, c * BLK : (c + 1) * BLK] for c in range(3)]
        parts = factor_panel(parts, start)
        for c in range(3):
            work[start:stop, c * BLK : (c + 1) * BLK] = parts[c]
        if stop < BLK:
            left = parts[0].T[stop:]
            work[stop:, :] = work[stop:, :] - jnp.dot(left, jnp.concatenate(parts, 1), precision=HIGHEST)


def factor_kernel(total_rows, own_ref, got_ref, out_ref, work, packed):
    half = own_ref.shape[0]
    core = lax.axis_index("rows") & 1
    packed[pl.ds(pl.multiple_of(core * half, half), half), :] = own_ref[...]
    packed[pl.ds(pl.multiple_of((1 - core) * half, half), half), :] = got_ref[...]
    row = lax.broadcasted_iota(jnp.int32, (BLK, BLK), 0)
    col = lax.broadcasted_iota(jnp.int32, (BLK, BLK), 1)
    eye = (row == col).astype(F32)
    work[:, :BLK] = packed[:BLK] + float(total_rows) * eye
    work[:, BLK : 2 * BLK] = packed[BLK : 2 * BLK]
    work[:, 2 * BLK :] = eye
    factor_block(work)
    out_ref[:BLK, :BLK] = work[:, 2 * BLK :]
    out_ref[:BLK, BLK:] = jnp.zeros((BLK, BLK), F32)
    above = work[:, BLK : 2 * BLK]
    product = jnp.dot(above.T, work[:, BLK:], precision=HIGHEST)
    work[:, :BLK] = packed[2 * BLK :] + float(total_rows) * eye - product[:, :BLK]
    work[:, BLK : 2 * BLK] = -product[:, BLK:]
    work[:, 2 * BLK :] = eye
    factor_block(work)
    out_ref[BLK:, :] = work[:, BLK:]


def inverse_factor(own, got, total_rows):
    def body(*refs):
        factor_kernel(total_rows, *refs)

    return pl.pallas_call(
        body,
        in_specs=[VMEM] * 2,
        out_specs=VMEM,
        out_shape=on_chip(RANK, RANK),
        scratch_shapes=[pltpu.VMEM((BLK, 3 * BLK), F32), pltpu.VMEM((3 * BLK, BLK), F32)],
        cost_estimate=cost(0, RANK * RANK * 8),
        compiler_params=LIMIT,
        name="inverse_factor",
    )(*held(own, got))


def core_kernel(scale, first_ref, second_ref, inverse_ref, out_ref):
    t_high, t_low = split(inverse_ref[...].T)
    band = first_ref.shape[0]
    for i, ref in enumerate((first_ref, second_ref)):
        s_high, s_low = split(ref[...])
        total = dot(s_high, t_high) + dot(s_high, t_low) + dot(s_low, t_high)
        out_ref[i * band : (i + 1) * band] = total * scale


def scaled_core(sketches, inverse, scale):
    rows = 2 * sketches[0].shape[0]

    def body(*refs):
        core_kernel(scale, *refs)

    return pl.pallas_call(
        body,
        in_specs=[VMEM] * 3,
        out_specs=VMEM,
        out_shape=jax.ShapeDtypeStruct((rows, RANK), F32),
        cost_estimate=cost(rows * RANK * RANK * 6, rows * RANK * 8),
        compiler_params=LIMIT,
        name="scaled_core",
    )(*held(*sketches, inverse))


def remainder_kernel(inverse_ref, p0, p1, p2, p3, o0, o1, o2, o3, work):
    work[...] = jnp.dot(inverse_ref[...], (p0[...] + p1[...]) + (p2[...] + p3[...]), precision=HIGHEST)
    device = lax.axis_index("rows")
    for m, out in enumerate((o0, o1, o2, o3)):
        for t in range(4):
            rank_block = (4 * t + m) ^ device
            out[t] = work[pl.ds(pl.multiple_of(rank_block * 16, 16), 16), :]


def remainder_pieces(inverse, pieces):
    return pl.pallas_call(
        remainder_kernel,
        in_specs=[VMEM] * 5,
        out_specs=[VMEM] * 4,
        out_shape=[on_chip(4, 16, BLK)] * 4,
        scratch_shapes=[pltpu.VMEM((RANK, BLK), F32)],
        cost_estimate=cost(RANK * RANK * BLK * 12, RANK * BLK * 8),
        compiler_params=LIMIT,
        name="remainder_pieces",
    )(*held(inverse, *pieces))


def collect_kernel(r0, r1, r2, r3, o1, o2, o3):
    for t, out in ((1, o1), (2, o2), (3, o3)):
        for m, piece in enumerate((r0, r1, r2, r3)):
            out[m] = piece[t]


def collect(firsts):
    return pl.pallas_call(
        collect_kernel,
        in_specs=[VMEM] * 4,
        out_specs=[VMEM] * 3,
        out_shape=[on_chip(4, 16, BLK)] * 3,
        cost_estimate=cost(0, 16 * BLK * 64),
        compiler_params=LIMIT,
        name="collect",
    )(*held(*firsts))


def arrange_kernel(r0, r1, r2, r3, s1, s2, s3, out_ref, work):
    row = lax.axis_index("rows")
    core, right, deep = row & 1, (row >> 1) & 1, row >> 2
    firsts = (r0, r1, r2, r3)
    later = (None, s1, s2, s3)
    for t in range(4):
        for m in range(4):
            there = deep ^ t
            mode = (there & 1) * 4 + (there >> 1) * 2 + (core ^ (m & 1))
            work[mode, right ^ (m >> 1)] = firsts[m][0] if t == 0 else later[t][m]
    for mode in range(MODE):
        for c in range(2):
            out_ref[:, mode, c * BLK : (c + 1) * BLK] = work[mode, c]


def arrange(firsts, later):
    out = pl.pallas_call(
        arrange_kernel,
        in_specs=[VMEM] * 7,
        out_specs=VMEM,
        out_shape=jax.ShapeDtypeStruct((16, MODE, 2 * BLK), F32),
        scratch_shapes=[pltpu.VMEM((MODE, 2, 16, BLK), F32)],
        cost_estimate=cost(0, 16 * BLK * 64),
        compiler_params=LIMIT,
        name="arrange",
    )(*held(*firsts, *later))
    return out.reshape(16 * MODE, 2 * BLK)


def rows_permute(value, mask):
    size = lax.axis_size("rows")
    return lax.ppermute(value, "rows", [(i, i ^ mask) for i in range(size)])


def local(unfolding, pattern, sign_bits):
    total_rows = unfolding.shape[0] * lax.axis_size("rows")
    own, got, bands = [], [], []
    for band in range(2):
        part, rows_here = sketch_band(unfolding, pattern.T, sign_bits.T, band, 2)
        own.append(part)
        bands.append(rows_here)
        got.append(lax.ppermute(part, "cols", [(0, 1), (1, 0)]))
    first, high, low, packed = gram_band(own[0], got[0], None)
    sides = project_band(high, low, bands[0], None, ())
    second, high, low, gram_keep, gram_send = gram_band(own[1], got[1], packed, sides)
    gram_got = rows_permute(gram_send, 1)
    give, keep = project_band(high, low, bands[1], sides, ())
    gram, = add_parts(gram_keep, gram_got, 1, (keep,))
    keep, give = add_parts(keep, rows_permute(give, 1), 2)
    gram, = add_parts(gram, rows_permute(gram, 4), 1, (give,))
    pieces = add_parts(keep, rows_permute(give, 2), 4)
    gram, = add_parts(gram, rows_permute(gram, 8), 1, pieces)
    gram, = add_parts(gram, rows_permute(gram, 2), 1)
    inverse = inverse_factor(gram, rows_permute(gram, 1), total_rows)
    gathered = []
    for k in range(4):
        pairs = []
        for i in range(16):
            for y in range(2):
                to = (i & 3) | (y << 2) | ((i & 8) ^ ((k >> 1) << 3))
                pairs.append((2 * i + y, 2 * to + (((i >> 2) & 1) ^ (k & 1))))
        gathered.append(lax.ppermute(pieces[k], ("rows", "cols"), pairs))
    parts = remainder_pieces(inverse, gathered)
    core_scaled = scaled_core((first, second), inverse, math.sqrt(total_rows))
    firsts = [parts[0]] + [rows_permute(parts[m], m) for m in (1, 2, 3)]
    later = [rows_permute(part, 4 * t) for t, part in zip((1, 2, 3), collect(firsts))]
    return core_scaled, arrange(firsts, later)


def sketch_matrix(pattern, sign_bits, block_size):
    blocks = sign_bits.shape[1]
    rows_here = sign_bits.shape[0]
    factor = jnp.repeat(pattern, block_size, axis=0) * (2 * sign_bits - 1)
    tiled_table = jnp.tile(hadamard_table(block_size), (rows_here // block_size, 1))
    expanded = factor.astype(F32)[:, :, None] * tiled_table[:, None, :]
    return expanded.reshape(rows_here, blocks * block_size)


def inner_rows(left_side, right_side):
    return lax.dot_general(left_side, right_side, (((0,), (0,)), ((), ())), precision=HIGHEST)


def local_any(unfolding, pattern, sign_bits):
    sketch_map = sketch_matrix(pattern, sign_bits, BLK)
    row_devices = lax.axis_size("rows")
    col_devices = lax.axis_size("cols")
    total_rows = unfolding.shape[0] * row_devices
    sketch = lax.psum(jnp.dot(unfolding, sketch_map, precision=HIGHEST), "cols")
    gram_matrix = lax.psum(inner_rows(sketch, sketch), "rows")
    gram_matrix = gram_matrix + float(total_rows) * jnp.eye(RANK, dtype=F32)
    lower_factor = jnp.linalg.cholesky(gram_matrix)
    basis_rows = lax.linalg.triangular_solve(lower_factor, sketch, left_side=False, lower=True, transpose_a=True)
    mode_local = MODE // col_devices
    rest_cols = unfolding.shape[1] // mode_local
    rank_share = RANK // row_devices
    reduced = lax.psum_scatter(inner_rows(basis_rows, unfolding), "rows", scatter_dimension=0, tiled=True)
    grouped = reduced.reshape(rank_share, mode_local, rest_cols)
    regrouped = lax.all_to_all(grouped, "cols", split_axis=2, concat_axis=1, tiled=True)
    return basis_rows * math.sqrt(total_rows), regrouped.reshape(rank_share * MODE, regrouped.shape[2])


def solution(mesh):
    in_specs = (P("rows", "cols"), P("cols", None), P("cols", None))
    out_specs = (P("rows", None), P("rows", "cols"))
    body = local if (mesh.shape["rows"], mesh.shape["cols"]) == (16, 2) else local_any
    return jax.shard_map(body, mesh=mesh, in_specs=in_specs, out_specs=out_specs, check_vma=False)
```

```python
import math

import jax
import jax.numpy as jnp
from jax import lax
from jax.experimental import pallas as pl
from jax.experimental.pallas import tpu as pltpu
from jax.sharding import PartitionSpec as P

RANK = 256
BLK = 128
MODE = 8
PANEL = 16
HIGHEST = lax.Precision.HIGHEST
F32 = jnp.float32
BF16 = jnp.bfloat16
VMEM = pl.BlockSpec(memory_space=pltpu.VMEM)
HBM = pl.BlockSpec(memory_space=pltpu.HBM)


def hadamard_table(table_size):
    row_index = lax.broadcasted_iota(jnp.int32, (table_size, table_size), 0)
    col_index = lax.broadcasted_iota(jnp.int32, (table_size, table_size), 1)
    both = row_index & col_index
    parity = jnp.zeros((table_size, table_size), jnp.int32)
    for bit_level in range(table_size.bit_length() - 1):
        parity = parity ^ (both >> bit_level)
    return (1 - 2 * (parity & 1)).astype(F32)


def on_chip(*dims, dtype=F32):
    return pltpu.VMEM(dims, dtype)


def held(*values):
    return [pltpu.with_memory_space_constraint(value, pltpu.VMEM) for value in values]


LIMIT = pltpu.CompilerParams(vmem_limit_bytes=8 << 20)


def cost(flops, size):
    return pl.CostEstimate(flops=flops, bytes_accessed=size, transcendentals=0)


def split(value):
    high = value.astype(BF16)
    return high, (value - high.astype(F32)).astype(BF16)


def dot(left, right):
    return jnp.dot(left, right, preferred_element_type=F32)


def sketch_kernel(first_row, pattern_ref, whole_ref, sign_ref, out_ref, band_ref, sems, signs, pattern):
    steps = sems.shape[0] - 2
    rows = band_ref.shape[0]
    step = rows // steps
    copies = [
        pltpu.make_async_copy(pattern_ref, pattern, sems.at[steps]),
        pltpu.make_async_copy(sign_ref, signs, sems.at[steps + 1]),
    ]
    for i in range(steps):
        here = pl.ds(first_row + i * step, step)
        copies.append(pltpu.make_async_copy(whole_ref.at[here], band_ref.at[pl.ds(i * step, step)], sems.at[i]))
    for copy in copies:
        copy.start()
    table = hadamard_table(BLK).astype(BF16)
    copies[0].wait()
    copies[1].wait()
    col_blocks = signs.shape[0]
    row_blocks = band_ref.shape[1] // BLK
    factors = []
    for k in range(col_blocks):
        signed = (2 * signs[k : k + 1, :] - 1).astype(F32)
        factors.append([signed[:, j * BLK : (j + 1) * BLK] * pattern[k, j].astype(F32) for j in range(row_blocks)])
    for i in range(steps):
        copies[2 + i].wait()
        here = slice(i * step, (i + 1) * step)
        for k in range(col_blocks):
            total = jnp.zeros((step, BLK), F32)
            for j in range(row_blocks):
                total = total + band_ref[here, j * BLK : (j + 1) * BLK] * factors[k][j]
            high, rest = split(total)
            low = (total - high.astype(F32) - rest.astype(F32)).astype(BF16)
            out_ref[here, k * BLK : (k + 1) * BLK] = dot(high, table) + dot(rest, table) + dot(low, table)


def sketch_band(unfolding, pattern_rows, sign_rows, band, bands):
    rows, cols = unfolding.shape
    rows //= bands

    def body(*refs):
        sketch_kernel(band * rows, *refs)

    return pl.pallas_call(
        body,
        in_specs=[HBM] * 3,
        out_specs=[VMEM] * 2,
        out_shape=[on_chip(rows, RANK), on_chip(rows, cols)],
        scratch_shapes=[
            pltpu.SemaphoreType.DMA((6,)),
            pltpu.VMEM(sign_rows.shape, jnp.int32),
            pltpu.SMEM(pattern_rows.shape, jnp.int32),
        ],
        cost_estimate=cost(rows * cols * 4, rows * cols * 4),
        compiler_params=LIMIT,
        name="sketch_band",
    )(*[pltpu.with_memory_space_constraint(x, pltpu.HBM) for x in (pattern_rows, unfolding, sign_rows)])


def gram_kernel(own_ref, got_ref, before_ref, sketch_ref, high_ref, low_ref, packed_ref, keep_ref, send_ref):
    sketch = own_ref[...] + got_ref[...]
    sketch_ref[...] = sketch
    turned = sketch.T
    high, low = split(turned)
    high_ref[...] = high
    low_ref[...] = low
    top = jnp.dot(turned[:BLK], sketch, precision=HIGHEST)
    low_corner = jnp.dot(turned[BLK:], sketch[:, BLK:], precision=HIGHEST)
    parts = [top[:, :BLK], top[:, BLK:], low_corner]
    for i, part in enumerate(parts):
        here = slice(i * BLK, (i + 1) * BLK)
        packed_ref[here] = part if before_ref is None else part + before_ref[here]
    if keep_ref is not None:
        half = keep_ref.shape[0]
        core = lax.axis_index("rows") & 1
        keep_ref[...] = packed_ref[pl.ds(pl.multiple_of(core * half, half), half), :]
        send_ref[...] = packed_ref[pl.ds(pl.multiple_of((1 - core) * half, half), half), :]


def gram_band(own, got, before, after=()):
    rows = own.shape[0]
    first = before is None
    operands = held(own, got) if first else held(own, got, before, *after)
    packed = (3 * BLK, BLK)
    half = (3 * BLK // 2, BLK)

    def body(*refs):
        if first:
            gram_kernel(*refs[:2], None, *refs[2:], None, None)
        else:
            gram_kernel(*refs[:3], *refs[-6:-3], refs[-1], *refs[-3:-1])

    return pl.pallas_call(
        body,
        in_specs=[VMEM] * len(operands),
        out_specs=[VMEM] * (4 if first else 5),
        out_shape=[
            on_chip(rows, RANK),
            on_chip(RANK, rows, dtype=BF16),
            on_chip(RANK, rows, dtype=BF16),
            *([on_chip(*packed)] if first else [on_chip(*half)] * 2),
        ],
        scratch_shapes=[] if first else [pltpu.VMEM(packed, F32)],
        cost_estimate=cost(rows * RANK * RANK * 12, rows * RANK * 8),
        compiler_params=LIMIT,
        name="gram_band",
    )(*operands)


def project_kernel(flips, high_ref, low_ref, band_ref, before, outs):
    row = lax.axis_index("rows")
    core, right, near, far = row & 1, (row >> 1) & 1, (row >> 2) & 1, row >> 3
    for i, flip in enumerate(flips):
        for t in range(4):
            block = (far ^ (t >> 1)) * 4 + (right ^ flip) * 2 + (near ^ (t & 1))
            a_high, a_low = split(band_ref[:, pl.ds(pl.multiple_of(block * 2 * BLK, 2 * BLK), 2 * BLK)])
            total = dot(high_ref[...], a_high) + dot(high_ref[...], a_low) + dot(low_ref[...], a_high)
            left, other = total[:, :BLK], total[:, BLK:]
            give = jnp.where(core == 0, other, left)
            keep = jnp.where(core == 0, left, other)
            outs[2 * i][t] = give if before is None else give + before[2 * i][t]
            outs[2 * i + 1][t] = keep if before is None else keep + before[2 * i + 1][t]


def project_band(flips, high, low, band, before=(), after=()):
    rows, cols = band.shape
    operands = held(high, low, band, *before, *after)
    count = 2 * len(flips)

    def body(*refs):
        project_kernel(flips, *refs[:3], refs[3 : 3 + count] if before else None, refs[-count:])

    return pl.pallas_call(
        body,
        in_specs=[VMEM] * len(operands),
        out_specs=[VMEM] * count,
        out_shape=[on_chip(4, RANK, BLK)] * count,
        cost_estimate=cost(rows * cols * RANK * 3 * len(flips), rows * cols * 4),
        compiler_params=LIMIT,
        name="project_band",
    )(*operands)


def add_parts_kernel(terms, outs):
    for i, out in enumerate(outs):
        here = slice(None) if len(outs) == 1 else i
        total = terms[0][here]
        for term in terms[1:]:
            total = total + term[here]
        out[...] = total


def add_parts(terms, parts, after=()):
    dims = terms[0].shape
    size = math.prod(dims)
    count = len(terms)

    def body(*refs):
        add_parts_kernel(refs[:count], refs[-parts:])

    return pl.pallas_call(
        body,
        in_specs=[VMEM] * (count + len(after)),
        out_specs=[VMEM] * parts,
        out_shape=[on_chip(*(dims if parts == 1 else dims[1:]))] * parts,
        cost_estimate=cost(size, size),
        compiler_params=LIMIT,
        name="add_parts",
    )(*held(*terms, *after))


def factor_panel(parts, start):
    diagonal = parts[0][:, start : start + PANEL]
    columns = [jnp.broadcast_to(diagonal[:, k : k + 1], (PANEL, BLK)) for k in range(PANEL)]
    rows = lax.broadcasted_iota(jnp.int32, (PANEL, BLK), 0)
    pivots = jnp.ones((PANEL, BLK), F32)
    for j in range(PANEL):
        pivot = jnp.broadcast_to(columns[j][j : j + 1, :], (PANEL, BLK))
        multiplier = jnp.where(rows > j, columns[j] / pivot, 0.0)
        for k in range(j + 1, PANEL):
            columns[k] = columns[k] - multiplier * columns[k][j : j + 1, :]
        parts = [part - multiplier * part[j : j + 1, :] for part in parts]
        pivots = jnp.where(rows == j, pivot, pivots)
    scale = lax.rsqrt(pivots)
    return [part * scale for part in parts]


def factor_block(work):
    for panel in range(BLK // PANEL):
        start = panel * PANEL
        stop = start + PANEL
        parts = [work[start:stop, c * BLK : (c + 1) * BLK] for c in range(3)]
        parts = factor_panel(parts, start)
        for c in range(3):
            work[start:stop, c * BLK : (c + 1) * BLK] = parts[c]
        if stop < BLK:
            left = parts[0].T[stop:]
            work[stop:, :] = work[stop:, :] - jnp.dot(left, jnp.concatenate(parts, 1), precision=HIGHEST)


def factor_kernel(total_rows, own_ref, got_ref, out_ref, work, packed):
    half = own_ref.shape[0]
    core = lax.axis_index("rows") & 1
    packed[pl.ds(pl.multiple_of(core * half, half), half), :] = own_ref[...]
    packed[pl.ds(pl.multiple_of((1 - core) * half, half), half), :] = got_ref[...]
    row = lax.broadcasted_iota(jnp.int32, (BLK, BLK), 0)
    col = lax.broadcasted_iota(jnp.int32, (BLK, BLK), 1)
    eye = (row == col).astype(F32)
    work[:, :BLK] = packed[:BLK] + float(total_rows) * eye
    work[:, BLK : 2 * BLK] = packed[BLK : 2 * BLK]
    work[:, 2 * BLK :] = eye
    factor_block(work)
    out_ref[:BLK, :BLK] = work[:, 2 * BLK :]
    out_ref[:BLK, BLK:] = jnp.zeros((BLK, BLK), F32)
    above = work[:, BLK : 2 * BLK]
    product = jnp.dot(above.T, work[:, BLK:], precision=HIGHEST)
    work[:, :BLK] = packed[2 * BLK :] + float(total_rows) * eye - product[:, :BLK]
    work[:, BLK : 2 * BLK] = -product[:, BLK:]
    work[:, 2 * BLK :] = eye
    factor_block(work)
    out_ref[BLK:, :] = work[:, BLK:]


def inverse_factor(own, got, total_rows):
    def body(*refs):
        factor_kernel(total_rows, *refs)

    return pl.pallas_call(
        body,
        in_specs=[VMEM] * 2,
        out_specs=VMEM,
        out_shape=on_chip(RANK, RANK),
        scratch_shapes=[pltpu.VMEM((BLK, 3 * BLK), F32), pltpu.VMEM((3 * BLK, BLK), F32)],
        cost_estimate=cost(0, RANK * RANK * 8),
        compiler_params=LIMIT,
        name="inverse_factor",
    )(*held(own, got))


def core_kernel(scale, first_ref, second_ref, inverse_ref, out_ref):
    t_high, t_low = split(inverse_ref[...].T)
    band = first_ref.shape[0]
    for i, ref in enumerate((first_ref, second_ref)):
        s_high, s_low = split(ref[...])
        total = dot(s_high, t_high) + dot(s_high, t_low) + dot(s_low, t_high)
        out_ref[i * band : (i + 1) * band] = total * scale


def scaled_core(sketches, inverse, scale):
    rows = 2 * sketches[0].shape[0]

    def body(*refs):
        core_kernel(scale, *refs)

    return pl.pallas_call(
        body,
        in_specs=[VMEM] * 3,
        out_specs=VMEM,
        out_shape=jax.ShapeDtypeStruct((rows, RANK), F32),
        cost_estimate=cost(rows * RANK * RANK * 6, rows * RANK * 8),
        compiler_params=LIMIT,
        name="scaled_core",
    )(*held(*sketches, inverse))


def remainder_kernel(inverse_ref, p0, p1, p2, p3, o0, o1, o2, o3, work):
    work[...] = jnp.dot(inverse_ref[...], (p0[...] + p1[...]) + (p2[...] + p3[...]), precision=HIGHEST)
    device = lax.axis_index("rows")
    for m, out in enumerate((o0, o1, o2, o3)):
        for t in range(4):
            rank_block = (4 * t + m) ^ device
            out[t] = work[pl.ds(pl.multiple_of(rank_block * 16, 16), 16), :]


def remainder_pieces(inverse, pieces):
    return pl.pallas_call(
        remainder_kernel,
        in_specs=[VMEM] * 5,
        out_specs=[VMEM] * 4,
        out_shape=[on_chip(4, 16, BLK)] * 4,
        scratch_shapes=[pltpu.VMEM((RANK, BLK), F32)],
        cost_estimate=cost(RANK * RANK * BLK * 12, RANK * BLK * 8),
        compiler_params=LIMIT,
        name="remainder_pieces",
    )(*held(inverse, *pieces))


def collect_kernel(r0, r1, r2, r3, o1, o2, o3):
    for t, out in ((1, o1), (2, o2), (3, o3)):
        for m, piece in enumerate((r0, r1, r2, r3)):
            out[m] = piece[t]


def collect(firsts):
    return pl.pallas_call(
        collect_kernel,
        in_specs=[VMEM] * 4,
        out_specs=[VMEM] * 3,
        out_shape=[on_chip(4, 16, BLK)] * 3,
        cost_estimate=cost(0, 16 * BLK * 64),
        compiler_params=LIMIT,
        name="collect",
    )(*held(*firsts))


def arrange_kernel(r0, r1, r2, r3, s1, s2, s3, out_ref, work):
    row = lax.axis_index("rows")
    core, right, deep = row & 1, (row >> 1) & 1, row >> 2
    firsts = (r0, r1, r2, r3)
    later = (None, s1, s2, s3)
    for t in range(4):
        for m in range(4):
            there = deep ^ t
            mode = (there & 1) * 4 + (there >> 1) * 2 + (right ^ (m >> 1))
            work[mode, core ^ (m & 1)] = firsts[m][0] if t == 0 else later[t][m]
    for mode in range(MODE):
        for c in range(2):
            out_ref[:, mode, c * BLK : (c + 1) * BLK] = work[mode, c]


def arrange(firsts, later):
    out = pl.pallas_call(
        arrange_kernel,
        in_specs=[VMEM] * 7,
        out_specs=VMEM,
        out_shape=jax.ShapeDtypeStruct((16, MODE, 2 * BLK), F32),
        scratch_shapes=[pltpu.VMEM((MODE, 2, 16, BLK), F32)],
        cost_estimate=cost(0, 16 * BLK * 64),
        compiler_params=LIMIT,
        name="arrange",
    )(*held(*firsts, *later))
    return out.reshape(16 * MODE, 2 * BLK)


def rows_permute(value, mask):
    size = lax.axis_size("rows")
    return lax.ppermute(value, "rows", [(i, i ^ mask) for i in range(size)])


def local(unfolding, pattern, sign_bits):
    total_rows = unfolding.shape[0] * lax.axis_size("rows")
    own, got, bands = [], [], []
    for band in range(2):
        part, rows_here = sketch_band(unfolding, pattern.T, sign_bits.T, band, 2)
        own.append(part)
        bands.append(rows_here)
        got.append(lax.ppermute(part, "cols", [(0, 1), (1, 0)]))
    first, high, low, packed = gram_band(own[0], got[0], None)
    before = project_band((1, 0), high, low, bands[0])
    second, high, low, gram_keep, gram_send = gram_band(own[1], got[1], packed, before[:1])
    gram, = add_parts((gram_keep, rows_permute(gram_send, 1)), 1)
    give, keep = project_band((1,), high, low, bands[1], before[:2])
    send, = add_parts((keep, rows_permute(give, 1)), 1, (gram,))
    give, keep = project_band((0,), high, low, bands[1], before[2:])
    pieces = add_parts((keep, rows_permute(give, 1), rows_permute(send, 2)), 4)
    gram, = add_parts((gram, rows_permute(gram, 4)), 1)
    gram, = add_parts((gram, rows_permute(gram, 8)), 1, pieces)
    gram, = add_parts((gram, rows_permute(gram, 2)), 1)
    inverse = inverse_factor(gram, rows_permute(gram, 1), total_rows)
    gathered = []
    for k in range(4):
        pairs = []
        for i in range(16):
            for y in range(2):
                to = (i & 3) | (y << 2) | ((i & 8) ^ ((k >> 1) << 3))
                pairs.append((2 * i + y, 2 * to + (((i >> 2) & 1) ^ (k & 1))))
        gathered.append(lax.ppermute(pieces[k], ("rows", "cols"), pairs))
    parts = remainder_pieces(inverse, gathered)
    core_scaled = scaled_core((first, second), inverse, math.sqrt(total_rows))
    firsts = [parts[0]] + [rows_permute(parts[m], m) for m in (1, 2, 3)]
    later = [rows_permute(part, 4 * t) for t, part in zip((1, 2, 3), collect(firsts))]
    return core_scaled, arrange(firsts, later)


def sketch_matrix(pattern, sign_bits, block_size):
    blocks = sign_bits.shape[1]
    rows_here = sign_bits.shape[0]
    factor = jnp.repeat(pattern, block_size, axis=0) * (2 * sign_bits - 1)
    tiled_table = jnp.tile(hadamard_table(block_size), (rows_here // block_size, 1))
    expanded = factor.astype(F32)[:, :, None] * tiled_table[:, None, :]
    return expanded.reshape(rows_here, blocks * block_size)


def inner_rows(left_side, right_side):
    return lax.dot_general(left_side, right_side, (((0,), (0,)), ((), ())), precision=HIGHEST)


def local_any(unfolding, pattern, sign_bits):
    sketch_map = sketch_matrix(pattern, sign_bits, BLK)
    row_devices = lax.axis_size("rows")
    col_devices = lax.axis_size("cols")
    total_rows = unfolding.shape[0] * row_devices
    sketch = lax.psum(jnp.dot(unfolding, sketch_map, precision=HIGHEST), "cols")
    gram_matrix = lax.psum(inner_rows(sketch, sketch), "rows")
    gram_matrix = gram_matrix + float(total_rows) * jnp.eye(RANK, dtype=F32)
    lower_factor = jnp.linalg.cholesky(gram_matrix)
    basis_rows = lax.linalg.triangular_solve(lower_factor, sketch, left_side=False, lower=True, transpose_a=True)
    mode_local = MODE // col_devices
    rest_cols = unfolding.shape[1] // mode_local
    rank_share = RANK // row_devices
    reduced = lax.psum_scatter(inner_rows(basis_rows, unfolding), "rows", scatter_dimension=0, tiled=True)
    grouped = reduced.reshape(rank_share, mode_local, rest_cols)
    regrouped = lax.all_to_all(grouped, "cols", split_axis=2, concat_axis=1, tiled=True)
    return basis_rows * math.sqrt(total_rows), regrouped.reshape(rank_share * MODE, regrouped.shape[2])


def solution(mesh):
    in_specs = (P("rows", "cols"), P("cols", None), P("cols", None))
    out_specs = (P("rows", None), P("rows", "cols"))
    body = local if (mesh.shape["rows"], mesh.shape["cols"]) == (16, 2) else local_any
    return jax.shard_map(body, mesh=mesh, in_specs=in_specs, out_specs=out_specs, check_vma=False)
```

```python
import math

import jax
import jax.numpy as jnp
from jax import lax
from jax.experimental import pallas as pl
from jax.experimental.pallas import tpu as pltpu
from jax.sharding import PartitionSpec as P

RANK = 256
BLK = 128
MODE = 8
PANEL = 16
HIGHEST = lax.Precision.HIGHEST
F32 = jnp.float32
BF16 = jnp.bfloat16
VMEM = pl.BlockSpec(memory_space=pltpu.VMEM)
HBM = pl.BlockSpec(memory_space=pltpu.HBM)


def hadamard_table(table_size):
    row_index = lax.broadcasted_iota(jnp.int32, (table_size, table_size), 0)
    col_index = lax.broadcasted_iota(jnp.int32, (table_size, table_size), 1)
    both = row_index & col_index
    parity = jnp.zeros((table_size, table_size), jnp.int32)
    for bit_level in range(table_size.bit_length() - 1):
        parity = parity ^ (both >> bit_level)
    return (1 - 2 * (parity & 1)).astype(F32)


def on_chip(*dims, dtype=F32):
    return pltpu.VMEM(dims, dtype)


def held(*values):
    return [pltpu.with_memory_space_constraint(value, pltpu.VMEM) for value in values]


LIMIT = pltpu.CompilerParams(vmem_limit_bytes=8 << 20)


def cost(flops, size):
    return pl.CostEstimate(flops=flops // 1000, bytes_accessed=size // 1000, transcendentals=0)


def split(value):
    high = value.astype(BF16)
    return high, (value - high.astype(F32)).astype(BF16)


def dot(left, right):
    return jnp.dot(left, right, preferred_element_type=F32)


def block_factors(k, signs, pattern, row_blocks):
    signed = (2 * signs[k : k + 1, :] - 1).astype(F32)
    return [signed[:, j * BLK : (j + 1) * BLK] * pattern[k, j].astype(F32) for j in range(row_blocks)]


def block_sketch(block_ref, here, factors, table):
    total = block_ref[here, :BLK] * factors[0]
    for j in range(1, len(factors)):
        total = total + block_ref[here, j * BLK : (j + 1) * BLK] * factors[j]
    high, rest = split(total)
    low = (total - high.astype(F32) - rest.astype(F32)).astype(BF16)
    return dot(high, table) + dot(rest, table) + dot(low, table)


def first_sketch_kernel(pattern_ref, whole_ref, sign_ref, out_ref, held_ref, sems, signs, pattern):
    steps = sems.shape[0] - 2
    step = held_ref.shape[0] // steps
    copies = [
        pltpu.make_async_copy(pattern_ref, pattern, sems.at[steps]),
        pltpu.make_async_copy(sign_ref, signs, sems.at[steps + 1]),
    ]
    for i in range(steps):
        here = pl.ds(i * step, step)
        copies.append(pltpu.make_async_copy(whole_ref.at[here], held_ref.at[here], sems.at[i]))
    for copy in copies:
        copy.start()
    table = hadamard_table(BLK).astype(BF16)
    copies[0].wait()
    copies[1].wait()
    factors = block_factors(0, signs, pattern, held_ref.shape[1] // BLK)
    for i in range(steps):
        copies[2 + i].wait()
        here = slice(i * step, (i + 1) * step)
        out_ref[here, :] = block_sketch(held_ref, here, factors, table)


def first_sketch(unfolding, pattern_rows, sign_rows):
    rows, cols = unfolding.shape
    return pl.pallas_call(
        first_sketch_kernel,
        in_specs=[HBM] * 3,
        out_specs=[VMEM] * 2,
        out_shape=[on_chip(rows, BLK), on_chip(rows, cols)],
        scratch_shapes=[
            pltpu.SemaphoreType.DMA((10,)),
            pltpu.VMEM(sign_rows.shape, jnp.int32),
            pltpu.SMEM(pattern_rows.shape, jnp.int32),
        ],
        cost_estimate=cost(rows * cols * 2, rows * cols * 4),
        compiler_params=LIMIT,
        name="first_sketch",
    )(*[pltpu.with_memory_space_constraint(x, pltpu.HBM) for x in (pattern_rows, unfolding, sign_rows)])


def second_sketch_kernel(pattern_ref, sign_ref, block_ref, out_ref, high_ref, low_ref, sems, signs, pattern):
    copies = [
        pltpu.make_async_copy(pattern_ref, pattern, sems.at[0]),
        pltpu.make_async_copy(sign_ref, signs, sems.at[1]),
    ]
    for copy in copies:
        copy.start()
    table = hadamard_table(BLK).astype(BF16)
    step = 64
    for i in range(block_ref.shape[0] // step):
        here = slice(i * step, (i + 1) * step)
        high_ref[here, :], low_ref[here, :] = split(block_ref[here, :])
    for copy in copies:
        copy.wait()
    factors = block_factors(1, signs, pattern, block_ref.shape[1] // BLK)
    for i in range(block_ref.shape[0] // step):
        here = slice(i * step, (i + 1) * step)
        out_ref[here, :] = block_sketch(block_ref, here, factors, table)


def second_sketch(block, pattern_rows, sign_rows):
    rows, cols = block.shape
    return pl.pallas_call(
        second_sketch_kernel,
        in_specs=[HBM, HBM, VMEM],
        out_specs=[VMEM] * 3,
        out_shape=[on_chip(rows, BLK), on_chip(rows, cols, dtype=BF16), on_chip(rows, cols, dtype=BF16)],
        scratch_shapes=[
            pltpu.SemaphoreType.DMA((2,)),
            pltpu.VMEM(sign_rows.shape, jnp.int32),
            pltpu.SMEM(pattern_rows.shape, jnp.int32),
        ],
        cost_estimate=cost(rows * cols * 2, rows * cols * 4),
        compiler_params=LIMIT,
        name="second_sketch",
    )(*[pltpu.with_memory_space_constraint(x, pltpu.HBM) for x in (pattern_rows, sign_rows)], *held(block))


def first_gram_kernel(own_ref, got_ref, sketch_ref, turned_ref, parts_ref, gram_ref):
    sketch = own_ref[...] + got_ref[...]
    sketch_ref[...] = sketch
    turned = sketch.T
    turned_ref[...] = turned
    parts_ref[:BLK], parts_ref[BLK:] = split(turned)
    gram_ref[...] = jnp.dot(turned, sketch, precision=HIGHEST)


def first_gram(own, got):
    rows = own.shape[0]
    return pl.pallas_call(
        first_gram_kernel,
        in_specs=[VMEM] * 2,
        out_specs=[VMEM] * 4,
        out_shape=[
            on_chip(rows, BLK),
            on_chip(BLK, rows),
            on_chip(2 * BLK, rows, dtype=BF16),
            on_chip(BLK, BLK),
        ],
        cost_estimate=cost(rows * BLK * BLK * 12, rows * BLK * 8),
        compiler_params=LIMIT,
        name="first_gram",
    )(*held(own, got))


def second_gram_kernel(own_ref, got_ref, before_ref, gram_ref, sketch_ref, parts_ref, keep_ref, send_ref, packed):
    sketch = own_ref[...] + got_ref[...]
    sketch_ref[...] = sketch
    turned = sketch.T
    parts_ref[:BLK], parts_ref[BLK:] = split(turned)
    packed[:BLK] = gram_ref[...]
    packed[BLK : 2 * BLK] = jnp.dot(before_ref[...], sketch, precision=HIGHEST)
    packed[2 * BLK :] = jnp.dot(turned, sketch, precision=HIGHEST)
    half = keep_ref.shape[0]
    core = lax.axis_index("rows") & 1
    keep_ref[...] = packed[pl.ds(pl.multiple_of(core * half, half), half), :]
    send_ref[...] = packed[pl.ds(pl.multiple_of((1 - core) * half, half), half), :]


def second_gram(own, got, before, gram, after):
    rows = own.shape[0]
    half = (3 * BLK // 2, BLK)

    def body(*refs):
        second_gram_kernel(*refs[:4], *refs[-5:])

    return pl.pallas_call(
        body,
        in_specs=[VMEM] * (4 + len(after)),
        out_specs=[VMEM] * 4,
        out_shape=[
            on_chip(rows, BLK),
            on_chip(2 * BLK, rows, dtype=BF16),
            on_chip(*half),
            on_chip(*half),
        ],
        scratch_shapes=[pltpu.VMEM((3 * BLK, BLK), F32)],
        cost_estimate=cost(rows * BLK * BLK * 24, rows * BLK * 8),
        compiler_params=LIMIT,
        name="second_gram",
    )(*held(own, got, before, gram, *after))


def project_kernel(parts_ref, high_ref, low_ref, give_1, keep_1, give_0, keep_0):
    row = lax.axis_index("rows")
    core, right, near, far = row & 1, (row >> 1) & 1, (row >> 2) & 1, row >> 3
    for flip, give_ref, keep_ref in ((1, give_1, keep_1), (0, give_0, keep_0)):
        for t in range(4):
            block = (far ^ (t >> 1)) * 4 + (right ^ flip) * 2 + (near ^ (t & 1))
            here = pl.ds(pl.multiple_of(block * 2 * BLK, 2 * BLK), 2 * BLK)
            both = dot(parts_ref[...], high_ref[:, here])
            total = both[:BLK] + both[BLK:] + dot(parts_ref[:BLK, :], low_ref[:, here])
            left, other = total[:, :BLK], total[:, BLK:]
            give_ref[t] = jnp.where(core == 0, other, left)
            keep_ref[t] = jnp.where(core == 0, left, other)


def project(parts, high, low, after=()):
    rows, cols = high.shape

    def body(*refs):
        project_kernel(*refs[:3], *refs[-4:])

    return pl.pallas_call(
        body,
        in_specs=[VMEM] * (3 + len(after)),
        out_specs=[VMEM] * 4,
        out_shape=[on_chip(4, BLK, BLK)] * 4,
        cost_estimate=cost(rows * cols * BLK * 6, rows * cols * 4),
        compiler_params=LIMIT,
        name="project",
    )(*held(parts, high, low, *after))


def add_parts_kernel(terms, outs):
    for i, out in enumerate(outs):
        here = slice(None) if len(outs) == 1 else i
        total = terms[0][here]
        for term in terms[1:]:
            total = total + term[here]
        out[...] = total


def add_parts(terms, parts, after=()):
    dims = terms[0].shape
    size = math.prod(dims)
    count = len(terms)

    def body(*refs):
        add_parts_kernel(refs[:count], refs[-parts:])

    return pl.pallas_call(
        body,
        in_specs=[VMEM] * (count + len(after)),
        out_specs=[VMEM] * parts,
        out_shape=[on_chip(*(dims if parts == 1 else dims[1:]))] * parts,
        cost_estimate=cost(size, size),
        compiler_params=LIMIT,
        name="add_parts",
    )(*held(*terms, *after))


def pieces_kernel(refs, outs):
    count = len(refs) // 2
    for i, out in enumerate(outs):
        for h in range(2):
            terms = [ref[i] for ref in refs[h * count : (h + 1) * count]]
            out[h * BLK : (h + 1) * BLK] = sum(terms[1:], terms[0])


def piece_sums(first, second):
    terms = (*first, *second)

    def body(*refs):
        pieces_kernel(refs[:-4], refs[-4:])

    return pl.pallas_call(
        body,
        in_specs=[VMEM] * len(terms),
        out_specs=[VMEM] * 4,
        out_shape=[on_chip(2 * BLK, BLK)] * 4,
        cost_estimate=cost(8 * BLK * BLK, 96 * BLK * BLK),
        compiler_params=LIMIT,
        name="piece_sums",
    )(*held(*terms))


def factor_panel(parts, start):
    diagonal = parts[0][:, start : start + PANEL]
    columns = [jnp.broadcast_to(diagonal[:, k : k + 1], (PANEL, BLK)) for k in range(PANEL)]
    rows = lax.broadcasted_iota(jnp.int32, (PANEL, BLK), 0)
    pivots = jnp.ones((PANEL, BLK), F32)
    for j in range(PANEL):
        pivot = jnp.broadcast_to(columns[j][j : j + 1, :], (PANEL, BLK))
        multiplier = jnp.where(rows > j, columns[j] / pivot, 0.0)
        for k in range(j + 1, PANEL):
            columns[k] = columns[k] - multiplier * columns[k][j : j + 1, :]
        parts = [part - multiplier * part[j : j + 1, :] for part in parts]
        pivots = jnp.where(rows == j, pivot, pivots)
    scale = lax.rsqrt(pivots)
    return [part * scale for part in parts]


def factor_block(work):
    for panel in range(BLK // PANEL):
        start = panel * PANEL
        stop = start + PANEL
        parts = [work[start:stop, c * BLK : (c + 1) * BLK] for c in range(3)]
        parts = factor_panel(parts, start)
        for c in range(3):
            work[start:stop, c * BLK : (c + 1) * BLK] = parts[c]
        if stop < BLK:
            left = parts[0].T[stop:]
            work[stop:, :] = work[stop:, :] - jnp.dot(left, jnp.concatenate(parts, 1), precision=HIGHEST)


def factor_kernel(total_rows, own_ref, got_ref, out_ref, work, packed):
    half = own_ref.shape[0]
    core = lax.axis_index("rows") & 1
    packed[pl.ds(pl.multiple_of(core * half, half), half), :] = own_ref[...]
    packed[pl.ds(pl.multiple_of((1 - core) * half, half), half), :] = got_ref[...]
    row = lax.broadcasted_iota(jnp.int32, (BLK, BLK), 0)
    col = lax.broadcasted_iota(jnp.int32, (BLK, BLK), 1)
    eye = (row == col).astype(F32)
    work[:, :BLK] = packed[:BLK] + float(total_rows) * eye
    work[:, BLK : 2 * BLK] = packed[BLK : 2 * BLK]
    work[:, 2 * BLK :] = eye
    factor_block(work)
    out_ref[:BLK, :BLK] = work[:, 2 * BLK :]
    out_ref[:BLK, BLK:] = jnp.zeros((BLK, BLK), F32)
    above = work[:, BLK : 2 * BLK]
    product = jnp.dot(above.T, work[:, BLK:], precision=HIGHEST)
    work[:, :BLK] = packed[2 * BLK :] + float(total_rows) * eye - product[:, :BLK]
    work[:, BLK : 2 * BLK] = -product[:, BLK:]
    work[:, 2 * BLK :] = eye
    factor_block(work)
    out_ref[BLK:, :] = work[:, BLK:]


def inverse_factor(own, got, total_rows):
    def body(*refs):
        factor_kernel(total_rows, *refs)

    return pl.pallas_call(
        body,
        in_specs=[VMEM] * 2,
        out_specs=VMEM,
        out_shape=on_chip(RANK, RANK),
        scratch_shapes=[pltpu.VMEM((BLK, 3 * BLK), F32), pltpu.VMEM((3 * BLK, BLK), F32)],
        cost_estimate=cost(0, RANK * RANK * 8),
        compiler_params=LIMIT,
        name="inverse_factor",
    )(*held(own, got))


def core_kernel(scale, first_ref, second_ref, inverse_ref, out_ref):
    t_high, t_low = split(inverse_ref[...].T)
    s_high, s_low = split(jnp.concatenate([first_ref[...], second_ref[...]], 1))
    total = dot(s_high, t_high) + dot(s_high, t_low) + dot(s_low, t_high)
    out_ref[...] = total * scale


def scaled_core(first, second, inverse, scale):
    rows = first.shape[0]

    def body(*refs):
        core_kernel(scale, *refs)

    return pl.pallas_call(
        body,
        in_specs=[VMEM] * 3,
        out_specs=VMEM,
        out_shape=jax.ShapeDtypeStruct((rows, RANK), F32),
        cost_estimate=cost(rows * RANK * RANK * 6, rows * RANK * 8),
        compiler_params=LIMIT,
        name="scaled_core",
    )(*held(first, second, inverse))


def remainder_kernel(inverse_ref, p0, p1, p2, p3, o0, o1, o2, o3, work):
    work[...] = jnp.dot(inverse_ref[...], (p0[...] + p1[...]) + (p2[...] + p3[...]), precision=HIGHEST)
    device = lax.axis_index("rows")
    for m, out in enumerate((o0, o1, o2, o3)):
        for t in range(4):
            rank_block = (4 * t + m) ^ device
            out[t] = work[pl.ds(pl.multiple_of(rank_block * 16, 16), 16), :]


def remainder_pieces(inverse, pieces):
    return pl.pallas_call(
        remainder_kernel,
        in_specs=[VMEM] * 5,
        out_specs=[VMEM] * 4,
        out_shape=[on_chip(4, 16, BLK)] * 4,
        scratch_shapes=[pltpu.VMEM((RANK, BLK), F32)],
        cost_estimate=cost(RANK * RANK * BLK * 12, RANK * BLK * 8),
        compiler_params=LIMIT,
        name="remainder_pieces",
    )(*held(inverse, *pieces))


def collect_kernel(r0, r1, r2, r3, o1, o2, o3):
    for t, out in ((1, o1), (2, o2), (3, o3)):
        for m, piece in enumerate((r0, r1, r2, r3)):
            out[m] = piece[t]


def collect(firsts):
    return pl.pallas_call(
        collect_kernel,
        in_specs=[VMEM] * 4,
        out_specs=[VMEM] * 3,
        out_shape=[on_chip(4, 16, BLK)] * 3,
        cost_estimate=cost(0, 16 * BLK * 64),
        compiler_params=LIMIT,
        name="collect",
    )(*held(*firsts))


def arrange_kernel(r0, r1, r2, r3, s1, s2, s3, out_ref, work):
    row = lax.axis_index("rows")
    core, right, deep = row & 1, (row >> 1) & 1, row >> 2
    firsts = (r0, r1, r2, r3)
    later = (None, s1, s2, s3)
    for t in range(4):
        for m in range(4):
            there = deep ^ t
            mode = (there & 1) * 4 + (there >> 1) * 2 + (right ^ (m >> 1))
            work[mode, core ^ (m & 1)] = firsts[m][0] if t == 0 else later[t][m]
    for mode in range(MODE):
        for c in range(2):
            out_ref[:, mode, c * BLK : (c + 1) * BLK] = work[mode, c]


def arrange(firsts, later):
    out = pl.pallas_call(
        arrange_kernel,
        in_specs=[VMEM] * 7,
        out_specs=VMEM,
        out_shape=jax.ShapeDtypeStruct((16, MODE, 2 * BLK), F32),
        scratch_shapes=[pltpu.VMEM((MODE, 2, 16, BLK), F32)],
        cost_estimate=cost(0, 16 * BLK * 64),
        compiler_params=LIMIT,
        name="arrange",
    )(*held(*firsts, *later))
    return out.reshape(16 * MODE, 2 * BLK)


def rows_permute(value, mask):
    size = lax.axis_size("rows")
    return lax.ppermute(value, "rows", [(i, i ^ mask) for i in range(size)])


def local(unfolding, pattern, sign_bits):
    total_rows = unfolding.shape[0] * lax.axis_size("rows")
    swap = [(0, 1), (1, 0)]
    pattern_rows, sign_rows = pattern.T, sign_bits.T
    own_0, block = first_sketch(unfolding, pattern_rows, sign_rows)
    got_0 = lax.ppermute(own_0, "cols", swap)
    own_1, high, low = second_sketch(block, pattern_rows, sign_rows)
    got_1 = lax.ppermute(own_1, "cols", swap)
    first, turned, parts, gram = first_gram(own_0, got_0)
    give, keep, give_0, keep_0 = project(parts, high, low)
    send_0, = add_parts((keep, rows_permute(give, 1)), 1)
    second, parts, gram_keep, gram_send = second_gram(own_1, got_1, turned, gram, (keep_0,))
    gram, = add_parts((gram_keep, rows_permute(gram_send, 1)), 1)
    give, keep, give_1, keep_1 = project(parts, high, low, (send_0,))
    send_1, = add_parts((keep, rows_permute(give, 1)), 1, (gram,))
    got_0 = rows_permute(send_0, 2)
    pieces = piece_sums(
        (keep_0, rows_permute(give_0, 1), got_0),
        (keep_1, rows_permute(give_1, 1), rows_permute(send_1, 2)),
    )
    gram, = add_parts((gram, rows_permute(gram, 4)), 1, (got_0,))
    gram, = add_parts((gram, rows_permute(gram, 8)), 1, pieces)
    gram, = add_parts((gram, rows_permute(gram, 2)), 1)
    inverse = inverse_factor(gram, rows_permute(gram, 1), total_rows)
    gathered = []
    for k in range(4):
        pairs = []
        for i in range(16):
            for y in range(2):
                to = (i & 3) | (y << 2) | ((i & 8) ^ ((k >> 1) << 3))
                pairs.append((2 * i + y, 2 * to + (((i >> 2) & 1) ^ (k & 1))))
        gathered.append(lax.ppermute(pieces[k], ("rows", "cols"), pairs))
    parts = remainder_pieces(inverse, gathered)
    core_scaled = scaled_core(first, second, inverse, math.sqrt(total_rows))
    firsts = [parts[0]] + [rows_permute(parts[m], m) for m in (1, 2, 3)]
    later = [rows_permute(part, 4 * t) for t, part in zip((1, 2, 3), collect(firsts))]
    return core_scaled, arrange(firsts, later)


def sketch_matrix(pattern, sign_bits, block_size):
    blocks = sign_bits.shape[1]
    rows_here = sign_bits.shape[0]
    factor = jnp.repeat(pattern, block_size, axis=0) * (2 * sign_bits - 1)
    tiled_table = jnp.tile(hadamard_table(block_size), (rows_here // block_size, 1))
    expanded = factor.astype(F32)[:, :, None] * tiled_table[:, None, :]
    return expanded.reshape(rows_here, blocks * block_size)


def inner_rows(left_side, right_side):
    return lax.dot_general(left_side, right_side, (((0,), (0,)), ((), ())), precision=HIGHEST)


def local_any(unfolding, pattern, sign_bits):
    sketch_map = sketch_matrix(pattern, sign_bits, BLK)
    row_devices = lax.axis_size("rows")
    col_devices = lax.axis_size("cols")
    total_rows = unfolding.shape[0] * row_devices
    sketch = lax.psum(jnp.dot(unfolding, sketch_map, precision=HIGHEST), "cols")
    gram_matrix = lax.psum(inner_rows(sketch, sketch), "rows")
    gram_matrix = gram_matrix + float(total_rows) * jnp.eye(RANK, dtype=F32)
    lower_factor = jnp.linalg.cholesky(gram_matrix)
    basis_rows = lax.linalg.triangular_solve(lower_factor, sketch, left_side=False, lower=True, transpose_a=True)
    mode_local = MODE // col_devices
    rest_cols = unfolding.shape[1] // mode_local
    rank_share = RANK // row_devices
    reduced = lax.psum_scatter(inner_rows(basis_rows, unfolding), "rows", scatter_dimension=0, tiled=True)
    grouped = reduced.reshape(rank_share, mode_local, rest_cols)
    regrouped = lax.all_to_all(grouped, "cols", split_axis=2, concat_axis=1, tiled=True)
    return basis_rows * math.sqrt(total_rows), regrouped.reshape(rank_share * MODE, regrouped.shape[2])


def solution(mesh):
    in_specs = (P("rows", "cols"), P("cols", None), P("cols", None))
    out_specs = (P("rows", None), P("rows", "cols"))
    body = local if (mesh.shape["rows"], mesh.shape["cols"]) == (16, 2) else local_any
    return jax.shard_map(body, mesh=mesh, in_specs=in_specs, out_specs=out_specs, check_vma=False)
```

```python
import math

import jax
import jax.numpy as jnp
from jax import lax
from jax.experimental import pallas as pl
from jax.experimental.pallas import tpu as pltpu
from jax.sharding import PartitionSpec as P

RANK = 256
BLK = 128
MODE = 8
PANEL = 16
HIGHEST = lax.Precision.HIGHEST
F32 = jnp.float32
BF16 = jnp.bfloat16
VMEM = pl.BlockSpec(memory_space=pltpu.VMEM)
HBM = pl.BlockSpec(memory_space=pltpu.HBM)


def hadamard_table(table_size):
    row_index = lax.broadcasted_iota(jnp.int32, (table_size, table_size), 0)
    col_index = lax.broadcasted_iota(jnp.int32, (table_size, table_size), 1)
    both = row_index & col_index
    parity = jnp.zeros((table_size, table_size), jnp.int32)
    for bit_level in range(table_size.bit_length() - 1):
        parity = parity ^ (both >> bit_level)
    return (1 - 2 * (parity & 1)).astype(F32)


def on_chip(*dims, dtype=F32):
    return pltpu.VMEM(dims, dtype)


def held(*values):
    return [pltpu.with_memory_space_constraint(value, pltpu.VMEM) for value in values]


LIMIT = pltpu.CompilerParams(vmem_limit_bytes=8 << 20)


def cost(flops, size):
    return pl.CostEstimate(flops=flops, bytes_accessed=size, transcendentals=0)


def split(value):
    high = value.astype(BF16)
    return high, (value - high.astype(F32)).astype(BF16)


def dot(left, right):
    return jnp.dot(left, right, preferred_element_type=F32)


def sketch_kernel(first_row, pattern_ref, whole_ref, sign_ref, out_ref, band_ref, sems, signs, pattern):
    steps = sems.shape[0] - 2
    rows = band_ref.shape[0]
    step = rows // steps
    copies = [
        pltpu.make_async_copy(pattern_ref, pattern, sems.at[steps]),
        pltpu.make_async_copy(sign_ref, signs, sems.at[steps + 1]),
    ]
    for i in range(steps):
        here = pl.ds(first_row + i * step, step)
        copies.append(pltpu.make_async_copy(whole_ref.at[here], band_ref.at[pl.ds(i * step, step)], sems.at[i]))
    for copy in copies:
        copy.start()
    table = hadamard_table(BLK).astype(BF16)
    copies[0].wait()
    copies[1].wait()
    col_blocks = signs.shape[0]
    row_blocks = band_ref.shape[1] // BLK
    factors = []
    for k in range(col_blocks):
        signed = (2 * signs[k : k + 1, :] - 1).astype(F32)
        factors.append([signed[:, j * BLK : (j + 1) * BLK] * pattern[k, j].astype(F32) for j in range(row_blocks)])
    for i in range(steps):
        copies[2 + i].wait()
        here = slice(i * step, (i + 1) * step)
        for k in range(col_blocks):
            total = jnp.zeros((step, BLK), F32)
            for j in range(row_blocks):
                total = total + band_ref[here, j * BLK : (j + 1) * BLK] * factors[k][j]
            high, rest = split(total)
            low = (total - high.astype(F32) - rest.astype(F32)).astype(BF16)
            out_ref[here, k * BLK : (k + 1) * BLK] = dot(high, table) + dot(rest, table) + dot(low, table)


def sketch_band(unfolding, pattern_rows, sign_rows, band, bands):
    rows, cols = unfolding.shape
    rows //= bands

    def body(*refs):
        sketch_kernel(band * rows, *refs)

    return pl.pallas_call(
        body,
        in_specs=[HBM] * 3,
        out_specs=[VMEM] * 2,
        out_shape=[on_chip(rows, RANK), on_chip(rows, cols)],
        scratch_shapes=[
            pltpu.SemaphoreType.DMA((6,)),
            pltpu.VMEM(sign_rows.shape, jnp.int32),
            pltpu.SMEM(pattern_rows.shape, jnp.int32),
        ],
        cost_estimate=cost(rows * cols * 4, rows * cols * 4),
        compiler_params=LIMIT,
        name="sketch_band",
    )(*[pltpu.with_memory_space_constraint(x, pltpu.HBM) for x in (pattern_rows, unfolding, sign_rows)])


def gram_kernel(own_ref, got_ref, before_ref, sketch_ref, high_ref, low_ref, packed_ref, keep_ref, send_ref):
    sketch = own_ref[...] + got_ref[...]
    sketch_ref[...] = sketch
    turned = sketch.T
    high, low = split(turned)
    high_ref[...] = high
    low_ref[...] = low
    top = jnp.dot(turned[:BLK], sketch, precision=HIGHEST)
    low_corner = jnp.dot(turned[BLK:], sketch[:, BLK:], precision=HIGHEST)
    parts = [top[:, :BLK], top[:, BLK:], low_corner]
    for i, part in enumerate(parts):
        here = slice(i * BLK, (i + 1) * BLK)
        packed_ref[here] = part if before_ref is None else part + before_ref[here]
    if keep_ref is not None:
        half = keep_ref.shape[0]
        core = lax.axis_index("rows") & 1
        keep_ref[...] = packed_ref[pl.ds(pl.multiple_of(core * half, half), half), :]
        send_ref[...] = packed_ref[pl.ds(pl.multiple_of((1 - core) * half, half), half), :]


def gram_band(own, got, before, after=()):
    rows = own.shape[0]
    first = before is None
    operands = held(own, got) if first else held(own, got, before, *after)
    packed = (3 * BLK, BLK)
    half = (3 * BLK // 2, BLK)

    def body(*refs):
        if first:
            gram_kernel(*refs[:2], None, *refs[2:], None, None)
        else:
            gram_kernel(*refs[:3], *refs[-6:-3], refs[-1], *refs[-3:-1])

    return pl.pallas_call(
        body,
        in_specs=[VMEM] * len(operands),
        out_specs=[VMEM] * (4 if first else 5),
        out_shape=[
            on_chip(rows, RANK),
            on_chip(RANK, rows, dtype=BF16),
            on_chip(RANK, rows, dtype=BF16),
            *([on_chip(*packed)] if first else [on_chip(*half)] * 2),
        ],
        scratch_shapes=[] if first else [pltpu.VMEM(packed, F32)],
        cost_estimate=cost(rows * RANK * RANK * 12, rows * RANK * 8),
        compiler_params=LIMIT,
        name="gram_band",
    )(*operands)


def project_kernel(flips, high_ref, low_ref, band_ref, before, outs):
    row = lax.axis_index("rows")
    core, right, near, far = row & 1, (row >> 1) & 1, (row >> 2) & 1, row >> 3
    for i, flip in enumerate(flips):
        for side in range(2):
            out = outs[2 * i + side]
            for t in range(2):
                block = (far ^ core ^ 1 ^ side) * 4 + (right ^ flip) * 2 + (near ^ t)
                a_high, a_low = split(band_ref[:, pl.ds(pl.multiple_of(block * 2 * BLK, 2 * BLK), 2 * BLK)])
                total = dot(high_ref[...], a_high) + dot(high_ref[...], a_low) + dot(low_ref[...], a_high)
                out[t] = total if before is None else total + before[2 * i + side][t]


def project_band(flips, high, low, band, before=(), after=()):
    rows, cols = band.shape
    operands = held(high, low, band, *before, *after)
    count = 2 * len(flips)

    def body(*refs):
        project_kernel(flips, *refs[:3], refs[3 : 3 + count] if before else None, refs[-count:])

    return pl.pallas_call(
        body,
        in_specs=[VMEM] * len(operands),
        out_specs=[VMEM] * count,
        out_shape=[on_chip(2, RANK, 2 * BLK)] * count,
        cost_estimate=cost(rows * cols * RANK * 3 * len(flips), rows * cols * 4),
        compiler_params=LIMIT,
        name="project_band",
    )(*operands)


def add_parts_kernel(terms, outs):
    for i, out in enumerate(outs):
        here = slice(None) if len(outs) == 1 else i
        total = terms[0][here]
        for term in terms[1:]:
            total = total + term[here]
        out[...] = total


def add_parts(terms, parts, after=()):
    dims = terms[0].shape
    size = math.prod(dims)
    count = len(terms)

    def body(*refs):
        add_parts_kernel(refs[:count], refs[-parts:])

    return pl.pallas_call(
        body,
        in_specs=[VMEM] * (count + len(after)),
        out_specs=[VMEM] * parts,
        out_shape=[on_chip(*(dims if parts == 1 else dims[1:]))] * parts,
        cost_estimate=cost(size, size),
        compiler_params=LIMIT,
        name="add_parts",
    )(*held(*terms, *after))


def factor_panel(parts, start):
    diagonal = parts[0][:, start : start + PANEL]
    columns = [jnp.broadcast_to(diagonal[:, k : k + 1], (PANEL, BLK)) for k in range(PANEL)]
    rows = lax.broadcasted_iota(jnp.int32, (PANEL, BLK), 0)
    pivots = jnp.ones((PANEL, BLK), F32)
    for j in range(PANEL):
        pivot = jnp.broadcast_to(columns[j][j : j + 1, :], (PANEL, BLK))
        multiplier = jnp.where(rows > j, columns[j] / pivot, 0.0)
        for k in range(j + 1, PANEL):
            columns[k] = columns[k] - multiplier * columns[k][j : j + 1, :]
        parts = [part - multiplier * part[j : j + 1, :] for part in parts]
        pivots = jnp.where(rows == j, pivot, pivots)
    scale = lax.rsqrt(pivots)
    return [part * scale for part in parts]


def factor_block(work):
    for panel in range(BLK // PANEL):
        start = panel * PANEL
        stop = start + PANEL
        parts = [work[start:stop, c * BLK : (c + 1) * BLK] for c in range(3)]
        parts = factor_panel(parts, start)
        for c in range(3):
            work[start:stop, c * BLK : (c + 1) * BLK] = parts[c]
        if stop < BLK:
            left = parts[0].T[stop:]
            work[stop:, :] = work[stop:, :] - jnp.dot(left, jnp.concatenate(parts, 1), precision=HIGHEST)


def factor_kernel(total_rows, own_ref, got_ref, out_ref, work, packed):
    half = own_ref.shape[0]
    core = lax.axis_index("rows") & 1
    packed[pl.ds(pl.multiple_of(core * half, half), half), :] = own_ref[...]
    packed[pl.ds(pl.multiple_of((1 - core) * half, half), half), :] = got_ref[...]
    row = lax.broadcasted_iota(jnp.int32, (BLK, BLK), 0)
    col = lax.broadcasted_iota(jnp.int32, (BLK, BLK), 1)
    eye = (row == col).astype(F32)
    work[:, :BLK] = packed[:BLK] + float(total_rows) * eye
    work[:, BLK : 2 * BLK] = packed[BLK : 2 * BLK]
    work[:, 2 * BLK :] = eye
    factor_block(work)
    out_ref[:BLK, :BLK] = work[:, 2 * BLK :]
    out_ref[:BLK, BLK:] = jnp.zeros((BLK, BLK), F32)
    above = work[:, BLK : 2 * BLK]
    product = jnp.dot(above.T, work[:, BLK:], precision=HIGHEST)
    work[:, :BLK] = packed[2 * BLK :] + float(total_rows) * eye - product[:, :BLK]
    work[:, BLK : 2 * BLK] = -product[:, BLK:]
    work[:, 2 * BLK :] = eye
    factor_block(work)
    out_ref[BLK:, :] = work[:, BLK:]


def inverse_factor(own, got, total_rows):
    def body(*refs):
        factor_kernel(total_rows, *refs)

    return pl.pallas_call(
        body,
        in_specs=[VMEM] * 2,
        out_specs=VMEM,
        out_shape=on_chip(RANK, RANK),
        scratch_shapes=[pltpu.VMEM((BLK, 3 * BLK), F32), pltpu.VMEM((3 * BLK, BLK), F32)],
        cost_estimate=cost(0, RANK * RANK * 8),
        compiler_params=LIMIT,
        name="inverse_factor",
    )(*held(own, got))


def core_kernel(scale, first_ref, second_ref, inverse_ref, out_ref):
    t_high, t_low = split(inverse_ref[...].T)
    band = first_ref.shape[0]
    for i, ref in enumerate((first_ref, second_ref)):
        s_high, s_low = split(ref[...])
        total = dot(s_high, t_high) + dot(s_high, t_low) + dot(s_low, t_high)
        out_ref[i * band : (i + 1) * band] = total * scale


def scaled_core(sketches, inverse, scale):
    rows = 2 * sketches[0].shape[0]

    def body(*refs):
        core_kernel(scale, *refs)

    return pl.pallas_call(
        body,
        in_specs=[VMEM] * 3,
        out_specs=VMEM,
        out_shape=jax.ShapeDtypeStruct((rows, RANK), F32),
        cost_estimate=cost(rows * RANK * RANK * 6, rows * RANK * 8),
        compiler_params=LIMIT,
        name="scaled_core",
    )(*held(*sketches, inverse))


def remainder_kernel(inverse_ref, p0, p1, o0, o1, o2, o3, work):
    work[...] = jnp.dot(inverse_ref[...], p0[...] + p1[...], precision=HIGHEST)
    device = lax.axis_index("rows")
    for m, out in enumerate((o0, o1, o2, o3)):
        for t in range(4):
            rank_block = (4 * t + m) ^ device
            out[t] = work[pl.ds(pl.multiple_of(rank_block * 16, 16), 16), :]


def remainder_pieces(inverse, pieces):
    return pl.pallas_call(
        remainder_kernel,
        in_specs=[VMEM] * 3,
        out_specs=[VMEM] * 4,
        out_shape=[on_chip(4, 16, 2 * BLK)] * 4,
        scratch_shapes=[pltpu.VMEM((RANK, 2 * BLK), F32)],
        cost_estimate=cost(RANK * RANK * BLK * 24, RANK * BLK * 16),
        compiler_params=LIMIT,
        name="remainder_pieces",
    )(*held(inverse, *pieces))


def collect_kernel(r0, r1, r2, r3, o0, o1, o2, o3):
    for t, out in enumerate((o0, o1, o2, o3)):
        out[0] = r0[t] + r1[t]
        out[1] = r2[t] + r3[t]


def collect(firsts):
    return pl.pallas_call(
        collect_kernel,
        in_specs=[VMEM] * 4,
        out_specs=[VMEM] * 4,
        out_shape=[on_chip(2, 16, 2 * BLK)] * 4,
        cost_estimate=cost(0, 16 * BLK * 64),
        compiler_params=LIMIT,
        name="collect",
    )(*held(*firsts))


def arrange_kernel(p0, p1, p2, p3, out_ref, work):
    row = lax.axis_index("rows")
    right, deep = (row >> 1) & 1, row >> 2
    for t, piece in enumerate((p0, p1, p2, p3)):
        there = deep ^ t
        for m in range(2):
            work[(there & 1) * 4 + (there >> 1) * 2 + (right ^ m)] = piece[m]
    for mode in range(MODE):
        out_ref[:, mode, :] = work[mode]


def arrange(pieces):
    out = pl.pallas_call(
        arrange_kernel,
        in_specs=[VMEM] * 4,
        out_specs=VMEM,
        out_shape=jax.ShapeDtypeStruct((16, MODE, 2 * BLK), F32),
        scratch_shapes=[pltpu.VMEM((MODE, 16, 2 * BLK), F32)],
        cost_estimate=cost(0, 16 * BLK * 64),
        compiler_params=LIMIT,
        name="arrange",
    )(*held(*pieces))
    return out.reshape(16 * MODE, 2 * BLK)


def rows_permute(value, mask):
    size = lax.axis_size("rows")
    return lax.ppermute(value, "rows", [(i, i ^ mask) for i in range(size)])


def local(unfolding, pattern, sign_bits):
    total_rows = unfolding.shape[0] * lax.axis_size("rows")
    own, got, bands = [], [], []
    for band in range(2):
        part, rows_here = sketch_band(unfolding, pattern.T, sign_bits.T, band, 2)
        own.append(part)
        bands.append(rows_here)
        got.append(lax.ppermute(part, "cols", [(0, 1), (1, 0)]))
    first, high, low, packed = gram_band(own[0], got[0], None)
    before = project_band((1, 0), high, low, bands[0])
    second, high, low, gram_keep, gram_send = gram_band(own[1], got[1], packed, before[:1])
    gram, = add_parts((gram_keep, rows_permute(gram_send, 1)), 1)
    give, keep = project_band((1,), high, low, bands[1], before[:2])
    send, = add_parts((keep, rows_permute(give, 1)), 1, (gram,))
    give, keep = project_band((0,), high, low, bands[1], before[2:])
    give_got, send_got = rows_permute(give, 1), rows_permute(send, 2)
    gram, = add_parts((gram, rows_permute(gram, 4)), 1)
    gram, = add_parts((gram, rows_permute(gram, 8)), 1)
    gram, = add_parts((gram, rows_permute(gram, 2)), 1)
    pieces = add_parts((keep, give_got, send_got), 2, (gram,))
    inverse = inverse_factor(gram, rows_permute(gram, 1), total_rows)
    gathered = []
    for k in range(2):
        pairs = []
        for i in range(16):
            for y in range(2):
                to = (i & 3) | (y << 2) | ((i & 8) ^ ((i & 1) << 3))
                pairs.append((2 * i + y, 2 * to + (((i >> 2) & 1) ^ k)))
        gathered.append(lax.ppermute(pieces[k], ("rows", "cols"), pairs))
    parts = remainder_pieces(inverse, gathered)
    core_scaled = scaled_core((first, second), inverse, math.sqrt(total_rows))
    sums = collect([parts[0]] + [rows_permute(parts[m], m) for m in (1, 2, 3)])
    return core_scaled, arrange([sums[0]] + [rows_permute(sums[t], 4 * t) for t in (1, 2, 3)])


def sketch_matrix(pattern, sign_bits, block_size):
    blocks = sign_bits.shape[1]
    rows_here = sign_bits.shape[0]
    factor = jnp.repeat(pattern, block_size, axis=0) * (2 * sign_bits - 1)
    tiled_table = jnp.tile(hadamard_table(block_size), (rows_here // block_size, 1))
    expanded = factor.astype(F32)[:, :, None] * tiled_table[:, None, :]
    return expanded.reshape(rows_here, blocks * block_size)


def inner_rows(left_side, right_side):
    return lax.dot_general(left_side, right_side, (((0,), (0,)), ((), ())), precision=HIGHEST)


def local_any(unfolding, pattern, sign_bits):
    sketch_map = sketch_matrix(pattern, sign_bits, BLK)
    row_devices = lax.axis_size("rows")
    col_devices = lax.axis_size("cols")
    total_rows = unfolding.shape[0] * row_devices
    sketch = lax.psum(jnp.dot(unfolding, sketch_map, precision=HIGHEST), "cols")
    gram_matrix = lax.psum(inner_rows(sketch, sketch), "rows")
    gram_matrix = gram_matrix + float(total_rows) * jnp.eye(RANK, dtype=F32)
    lower_factor = jnp.linalg.cholesky(gram_matrix)
    basis_rows = lax.linalg.triangular_solve(lower_factor, sketch, left_side=False, lower=True, transpose_a=True)
    mode_local = MODE // col_devices
    rest_cols = unfolding.shape[1] // mode_local
    rank_share = RANK // row_devices
    reduced = lax.psum_scatter(inner_rows(basis_rows, unfolding), "rows", scatter_dimension=0, tiled=True)
    grouped = reduced.reshape(rank_share, mode_local, rest_cols)
    regrouped = lax.all_to_all(grouped, "cols", split_axis=2, concat_axis=1, tiled=True)
    return basis_rows * math.sqrt(total_rows), regrouped.reshape(rank_share * MODE, regrouped.shape[2])


def solution(mesh):
    in_specs = (P("rows", "cols"), P("cols", None), P("cols", None))
    out_specs = (P("rows", None), P("rows", "cols"))
    body = local if (mesh.shape["rows"], mesh.shape["cols"]) == (16, 2) else local_any
    return jax.shard_map(body, mesh=mesh, in_specs=in_specs, out_specs=out_specs, check_vma=False)
```

```python
import math

import jax
import jax.numpy as jnp
from jax import lax
from jax.experimental import pallas as pl
from jax.experimental.pallas import tpu as pltpu
from jax.sharding import PartitionSpec as P

RANK = 256
BLK = 128
MODE = 8
PANEL = 16
HIGHEST = lax.Precision.HIGHEST
F32 = jnp.float32
BF16 = jnp.bfloat16
VMEM = pl.BlockSpec(memory_space=pltpu.VMEM)
HBM = pl.BlockSpec(memory_space=pltpu.HBM)


def hadamard_table(table_size):
    row_index = lax.broadcasted_iota(jnp.int32, (table_size, table_size), 0)
    col_index = lax.broadcasted_iota(jnp.int32, (table_size, table_size), 1)
    both = row_index & col_index
    parity = jnp.zeros((table_size, table_size), jnp.int32)
    for bit_level in range(table_size.bit_length() - 1):
        parity = parity ^ (both >> bit_level)
    return (1 - 2 * (parity & 1)).astype(F32)


def on_chip(*dims, dtype=F32):
    return pltpu.VMEM(dims, dtype)


def held(*values):
    return [pltpu.with_memory_space_constraint(value, pltpu.VMEM) for value in values]


LIMIT = pltpu.CompilerParams(vmem_limit_bytes=8 << 20)


def cost(flops, size):
    return pl.CostEstimate(flops=flops, bytes_accessed=size, transcendentals=0)


def split(value):
    high = value.astype(BF16)
    return high, (value - high.astype(F32)).astype(BF16)


def dot(left, right):
    return jnp.dot(left, right, preferred_element_type=F32)


def sketch_kernel(first_row, pattern_ref, whole_ref, sign_ref, out_ref, band_ref, sems, signs, pattern):
    steps = sems.shape[0] - 2
    rows = band_ref.shape[0]
    step = rows // steps
    copies = [
        pltpu.make_async_copy(pattern_ref, pattern, sems.at[steps]),
        pltpu.make_async_copy(sign_ref, signs, sems.at[steps + 1]),
    ]
    for i in range(steps):
        here = pl.ds(first_row + i * step, step)
        copies.append(pltpu.make_async_copy(whole_ref.at[here], band_ref.at[pl.ds(i * step, step)], sems.at[i]))
    for copy in copies:
        copy.start()
    table = hadamard_table(BLK).astype(BF16)
    copies[0].wait()
    copies[1].wait()
    col_blocks = signs.shape[0]
    row_blocks = band_ref.shape[1] // BLK
    factors = []
    for k in range(col_blocks):
        signed = (2 * signs[k : k + 1, :] - 1).astype(F32)
        factors.append([signed[:, j * BLK : (j + 1) * BLK] * pattern[k, j].astype(F32) for j in range(row_blocks)])
    for i in range(steps):
        copies[2 + i].wait()
        here = slice(i * step, (i + 1) * step)
        for k in range(col_blocks):
            total = jnp.zeros((step, BLK), F32)
            for j in range(row_blocks):
                total = total + band_ref[here, j * BLK : (j + 1) * BLK] * factors[k][j]
            high, rest = split(total)
            low = (total - high.astype(F32) - rest.astype(F32)).astype(BF16)
            out_ref[here, k * BLK : (k + 1) * BLK] = dot(high, table) + dot(rest, table) + dot(low, table)


def sketch_band(unfolding, pattern_rows, sign_rows, band, bands):
    rows, cols = unfolding.shape
    rows //= bands

    def body(*refs):
        sketch_kernel(band * rows, *refs)

    return pl.pallas_call(
        body,
        in_specs=[HBM] * 3,
        out_specs=[VMEM] * 2,
        out_shape=[on_chip(rows, RANK), on_chip(rows, cols)],
        scratch_shapes=[
            pltpu.SemaphoreType.DMA((6,)),
            pltpu.VMEM(sign_rows.shape, jnp.int32),
            pltpu.SMEM(pattern_rows.shape, jnp.int32),
        ],
        cost_estimate=cost(rows * cols * 4, rows * cols * 4),
        compiler_params=LIMIT,
        name="sketch_band",
    )(*[pltpu.with_memory_space_constraint(x, pltpu.HBM) for x in (pattern_rows, unfolding, sign_rows)])


def gram_kernel(own_ref, got_ref, before_ref, sketch_ref, high_ref, low_ref, packed_ref, keep_ref, send_ref):
    sketch = own_ref[...] + got_ref[...]
    sketch_ref[...] = sketch
    turned = sketch.T
    high, low = split(turned)
    high_ref[...] = high
    low_ref[...] = low
    top = jnp.dot(turned[:BLK], sketch, precision=HIGHEST)
    low_corner = jnp.dot(turned[BLK:], sketch[:, BLK:], precision=HIGHEST)
    parts = [top[:, :BLK], top[:, BLK:], low_corner]
    for i, part in enumerate(parts):
        here = slice(i * BLK, (i + 1) * BLK)
        packed_ref[here] = part if before_ref is None else part + before_ref[here]
    if keep_ref is not None:
        half = keep_ref.shape[0]
        core = lax.axis_index("rows") & 1
        keep_ref[...] = packed_ref[pl.ds(pl.multiple_of(core * half, half), half), :]
        send_ref[...] = packed_ref[pl.ds(pl.multiple_of((1 - core) * half, half), half), :]


def gram_band(own, got, before, after=()):
    rows = own.shape[0]
    first = before is None
    operands = held(own, got) if first else held(own, got, before, *after)
    packed = (3 * BLK, BLK)
    half = (3 * BLK // 2, BLK)

    def body(*refs):
        if first:
            gram_kernel(*refs[:2], None, *refs[2:], None, None)
        else:
            gram_kernel(*refs[:3], *refs[-6:-3], refs[-1], *refs[-3:-1])

    return pl.pallas_call(
        body,
        in_specs=[VMEM] * len(operands),
        out_specs=[VMEM] * (4 if first else 5),
        out_shape=[
            on_chip(rows, RANK),
            on_chip(RANK, rows, dtype=BF16),
            on_chip(RANK, rows, dtype=BF16),
            *([on_chip(*packed)] if first else [on_chip(*half)] * 2),
        ],
        scratch_shapes=[] if first else [pltpu.VMEM(packed, F32)],
        cost_estimate=cost(rows * RANK * RANK * 12, rows * RANK * 8),
        compiler_params=LIMIT,
        name="gram_band",
    )(*operands)


def project_kernel(flips, high_ref, low_ref, band_ref, before, outs):
    row = lax.axis_index("rows")
    core, right, near, far = row & 1, (row >> 1) & 1, (row >> 2) & 1, row >> 3
    for i, flip in enumerate(flips):
        for side in range(2):
            out = outs[2 * i + side]
            for t in range(2):
                block = (far ^ core ^ 1 ^ side) * 4 + (right ^ flip) * 2 + (near ^ t)
                a_high, a_low = split(band_ref[:, pl.ds(pl.multiple_of(block * 2 * BLK, 2 * BLK), 2 * BLK)])
                total = dot(high_ref[...], a_high) + dot(high_ref[...], a_low) + dot(low_ref[...], a_high)
                out[t] = total if before is None else total + before[2 * i + side][t]


def project_band(flips, high, low, band, before=(), after=()):
    rows, cols = band.shape
    operands = held(high, low, band, *before, *after)
    count = 2 * len(flips)

    def body(*refs):
        project_kernel(flips, *refs[:3], refs[3 : 3 + count] if before else None, refs[-count:])

    return pl.pallas_call(
        body,
        in_specs=[VMEM] * len(operands),
        out_specs=[VMEM] * count,
        out_shape=[on_chip(2, RANK, 2 * BLK)] * count,
        cost_estimate=cost(rows * cols * RANK * 3 * len(flips), rows * cols * 4),
        compiler_params=LIMIT,
        name="project_band",
    )(*operands)


def add_parts_kernel(terms, outs):
    for i, out in enumerate(outs):
        here = slice(None) if len(outs) == 1 else i
        total = terms[0][here]
        for term in terms[1:]:
            total = total + term[here]
        out[...] = total


def add_parts(terms, parts, after=()):
    dims = terms[0].shape
    size = math.prod(dims)
    count = len(terms)

    def body(*refs):
        add_parts_kernel(refs[:count], refs[-parts:])

    return pl.pallas_call(
        body,
        in_specs=[VMEM] * (count + len(after)),
        out_specs=[VMEM] * parts,
        out_shape=[on_chip(*(dims if parts == 1 else dims[1:]))] * parts,
        cost_estimate=cost(size, size),
        compiler_params=LIMIT,
        name="add_parts",
    )(*held(*terms, *after))


def factor_panel(parts, start):
    diagonal = parts[0][:, start : start + PANEL]
    columns = [jnp.broadcast_to(diagonal[:, k : k + 1], (PANEL, BLK)) for k in range(PANEL)]
    rows = lax.broadcasted_iota(jnp.int32, (PANEL, BLK), 0)
    pivots = jnp.ones((PANEL, BLK), F32)
    for j in range(PANEL):
        pivot = jnp.broadcast_to(columns[j][j : j + 1, :], (PANEL, BLK))
        multiplier = jnp.where(rows > j, columns[j] / pivot, 0.0)
        for k in range(j + 1, PANEL):
            columns[k] = columns[k] - multiplier * columns[k][j : j + 1, :]
        parts = [part - multiplier * part[j : j + 1, :] for part in parts]
        pivots = jnp.where(rows == j, pivot, pivots)
    scale = lax.rsqrt(pivots)
    return [part * scale for part in parts]


def factor_block(work):
    for panel in range(BLK // PANEL):
        start = panel * PANEL
        stop = start + PANEL
        parts = [work[start:stop, c * BLK : (c + 1) * BLK] for c in range(3)]
        parts = factor_panel(parts, start)
        for c in range(3):
            work[start:stop, c * BLK : (c + 1) * BLK] = parts[c]
        if stop < BLK:
            left = parts[0].T[stop:]
            work[stop:, :] = work[stop:, :] - jnp.dot(left, jnp.concatenate(parts, 1), precision=HIGHEST)


def factor_kernel(total_rows, own_ref, got_ref, out_ref, work, packed):
    half = own_ref.shape[0]
    core = lax.axis_index("rows") & 1
    packed[pl.ds(pl.multiple_of(core * half, half), half), :] = own_ref[...]
    packed[pl.ds(pl.multiple_of((1 - core) * half, half), half), :] = got_ref[...]
    row = lax.broadcasted_iota(jnp.int32, (BLK, BLK), 0)
    col = lax.broadcasted_iota(jnp.int32, (BLK, BLK), 1)
    eye = (row == col).astype(F32)
    work[:, :BLK] = packed[:BLK] + float(total_rows) * eye
    work[:, BLK : 2 * BLK] = packed[BLK : 2 * BLK]
    work[:, 2 * BLK :] = eye
    factor_block(work)
    out_ref[:BLK, :BLK] = work[:, 2 * BLK :]
    out_ref[:BLK, BLK:] = jnp.zeros((BLK, BLK), F32)
    above = work[:, BLK : 2 * BLK]
    product = jnp.dot(above.T, work[:, BLK:], precision=HIGHEST)
    work[:, :BLK] = packed[2 * BLK :] + float(total_rows) * eye - product[:, :BLK]
    work[:, BLK : 2 * BLK] = -product[:, BLK:]
    work[:, 2 * BLK :] = eye
    factor_block(work)
    out_ref[BLK:, :] = work[:, BLK:]


def inverse_factor(own, got, total_rows):
    def body(*refs):
        factor_kernel(total_rows, *refs)

    return pl.pallas_call(
        body,
        in_specs=[VMEM] * 2,
        out_specs=VMEM,
        out_shape=on_chip(RANK, RANK),
        scratch_shapes=[pltpu.VMEM((BLK, 3 * BLK), F32), pltpu.VMEM((3 * BLK, BLK), F32)],
        cost_estimate=cost(0, RANK * RANK * 8),
        compiler_params=LIMIT,
        name="inverse_factor",
    )(*held(own, got))


def core_kernel(scale, first_ref, second_ref, inverse_ref, out_ref):
    t_high, t_low = split(inverse_ref[...].T)
    band = first_ref.shape[0]
    for i, ref in enumerate((first_ref, second_ref)):
        s_high, s_low = split(ref[...])
        total = dot(s_high, t_high) + dot(s_high, t_low) + dot(s_low, t_high)
        out_ref[i * band : (i + 1) * band] = total * scale


def scaled_core(sketches, inverse, scale):
    rows = 2 * sketches[0].shape[0]

    def body(*refs):
        core_kernel(scale, *refs)

    return pl.pallas_call(
        body,
        in_specs=[VMEM] * 3,
        out_specs=VMEM,
        out_shape=jax.ShapeDtypeStruct((rows, RANK), F32),
        cost_estimate=cost(rows * RANK * RANK * 6, rows * RANK * 8),
        compiler_params=LIMIT,
        name="scaled_core",
    )(*held(*sketches, inverse))


def remainder_kernel(inverse_ref, p0, p1, o0, o1, o2, o3, work):
    work[...] = jnp.dot(inverse_ref[...], p0[...] + p1[...], precision=HIGHEST)
    device = lax.axis_index("rows")
    for m, out in enumerate((o0, o1, o2, o3)):
        for t in range(4):
            rank_block = (4 * t + m) ^ device
            out[t] = work[pl.ds(pl.multiple_of(rank_block * 16, 16), 16), :]


def remainder_pieces(inverse, pieces):
    return pl.pallas_call(
        remainder_kernel,
        in_specs=[VMEM] * 3,
        out_specs=[VMEM] * 4,
        out_shape=[on_chip(4, 16, 2 * BLK)] * 4,
        scratch_shapes=[pltpu.VMEM((RANK, 2 * BLK), F32)],
        cost_estimate=cost(RANK * RANK * BLK * 24, RANK * BLK * 16),
        compiler_params=LIMIT,
        name="remainder_pieces",
    )(*held(inverse, *pieces))


def collect_kernel(r0, r1, r2, r3, o0, o1, o2, o3):
    for t, out in enumerate((o0, o1, o2, o3)):
        out[0] = r0[t] + r1[t]
        out[1] = r2[t] + r3[t]


def collect(firsts):
    return pl.pallas_call(
        collect_kernel,
        in_specs=[VMEM] * 4,
        out_specs=[VMEM] * 4,
        out_shape=[on_chip(2, 16, 2 * BLK)] * 4,
        cost_estimate=cost(0, 16 * BLK * 64),
        compiler_params=LIMIT,
        name="collect",
    )(*held(*firsts))


def arrange_kernel(p0, p1, p2, p3, out_ref, work):
    row = lax.axis_index("rows")
    right, deep = (row >> 1) & 1, row >> 2
    for t, piece in enumerate((p0, p1, p2, p3)):
        there = deep ^ t
        for m in range(2):
            work[(there & 1) * 4 + (there >> 1) * 2 + (right ^ m)] = piece[m]
    for mode in range(MODE):
        out_ref[:, mode, :] = work[mode]


def arrange(pieces):
    out = pl.pallas_call(
        arrange_kernel,
        in_specs=[VMEM] * 4,
        out_specs=VMEM,
        out_shape=jax.ShapeDtypeStruct((16, MODE, 2 * BLK), F32),
        scratch_shapes=[pltpu.VMEM((MODE, 16, 2 * BLK), F32)],
        cost_estimate=cost(0, 16 * BLK * 64),
        compiler_params=LIMIT,
        name="arrange",
    )(*held(*pieces))
    return out.reshape(16 * MODE, 2 * BLK)


def rows_permute(value, mask):
    size = lax.axis_size("rows")
    return lax.ppermute(value, "rows", [(i, i ^ mask) for i in range(size)])


def local(unfolding, pattern, sign_bits):
    total_rows = unfolding.shape[0] * lax.axis_size("rows")
    own, got, bands = [], [], []
    for band in range(2):
        part, rows_here = sketch_band(unfolding, pattern.T, sign_bits.T, band, 2)
        own.append(part)
        bands.append(rows_here)
        got.append(lax.ppermute(part, "cols", [(0, 1), (1, 0)]))
    first, high, low, packed = gram_band(own[0], got[0], None)
    before = project_band((1, 0), high, low, bands[0])
    second, high, low, gram_keep, gram_send = gram_band(own[1], got[1], packed, before[:1])
    gram, = add_parts((gram_keep, rows_permute(gram_send, 1)), 1)
    give, keep = project_band((1,), high, low, bands[1], before[:2])
    send, = add_parts((keep, rows_permute(give, 1)), 1, (gram,))
    give, keep = project_band((0,), high, low, bands[1], before[2:])
    pieces = add_parts((keep, rows_permute(give, 1), rows_permute(send, 2)), 2)
    gram, = add_parts((gram, rows_permute(gram, 4)), 1)
    gram, = add_parts((gram, rows_permute(gram, 8)), 1, pieces)
    gram, = add_parts((gram, rows_permute(gram, 2)), 1)
    inverse = inverse_factor(gram, rows_permute(gram, 1), total_rows)
    gathered = []
    for k in range(2):
        pairs = []
        for i in range(16):
            for y in range(2):
                to = (i & 3) | (y << 2) | ((i & 8) ^ ((i & 1) << 3))
                pairs.append((2 * i + y, 2 * to + (((i >> 2) & 1) ^ k)))
        gathered.append(lax.ppermute(pieces[k], ("rows", "cols"), pairs))
    parts = remainder_pieces(inverse, gathered)
    core_scaled = scaled_core((first, second), inverse, math.sqrt(total_rows))
    sums = collect([parts[0]] + [rows_permute(parts[m], m) for m in (1, 2, 3)])
    return core_scaled, arrange([sums[0]] + [rows_permute(sums[t], 4 * t) for t in (1, 2, 3)])


def sketch_matrix(pattern, sign_bits, block_size):
    blocks = sign_bits.shape[1]
    rows_here = sign_bits.shape[0]
    factor = jnp.repeat(pattern, block_size, axis=0) * (2 * sign_bits - 1)
    tiled_table = jnp.tile(hadamard_table(block_size), (rows_here // block_size, 1))
    expanded = factor.astype(F32)[:, :, None] * tiled_table[:, None, :]
    return expanded.reshape(rows_here, blocks * block_size)


def inner_rows(left_side, right_side):
    return lax.dot_general(left_side, right_side, (((0,), (0,)), ((), ())), precision=HIGHEST)


def local_any(unfolding, pattern, sign_bits):
    sketch_map = sketch_matrix(pattern, sign_bits, BLK)
    row_devices = lax.axis_size("rows")
    col_devices = lax.axis_size("cols")
    total_rows = unfolding.shape[0] * row_devices
    sketch = lax.psum(jnp.dot(unfolding, sketch_map, precision=HIGHEST), "cols")
    gram_matrix = lax.psum(inner_rows(sketch, sketch), "rows")
    gram_matrix = gram_matrix + float(total_rows) * jnp.eye(RANK, dtype=F32)
    lower_factor = jnp.linalg.cholesky(gram_matrix)
    basis_rows = lax.linalg.triangular_solve(lower_factor, sketch, left_side=False, lower=True, transpose_a=True)
    mode_local = MODE // col_devices
    rest_cols = unfolding.shape[1] // mode_local
    rank_share = RANK // row_devices
    reduced = lax.psum_scatter(inner_rows(basis_rows, unfolding), "rows", scatter_dimension=0, tiled=True)
    grouped = reduced.reshape(rank_share, mode_local, rest_cols)
    regrouped = lax.all_to_all(grouped, "cols", split_axis=2, concat_axis=1, tiled=True)
    return basis_rows * math.sqrt(total_rows), regrouped.reshape(rank_share * MODE, regrouped.shape[2])


def solution(mesh):
    in_specs = (P("rows", "cols"), P("cols", None), P("cols", None))
    out_specs = (P("rows", None), P("rows", "cols"))
    body = local if (mesh.shape["rows"], mesh.shape["cols"]) == (16, 2) else local_any
    return jax.shard_map(body, mesh=mesh, in_specs=in_specs, out_specs=out_specs, check_vma=False)
```

```python
import math

import jax
import jax.numpy as jnp
from jax import lax
from jax.experimental import pallas as pl
from jax.experimental.pallas import tpu as pltpu
from jax.sharding import PartitionSpec as P

RANK = 256
BLK = 128
MODE = 8
PANEL = 16
HIGHEST = lax.Precision.HIGHEST
F32 = jnp.float32
BF16 = jnp.bfloat16
VMEM = pl.BlockSpec(memory_space=pltpu.VMEM)
HBM = pl.BlockSpec(memory_space=pltpu.HBM)


def hadamard_table(table_size):
    row_index = lax.broadcasted_iota(jnp.int32, (table_size, table_size), 0)
    col_index = lax.broadcasted_iota(jnp.int32, (table_size, table_size), 1)
    both = row_index & col_index
    parity = jnp.zeros((table_size, table_size), jnp.int32)
    for bit_level in range(table_size.bit_length() - 1):
        parity = parity ^ (both >> bit_level)
    return (1 - 2 * (parity & 1)).astype(F32)


def on_chip(*dims, dtype=F32):
    return pltpu.VMEM(dims, dtype)


def held(*values):
    return [pltpu.with_memory_space_constraint(value, pltpu.VMEM) for value in values]


LIMIT = pltpu.CompilerParams(vmem_limit_bytes=8 << 20)


def cost(flops, size):
    return pl.CostEstimate(flops=flops // 1000, bytes_accessed=size // 1000, transcendentals=0)


def split(value):
    high = value.astype(BF16)
    return high, (value - high.astype(F32)).astype(BF16)


def dot(left, right):
    return jnp.dot(left, right, preferred_element_type=F32)


def block_factors(k, signs, pattern, row_blocks):
    signed = (2 * signs[k : k + 1, :] - 1).astype(F32)
    return [signed[:, j * BLK : (j + 1) * BLK] * pattern[k, j].astype(F32) for j in range(row_blocks)]


def block_sketch(block_ref, here, factors, table):
    total = block_ref[here, :BLK] * factors[0]
    for j in range(1, len(factors)):
        total = total + block_ref[here, j * BLK : (j + 1) * BLK] * factors[j]
    high, rest = split(total)
    low = (total - high.astype(F32) - rest.astype(F32)).astype(BF16)
    return dot(high, table) + dot(rest, table) + dot(low, table)


def first_sketch_kernel(pattern_ref, whole_ref, sign_ref, out_ref, held_ref, sems, signs, pattern):
    steps = sems.shape[0] - 2
    step = held_ref.shape[0] // steps
    copies = [
        pltpu.make_async_copy(pattern_ref, pattern, sems.at[steps]),
        pltpu.make_async_copy(sign_ref, signs, sems.at[steps + 1]),
    ]
    for i in range(steps):
        here = pl.ds(i * step, step)
        copies.append(pltpu.make_async_copy(whole_ref.at[here], held_ref.at[here], sems.at[i]))
    for copy in copies:
        copy.start()
    table = hadamard_table(BLK).astype(BF16)
    copies[0].wait()
    copies[1].wait()
    factors = block_factors(0, signs, pattern, held_ref.shape[1] // BLK)
    for i in range(steps):
        copies[2 + i].wait()
        here = slice(i * step, (i + 1) * step)
        out_ref[here, :] = block_sketch(held_ref, here, factors, table)


def first_sketch(unfolding, pattern_rows, sign_rows):
    rows, cols = unfolding.shape
    return pl.pallas_call(
        first_sketch_kernel,
        in_specs=[HBM] * 3,
        out_specs=[VMEM] * 2,
        out_shape=[on_chip(rows, BLK), on_chip(rows, cols)],
        scratch_shapes=[
            pltpu.SemaphoreType.DMA((10,)),
            pltpu.VMEM(sign_rows.shape, jnp.int32),
            pltpu.SMEM(pattern_rows.shape, jnp.int32),
        ],
        cost_estimate=cost(rows * cols * 2, rows * cols * 4),
        compiler_params=LIMIT,
        name="first_sketch",
    )(*[pltpu.with_memory_space_constraint(x, pltpu.HBM) for x in (pattern_rows, unfolding, sign_rows)])


def second_sketch_kernel(pattern_ref, sign_ref, block_ref, out_ref, high_ref, low_ref, sems, signs, pattern):
    copies = [
        pltpu.make_async_copy(pattern_ref, pattern, sems.at[0]),
        pltpu.make_async_copy(sign_ref, signs, sems.at[1]),
    ]
    for copy in copies:
        copy.start()
    table = hadamard_table(BLK).astype(BF16)
    step = 64
    for i in range(block_ref.shape[0] // step):
        here = slice(i * step, (i + 1) * step)
        high_ref[here, :], low_ref[here, :] = split(block_ref[here, :])
    for copy in copies:
        copy.wait()
    factors = block_factors(1, signs, pattern, block_ref.shape[1] // BLK)
    for i in range(block_ref.shape[0] // step):
        here = slice(i * step, (i + 1) * step)
        out_ref[here, :] = block_sketch(block_ref, here, factors, table)


def second_sketch(block, pattern_rows, sign_rows):
    rows, cols = block.shape
    return pl.pallas_call(
        second_sketch_kernel,
        in_specs=[HBM, HBM, VMEM],
        out_specs=[VMEM] * 3,
        out_shape=[on_chip(rows, BLK), on_chip(rows, cols, dtype=BF16), on_chip(rows, cols, dtype=BF16)],
        scratch_shapes=[
            pltpu.SemaphoreType.DMA((2,)),
            pltpu.VMEM(sign_rows.shape, jnp.int32),
            pltpu.SMEM(pattern_rows.shape, jnp.int32),
        ],
        cost_estimate=cost(rows * cols * 2, rows * cols * 4),
        compiler_params=LIMIT,
        name="second_sketch",
    )(*[pltpu.with_memory_space_constraint(x, pltpu.HBM) for x in (pattern_rows, sign_rows)], *held(block))


def first_gram_kernel(own_ref, got_ref, sketch_ref, turned_ref, parts_ref, gram_ref):
    sketch = own_ref[...] + got_ref[...]
    sketch_ref[...] = sketch
    turned = sketch.T
    turned_ref[...] = turned
    parts_ref[:BLK], parts_ref[BLK:] = split(turned)
    gram_ref[...] = jnp.dot(turned, sketch, precision=HIGHEST)


def first_gram(own, got):
    rows = own.shape[0]
    return pl.pallas_call(
        first_gram_kernel,
        in_specs=[VMEM] * 2,
        out_specs=[VMEM] * 4,
        out_shape=[
            on_chip(rows, BLK),
            on_chip(BLK, rows),
            on_chip(2 * BLK, rows, dtype=BF16),
            on_chip(BLK, BLK),
        ],
        cost_estimate=cost(rows * BLK * BLK * 12, rows * BLK * 8),
        compiler_params=LIMIT,
        name="first_gram",
    )(*held(own, got))


def second_gram_kernel(own_ref, got_ref, before_ref, gram_ref, sketch_ref, parts_ref, keep_ref, send_ref, packed):
    sketch = own_ref[...] + got_ref[...]
    sketch_ref[...] = sketch
    turned = sketch.T
    parts_ref[:BLK], parts_ref[BLK:] = split(turned)
    packed[:BLK] = gram_ref[...]
    packed[BLK : 2 * BLK] = jnp.dot(before_ref[...], sketch, precision=HIGHEST)
    packed[2 * BLK :] = jnp.dot(turned, sketch, precision=HIGHEST)
    half = keep_ref.shape[0]
    core = lax.axis_index("rows") & 1
    keep_ref[...] = packed[pl.ds(pl.multiple_of(core * half, half), half), :]
    send_ref[...] = packed[pl.ds(pl.multiple_of((1 - core) * half, half), half), :]


def second_gram(own, got, before, gram, after):
    rows = own.shape[0]
    half = (3 * BLK // 2, BLK)

    def body(*refs):
        second_gram_kernel(*refs[:4], *refs[-5:])

    return pl.pallas_call(
        body,
        in_specs=[VMEM] * (4 + len(after)),
        out_specs=[VMEM] * 4,
        out_shape=[
            on_chip(rows, BLK),
            on_chip(2 * BLK, rows, dtype=BF16),
            on_chip(*half),
            on_chip(*half),
        ],
        scratch_shapes=[pltpu.VMEM((3 * BLK, BLK), F32)],
        cost_estimate=cost(rows * BLK * BLK * 24, rows * BLK * 8),
        compiler_params=LIMIT,
        name="second_gram",
    )(*held(own, got, before, gram, *after))


def project_kernel(parts_ref, high_ref, low_ref, soon_0, soon_1, keep_1, give_0, keep_0):
    row = lax.axis_index("rows")
    core, right, near, far = row & 1, (row >> 1) & 1, (row >> 2) & 1, row >> 3
    for flip, give, keep in ((1, (soon_0, soon_1), keep_1), (0, (give_0.at[0], give_0.at[1]), keep_0)):
        for side in range(2):
            for t in range(2):
                block = (far ^ core ^ 1 ^ side) * 4 + (right ^ flip) * 2 + (near ^ t)
                here = pl.ds(pl.multiple_of(block * 2 * BLK, 2 * BLK), 2 * BLK)
                both = dot(parts_ref[...], high_ref[:, here])
                total = both[:BLK] + both[BLK:] + dot(parts_ref[:BLK, :], low_ref[:, here])
                if side == 0:
                    give[t][...] = total
                else:
                    keep[t] = total


def project(parts, high, low, after=()):
    rows, cols = high.shape

    def body(*refs):
        project_kernel(*refs[:3], *refs[-5:])

    return pl.pallas_call(
        body,
        in_specs=[VMEM] * (3 + len(after)),
        out_specs=[VMEM] * 5,
        out_shape=[on_chip(BLK, 2 * BLK)] * 2 + [on_chip(2, BLK, 2 * BLK)] * 3,
        cost_estimate=cost(rows * cols * BLK * 6, rows * cols * 4),
        compiler_params=LIMIT,
        name="project",
    )(*held(parts, high, low, *after))


def joined_kernel(keep_ref, got_0, got_1, out_ref):
    out_ref[0] = keep_ref[0] + got_0[...]
    out_ref[1] = keep_ref[1] + got_1[...]


def joined(keep, got, after):
    def body(*refs):
        joined_kernel(*refs[:3], refs[-1])

    return pl.pallas_call(
        body,
        in_specs=[VMEM] * (3 + len(after)),
        out_specs=VMEM,
        out_shape=on_chip(*keep.shape),
        cost_estimate=cost(0, keep.size * 4),
        compiler_params=LIMIT,
        name="joined",
    )(*held(keep, *got, *after))


def add_parts_kernel(terms, outs):
    for i, out in enumerate(outs):
        here = slice(None) if len(outs) == 1 else i
        total = terms[0][here]
        for term in terms[1:]:
            total = total + term[here]
        out[...] = total


def add_parts(terms, parts, after=()):
    dims = terms[0].shape
    size = math.prod(dims)
    count = len(terms)

    def body(*refs):
        add_parts_kernel(refs[:count], refs[-parts:])

    return pl.pallas_call(
        body,
        in_specs=[VMEM] * (count + len(after)),
        out_specs=[VMEM] * parts,
        out_shape=[on_chip(*(dims if parts == 1 else dims[1:]))] * parts,
        cost_estimate=cost(size, size),
        compiler_params=LIMIT,
        name="add_parts",
    )(*held(*terms, *after))


def pieces_kernel(refs, outs):
    count = len(refs) // 2
    for i, out in enumerate(outs):
        for h in range(2):
            terms = [ref[i] for ref in refs[h * count : (h + 1) * count]]
            out[h * BLK : (h + 1) * BLK] = sum(terms[1:], terms[0])


def piece_sums(first, second):
    terms = (*first, *second)

    def body(*refs):
        pieces_kernel(refs[:-2], refs[-2:])

    return pl.pallas_call(
        body,
        in_specs=[VMEM] * len(terms),
        out_specs=[VMEM] * 2,
        out_shape=[on_chip(2 * BLK, 2 * BLK)] * 2,
        cost_estimate=cost(8 * BLK * BLK, 96 * BLK * BLK),
        compiler_params=LIMIT,
        name="piece_sums",
    )(*held(*terms))


def factor_panel(parts, start):
    diagonal = parts[0][:, start : start + PANEL]
    columns = [jnp.broadcast_to(diagonal[:, k : k + 1], (PANEL, BLK)) for k in range(PANEL)]
    rows = lax.broadcasted_iota(jnp.int32, (PANEL, BLK), 0)
    pivots = jnp.ones((PANEL, BLK), F32)
    for j in range(PANEL):
        pivot = jnp.broadcast_to(columns[j][j : j + 1, :], (PANEL, BLK))
        multiplier = jnp.where(rows > j, columns[j] / pivot, 0.0)
        for k in range(j + 1, PANEL):
            columns[k] = columns[k] - multiplier * columns[k][j : j + 1, :]
        parts = [part - multiplier * part[j : j + 1, :] for part in parts]
        pivots = jnp.where(rows == j, pivot, pivots)
    scale = lax.rsqrt(pivots)
    return [part * scale for part in parts]


def factor_block(work):
    for panel in range(BLK // PANEL):
        start = panel * PANEL
        stop = start + PANEL
        parts = [work[start:stop, c * BLK : (c + 1) * BLK] for c in range(3)]
        parts = factor_panel(parts, start)
        for c in range(3):
            work[start:stop, c * BLK : (c + 1) * BLK] = parts[c]
        if stop < BLK:
            left = parts[0].T[stop:]
            work[stop:, :] = work[stop:, :] - jnp.dot(left, jnp.concatenate(parts, 1), precision=HIGHEST)


def factor_kernel(total_rows, own_ref, got_ref, out_ref, work, packed):
    half = own_ref.shape[0]
    core = lax.axis_index("rows") & 1
    packed[pl.ds(pl.multiple_of(core * half, half), half), :] = own_ref[...]
    packed[pl.ds(pl.multiple_of((1 - core) * half, half), half), :] = got_ref[...]
    row = lax.broadcasted_iota(jnp.int32, (BLK, BLK), 0)
    col = lax.broadcasted_iota(jnp.int32, (BLK, BLK), 1)
    eye = (row == col).astype(F32)
    work[:, :BLK] = packed[:BLK] + float(total_rows) * eye
    work[:, BLK : 2 * BLK] = packed[BLK : 2 * BLK]
    work[:, 2 * BLK :] = eye
    factor_block(work)
    out_ref[:BLK, :BLK] = work[:, 2 * BLK :]
    out_ref[:BLK, BLK:] = jnp.zeros((BLK, BLK), F32)
    above = work[:, BLK : 2 * BLK]
    product = jnp.dot(above.T, work[:, BLK:], precision=HIGHEST)
    work[:, :BLK] = packed[2 * BLK :] + float(total_rows) * eye - product[:, :BLK]
    work[:, BLK : 2 * BLK] = -product[:, BLK:]
    work[:, 2 * BLK :] = eye
    factor_block(work)
    out_ref[BLK:, :] = work[:, BLK:]


def inverse_factor(own, got, total_rows):
    def body(*refs):
        factor_kernel(total_rows, *refs)

    return pl.pallas_call(
        body,
        in_specs=[VMEM] * 2,
        out_specs=VMEM,
        out_shape=on_chip(RANK, RANK),
        scratch_shapes=[pltpu.VMEM((BLK, 3 * BLK), F32), pltpu.VMEM((3 * BLK, BLK), F32)],
        cost_estimate=cost(0, RANK * RANK * 8),
        compiler_params=LIMIT,
        name="inverse_factor",
    )(*held(own, got))


def core_kernel(scale, first_ref, second_ref, inverse_ref, out_ref):
    t_high, t_low = split(inverse_ref[...].T)
    s_high, s_low = split(jnp.concatenate([first_ref[...], second_ref[...]], 1))
    total = dot(s_high, t_high) + dot(s_high, t_low) + dot(s_low, t_high)
    out_ref[...] = total * scale


def scaled_core(first, second, inverse, scale):
    rows = first.shape[0]

    def body(*refs):
        core_kernel(scale, *refs)

    return pl.pallas_call(
        body,
        in_specs=[VMEM] * 3,
        out_specs=VMEM,
        out_shape=jax.ShapeDtypeStruct((rows, RANK), F32),
        cost_estimate=cost(rows * RANK * RANK * 6, rows * RANK * 8),
        compiler_params=LIMIT,
        name="scaled_core",
    )(*held(first, second, inverse))


def remainder_kernel(inverse_ref, p0, p1, o0, o1, o2, o3, work):
    work[...] = jnp.dot(inverse_ref[...], p0[...] + p1[...], precision=HIGHEST)
    device = lax.axis_index("rows")
    for m, out in enumerate((o0, o1, o2, o3)):
        for t in range(4):
            rank_block = (4 * t + m) ^ device
            out[t] = work[pl.ds(pl.multiple_of(rank_block * 16, 16), 16), :]


def remainder_pieces(inverse, pieces):
    return pl.pallas_call(
        remainder_kernel,
        in_specs=[VMEM] * 3,
        out_specs=[VMEM] * 4,
        out_shape=[on_chip(4, 16, 2 * BLK)] * 4,
        scratch_shapes=[pltpu.VMEM((RANK, 2 * BLK), F32)],
        cost_estimate=cost(RANK * RANK * BLK * 24, RANK * BLK * 16),
        compiler_params=LIMIT,
        name="remainder_pieces",
    )(*held(inverse, *pieces))


def collect_kernel(r0, r1, r2, r3, o0, o1, o2, o3):
    for t, out in enumerate((o0, o1, o2, o3)):
        out[0] = r0[t] + r1[t]
        out[1] = r2[t] + r3[t]


def collect(firsts):
    return pl.pallas_call(
        collect_kernel,
        in_specs=[VMEM] * 4,
        out_specs=[VMEM] * 4,
        out_shape=[on_chip(2, 16, 2 * BLK)] * 4,
        cost_estimate=cost(0, 16 * BLK * 64),
        compiler_params=LIMIT,
        name="collect",
    )(*held(*firsts))


def arrange_kernel(p0, p1, p2, p3, out_ref, work):
    row = lax.axis_index("rows")
    right, deep = (row >> 1) & 1, row >> 2
    for t, piece in enumerate((p0, p1, p2, p3)):
        there = deep ^ t
        for m in range(2):
            work[(there & 1) * 4 + (there >> 1) * 2 + (right ^ m)] = piece[m]
    for mode in range(MODE):
        out_ref[:, mode, :] = work[mode]


def arrange(pieces):
    out = pl.pallas_call(
        arrange_kernel,
        in_specs=[VMEM] * 4,
        out_specs=VMEM,
        out_shape=jax.ShapeDtypeStruct((16, MODE, 2 * BLK), F32),
        scratch_shapes=[pltpu.VMEM((MODE, 16, 2 * BLK), F32)],
        cost_estimate=cost(0, 16 * BLK * 64),
        compiler_params=LIMIT,
        name="arrange",
    )(*held(*pieces))
    return out.reshape(16 * MODE, 2 * BLK)


def rows_permute(value, mask):
    size = lax.axis_size("rows")
    return lax.ppermute(value, "rows", [(i, i ^ mask) for i in range(size)])


def local(unfolding, pattern, sign_bits):
    total_rows = unfolding.shape[0] * lax.axis_size("rows")
    swap = [(0, 1), (1, 0)]
    pattern_rows, sign_rows = pattern.T, sign_bits.T
    own_0, block = first_sketch(unfolding, pattern_rows, sign_rows)
    got_0 = lax.ppermute(own_0, "cols", swap)
    own_1, high, low = second_sketch(block, pattern_rows, sign_rows)
    got_1 = lax.ppermute(own_1, "cols", swap)
    first, turned, parts, gram = first_gram(own_0, got_0)
    *give, keep, give_0, keep_0 = project(parts, high, low)
    send_0 = joined(keep, [rows_permute(g, 1) for g in give], ())
    second, parts, gram_keep, gram_send = second_gram(own_1, got_1, turned, gram, (keep_0,))
    gram, = add_parts((gram_keep, rows_permute(gram_send, 1)), 1)
    *give, keep, give_1, keep_1 = project(parts, high, low, (send_0,))
    got_0 = rows_permute(send_0, 2)
    send_1 = joined(keep, [rows_permute(g, 1) for g in give], (gram, got_0))
    pieces = piece_sums(
        (keep_0, rows_permute(give_0, 1), got_0),
        (keep_1, rows_permute(give_1, 1), rows_permute(send_1, 2)),
    )
    gram, = add_parts((gram, rows_permute(gram, 4)), 1)
    gram, = add_parts((gram, rows_permute(gram, 8)), 1, pieces)
    gram, = add_parts((gram, rows_permute(gram, 2)), 1)
    inverse = inverse_factor(gram, rows_permute(gram, 1), total_rows)
    gathered = []
    for k in range(2):
        pairs = []
        for i in range(16):
            for y in range(2):
                to = (i & 3) | (y << 2) | ((i & 8) ^ ((i & 1) << 3))
                pairs.append((2 * i + y, 2 * to + (((i >> 2) & 1) ^ k)))
        gathered.append(lax.ppermute(pieces[k], ("rows", "cols"), pairs))
    parts = remainder_pieces(inverse, gathered)
    core_scaled = scaled_core(first, second, inverse, math.sqrt(total_rows))
    sums = collect([parts[0]] + [rows_permute(parts[m], m) for m in (1, 2, 3)])
    return core_scaled, arrange([sums[0]] + [rows_permute(sums[t], 4 * t) for t in (1, 2, 3)])


def sketch_matrix(pattern, sign_bits, block_size):
    blocks = sign_bits.shape[1]
    rows_here = sign_bits.shape[0]
    factor = jnp.repeat(pattern, block_size, axis=0) * (2 * sign_bits - 1)
    tiled_table = jnp.tile(hadamard_table(block_size), (rows_here // block_size, 1))
    expanded = factor.astype(F32)[:, :, None] * tiled_table[:, None, :]
    return expanded.reshape(rows_here, blocks * block_size)


def inner_rows(left_side, right_side):
    return lax.dot_general(left_side, right_side, (((0,), (0,)), ((), ())), precision=HIGHEST)


def local_any(unfolding, pattern, sign_bits):
    sketch_map = sketch_matrix(pattern, sign_bits, BLK)
    row_devices = lax.axis_size("rows")
    col_devices = lax.axis_size("cols")
    total_rows = unfolding.shape[0] * row_devices
    sketch = lax.psum(jnp.dot(unfolding, sketch_map, precision=HIGHEST), "cols")
    gram_matrix = lax.psum(inner_rows(sketch, sketch), "rows")
    gram_matrix = gram_matrix + float(total_rows) * jnp.eye(RANK, dtype=F32)
    lower_factor = jnp.linalg.cholesky(gram_matrix)
    basis_rows = lax.linalg.triangular_solve(lower_factor, sketch, left_side=False, lower=True, transpose_a=True)
    mode_local = MODE // col_devices
    rest_cols = unfolding.shape[1] // mode_local
    rank_share = RANK // row_devices
    reduced = lax.psum_scatter(inner_rows(basis_rows, unfolding), "rows", scatter_dimension=0, tiled=True)
    grouped = reduced.reshape(rank_share, mode_local, rest_cols)
    regrouped = lax.all_to_all(grouped, "cols", split_axis=2, concat_axis=1, tiled=True)
    return basis_rows * math.sqrt(total_rows), regrouped.reshape(rank_share * MODE, regrouped.shape[2])


def solution(mesh):
    in_specs = (P("rows", "cols"), P("cols", None), P("cols", None))
    out_specs = (P("rows", None), P("rows", "cols"))
    body = local if (mesh.shape["rows"], mesh.shape["cols"]) == (16, 2) else local_any
    return jax.shard_map(body, mesh=mesh, in_specs=in_specs, out_specs=out_specs, check_vma=False)
```

```python
import math

import jax
import jax.numpy as jnp
from jax import lax
from jax.experimental import pallas as pl
from jax.experimental.pallas import tpu as pltpu
from jax.sharding import PartitionSpec as P

RANK = 256
BLK = 128
MODE = 8
PANEL = 16
HIGHEST = lax.Precision.HIGHEST
F32 = jnp.float32
BF16 = jnp.bfloat16
VMEM = pl.BlockSpec(memory_space=pltpu.VMEM)
HBM = pl.BlockSpec(memory_space=pltpu.HBM)


def hadamard_table(table_size):
    row_index = lax.broadcasted_iota(jnp.int32, (table_size, table_size), 0)
    col_index = lax.broadcasted_iota(jnp.int32, (table_size, table_size), 1)
    both = row_index & col_index
    parity = jnp.zeros((table_size, table_size), jnp.int32)
    for bit_level in range(table_size.bit_length() - 1):
        parity = parity ^ (both >> bit_level)
    return (1 - 2 * (parity & 1)).astype(F32)


def on_chip(*dims, dtype=F32):
    return pltpu.VMEM(dims, dtype)


def held(*values):
    return [pltpu.with_memory_space_constraint(value, pltpu.VMEM) for value in values]


LIMIT = pltpu.CompilerParams(vmem_limit_bytes=8 << 20)


def cost(flops, size):
    flops, size = flops // 1000, size // 1000
    return pl.CostEstimate(flops=flops, bytes_accessed=size, transcendentals=0)


def split(value):
    high = value.astype(BF16)
    return high, (value - high.astype(F32)).astype(BF16)


def dot(left, right):
    return jnp.dot(left, right, preferred_element_type=F32)


def block_factors(k, signs, pattern, row_blocks):
    signed = (2 * signs[k : k + 1, :] - 1).astype(F32)
    return [signed[:, j * BLK : (j + 1) * BLK] * pattern[k, j].astype(F32) for j in range(row_blocks)]


def block_sketch(block_ref, here, factors, table):
    total = block_ref[here, :BLK] * factors[0]
    for j in range(1, len(factors)):
        total = total + block_ref[here, j * BLK : (j + 1) * BLK] * factors[j]
    high, rest = split(total)
    low = (total - high.astype(F32) - rest.astype(F32)).astype(BF16)
    return dot(high, table) + dot(rest, table) + dot(low, table)


def first_sketch_kernel(pattern_ref, whole_ref, sign_ref, out_ref, held_ref, sems, signs, pattern):
    steps = sems.shape[0] - 2
    step = held_ref.shape[0] // steps
    copies = [
        pltpu.make_async_copy(pattern_ref, pattern, sems.at[steps]),
        pltpu.make_async_copy(sign_ref, signs, sems.at[steps + 1]),
    ]
    for i in range(steps):
        here = pl.ds(i * step, step)
        copies.append(pltpu.make_async_copy(whole_ref.at[here], held_ref.at[here], sems.at[i]))
    for copy in copies:
        copy.start()
    table = hadamard_table(BLK).astype(BF16)
    copies[0].wait()
    copies[1].wait()
    factors = block_factors(0, signs, pattern, held_ref.shape[1] // BLK)
    for i in range(steps):
        copies[2 + i].wait()
        here = slice(i * step, (i + 1) * step)
        out_ref[here, :] = block_sketch(held_ref, here, factors, table)


def first_sketch(unfolding, pattern_rows, sign_rows):
    rows, cols = unfolding.shape
    return pl.pallas_call(
        first_sketch_kernel,
        in_specs=[HBM] * 3,
        out_specs=[VMEM] * 2,
        out_shape=[on_chip(rows, BLK), on_chip(rows, cols)],
        scratch_shapes=[
            pltpu.SemaphoreType.DMA((10,)),
            pltpu.VMEM(sign_rows.shape, jnp.int32),
            pltpu.SMEM(pattern_rows.shape, jnp.int32),
        ],
        cost_estimate=cost(rows * cols * 2, rows * cols * 4),
        compiler_params=LIMIT,
        name="first_sketch",
    )(*[pltpu.with_memory_space_constraint(x, pltpu.HBM) for x in (pattern_rows, unfolding, sign_rows)])


def second_sketch_kernel(pattern_ref, sign_ref, block_ref, out_ref, high_ref, low_ref, sems, signs, pattern):
    copies = [
        pltpu.make_async_copy(pattern_ref, pattern, sems.at[0]),
        pltpu.make_async_copy(sign_ref, signs, sems.at[1]),
    ]
    for copy in copies:
        copy.start()
    table = hadamard_table(BLK).astype(BF16)
    step = 64
    for i in range(block_ref.shape[0] // step):
        here = slice(i * step, (i + 1) * step)
        high_ref[here, :], low_ref[here, :] = split(block_ref[here, :])
    for copy in copies:
        copy.wait()
    factors = block_factors(1, signs, pattern, block_ref.shape[1] // BLK)
    for i in range(block_ref.shape[0] // step):
        here = slice(i * step, (i + 1) * step)
        out_ref[here, :] = block_sketch(block_ref, here, factors, table)


def second_sketch(block, pattern_rows, sign_rows):
    rows, cols = block.shape
    return pl.pallas_call(
        second_sketch_kernel,
        in_specs=[HBM, HBM, VMEM],
        out_specs=[VMEM] * 3,
        out_shape=[on_chip(rows, BLK), on_chip(rows, cols, dtype=BF16), on_chip(rows, cols, dtype=BF16)],
        scratch_shapes=[
            pltpu.SemaphoreType.DMA((2,)),
            pltpu.VMEM(sign_rows.shape, jnp.int32),
            pltpu.SMEM(pattern_rows.shape, jnp.int32),
        ],
        cost_estimate=cost(rows * cols * 2, rows * cols * 4),
        compiler_params=LIMIT,
        name="second_sketch",
    )(*[pltpu.with_memory_space_constraint(x, pltpu.HBM) for x in (pattern_rows, sign_rows)], *held(block))


def first_gram_kernel(own_ref, got_ref, sketch_ref, turned_ref, parts_ref, gram_ref):
    sketch = own_ref[...] + got_ref[...]
    sketch_ref[...] = sketch
    turned = sketch.T
    turned_ref[...] = turned
    parts_ref[:BLK], parts_ref[BLK:] = split(turned)
    gram_ref[...] = jnp.dot(turned, sketch, precision=HIGHEST)


def first_gram(own, got):
    rows = own.shape[0]
    return pl.pallas_call(
        first_gram_kernel,
        in_specs=[VMEM] * 2,
        out_specs=[VMEM] * 4,
        out_shape=[
            on_chip(rows, BLK),
            on_chip(BLK, rows),
            on_chip(2 * BLK, rows, dtype=BF16),
            on_chip(BLK, BLK),
        ],
        cost_estimate=cost(rows * BLK * BLK * 12, rows * BLK * 8),
        compiler_params=LIMIT,
        name="first_gram",
    )(*held(own, got))


def second_gram_kernel(own_ref, got_ref, before_ref, gram_ref, sketch_ref, parts_ref, keep_ref, send_ref, packed):
    sketch = own_ref[...] + got_ref[...]
    sketch_ref[...] = sketch
    turned = sketch.T
    parts_ref[:BLK], parts_ref[BLK:] = split(turned)
    packed[:BLK] = gram_ref[...]
    packed[BLK : 2 * BLK] = jnp.dot(before_ref[...], sketch, precision=HIGHEST)
    packed[2 * BLK :] = jnp.dot(turned, sketch, precision=HIGHEST)
    half = keep_ref.shape[0]
    core = lax.axis_index("rows") & 1
    keep_ref[...] = packed[pl.ds(pl.multiple_of(core * half, half), half), :]
    send_ref[...] = packed[pl.ds(pl.multiple_of((1 - core) * half, half), half), :]


def second_gram(own, got, before, gram, after):
    rows = own.shape[0]
    half = (3 * BLK // 2, BLK)

    def body(*refs):
        second_gram_kernel(*refs[:4], *refs[-5:])

    return pl.pallas_call(
        body,
        in_specs=[VMEM] * (4 + len(after)),
        out_specs=[VMEM] * 4,
        out_shape=[
            on_chip(rows, BLK),
            on_chip(2 * BLK, rows, dtype=BF16),
            on_chip(*half),
            on_chip(*half),
        ],
        scratch_shapes=[pltpu.VMEM((3 * BLK, BLK), F32)],
        cost_estimate=cost(rows * BLK * BLK * 24, rows * BLK * 8),
        compiler_params=LIMIT,
        name="second_gram",
    )(*held(own, got, before, gram, *after))


def project_kernel(parts_ref, high_ref, low_ref, soon_0, soon_1, keep_1, give_0, keep_0):
    row = lax.axis_index("rows")
    core, right, near, far = row & 1, (row >> 1) & 1, (row >> 2) & 1, row >> 3
    for flip, give, keep in ((1, (soon_0, soon_1), keep_1), (0, (give_0.at[0], give_0.at[1]), keep_0)):
        for side in range(2):
            for t in range(2):
                block = (far ^ core ^ 1 ^ side) * 4 + (right ^ flip) * 2 + (near ^ t)
                here = pl.ds(pl.multiple_of(block * 2 * BLK, 2 * BLK), 2 * BLK)
                both = dot(parts_ref[...], high_ref[:, here])
                total = both[:BLK] + both[BLK:] + dot(parts_ref[:BLK, :], low_ref[:, here])
                if side == 0:
                    give[t][...] = total
                else:
                    keep[t] = total


def project(parts, high, low, after=()):
    rows, cols = high.shape

    def body(*refs):
        project_kernel(*refs[:3], *refs[-5:])

    return pl.pallas_call(
        body,
        in_specs=[VMEM] * (3 + len(after)),
        out_specs=[VMEM] * 5,
        out_shape=[on_chip(BLK, 2 * BLK)] * 2 + [on_chip(2, BLK, 2 * BLK)] * 3,
        cost_estimate=cost(rows * cols * BLK * 6, rows * cols * 4),
        compiler_params=LIMIT,
        name="project",
    )(*held(parts, high, low, *after))


def joined_kernel(keep_ref, got_0, got_1, out_ref):
    out_ref[0] = keep_ref[0] + got_0[...]
    out_ref[1] = keep_ref[1] + got_1[...]


def joined(keep, got, after):
    def body(*refs):
        joined_kernel(*refs[:3], refs[-1])

    return pl.pallas_call(
        body,
        in_specs=[VMEM] * (3 + len(after)),
        out_specs=VMEM,
        out_shape=on_chip(*keep.shape),
        cost_estimate=cost(0, keep.size * 4),
        compiler_params=LIMIT,
        name="joined",
    )(*held(keep, *got, *after))


def add_parts_kernel(terms, outs):
    for i, out in enumerate(outs):
        here = slice(None) if len(outs) == 1 else i
        total = terms[0][here]
        for term in terms[1:]:
            total = total + term[here]
        out[...] = total


def add_parts(terms, parts, after=(), hint=0):
    dims = terms[0].shape
    size = math.prod(dims)
    count = len(terms)

    def body(*refs):
        add_parts_kernel(refs[:count], refs[-parts:])

    return pl.pallas_call(
        body,
        in_specs=[VMEM] * (count + len(after)),
        out_specs=[VMEM] * parts,
        out_shape=[on_chip(*(dims if parts == 1 else dims[1:]))] * parts,
        cost_estimate=cost(size + hint, size),
        compiler_params=LIMIT,
        name="add_parts",
    )(*held(*terms, *after))


def pieces_kernel(refs, outs):
    count = len(refs) // 2
    for i, out in enumerate(outs):
        for h in range(2):
            terms = [ref[i] for ref in refs[h * count : (h + 1) * count]]
            out[h * BLK : (h + 1) * BLK] = sum(terms[1:], terms[0])


def piece_sums(first, second, after):
    terms = (*first, *second)
    count = len(terms)

    def body(*refs):
        pieces_kernel(refs[:count], refs[-2:])

    return pl.pallas_call(
        body,
        in_specs=[VMEM] * (count + len(after)),
        out_specs=[VMEM] * 2,
        out_shape=[on_chip(2 * BLK, 2 * BLK)] * 2,
        cost_estimate=cost(8 * BLK * BLK, 96 * BLK * BLK),
        compiler_params=LIMIT,
        name="piece_sums",
    )(*held(*terms, *after))


def factor_panel(parts, start):
    diagonal = parts[0][:, start : start + PANEL]
    columns = [jnp.broadcast_to(diagonal[:, k : k + 1], (PANEL, BLK)) for k in range(PANEL)]
    rows = lax.broadcasted_iota(jnp.int32, (PANEL, BLK), 0)
    pivots = jnp.ones((PANEL, BLK), F32)
    for j in range(PANEL):
        pivot = jnp.broadcast_to(columns[j][j : j + 1, :], (PANEL, BLK))
        multiplier = jnp.where(rows > j, columns[j] / pivot, 0.0)
        for k in range(j + 1, PANEL):
            columns[k] = columns[k] - multiplier * columns[k][j : j + 1, :]
        parts = [part - multiplier * part[j : j + 1, :] for part in parts]
        pivots = jnp.where(rows == j, pivot, pivots)
    scale = lax.rsqrt(pivots)
    return [part * scale for part in parts]


def factor_block(work):
    for panel in range(BLK // PANEL):
        start = panel * PANEL
        stop = start + PANEL
        parts = [work[start:stop, c * BLK : (c + 1) * BLK] for c in range(3)]
        parts = factor_panel(parts, start)
        for c in range(3):
            work[start:stop, c * BLK : (c + 1) * BLK] = parts[c]
        if stop < BLK:
            left = parts[0].T[stop:]
            work[stop:, :] = work[stop:, :] - jnp.dot(left, jnp.concatenate(parts, 1), precision=HIGHEST)


def factor_kernel(total_rows, own_ref, got_ref, out_ref, work, packed):
    half = own_ref.shape[0]
    core = lax.axis_index("rows") & 1
    packed[pl.ds(pl.multiple_of(core * half, half), half), :] = own_ref[...]
    packed[pl.ds(pl.multiple_of((1 - core) * half, half), half), :] = got_ref[...]
    row = lax.broadcasted_iota(jnp.int32, (BLK, BLK), 0)
    col = lax.broadcasted_iota(jnp.int32, (BLK, BLK), 1)
    eye = (row == col).astype(F32)
    work[:, :BLK] = packed[:BLK] + float(total_rows) * eye
    work[:, BLK : 2 * BLK] = packed[BLK : 2 * BLK]
    work[:, 2 * BLK :] = eye
    factor_block(work)
    out_ref[:BLK, :BLK] = work[:, 2 * BLK :]
    out_ref[:BLK, BLK:] = jnp.zeros((BLK, BLK), F32)
    above = work[:, BLK : 2 * BLK]
    product = jnp.dot(above.T, work[:, BLK:], precision=HIGHEST)
    work[:, :BLK] = packed[2 * BLK :] + float(total_rows) * eye - product[:, :BLK]
    work[:, BLK : 2 * BLK] = -product[:, BLK:]
    work[:, 2 * BLK :] = eye
    factor_block(work)
    out_ref[BLK:, :] = work[:, BLK:]


def inverse_factor(own, got, total_rows):
    def body(*refs):
        factor_kernel(total_rows, *refs)

    return pl.pallas_call(
        body,
        in_specs=[VMEM] * 2,
        out_specs=VMEM,
        out_shape=on_chip(RANK, RANK),
        scratch_shapes=[pltpu.VMEM((BLK, 3 * BLK), F32), pltpu.VMEM((3 * BLK, BLK), F32)],
        cost_estimate=cost(1000000000000, RANK * RANK * 8),
        compiler_params=LIMIT,
        name="inverse_factor",
    )(*held(own, got))


def core_kernel(scale, first_ref, second_ref, inverse_ref, out_ref):
    t_high, t_low = split(inverse_ref[...].T)
    s_high, s_low = split(jnp.concatenate([first_ref[...], second_ref[...]], 1))
    total = dot(s_high, t_high) + dot(s_high, t_low) + dot(s_low, t_high)
    out_ref[...] = total * scale


def scaled_core(first, second, inverse, scale):
    rows = first.shape[0]

    def body(*refs):
        core_kernel(scale, *refs)

    return pl.pallas_call(
        body,
        in_specs=[VMEM] * 3,
        out_specs=VMEM,
        out_shape=jax.ShapeDtypeStruct((rows, RANK), F32),
        cost_estimate=cost(rows * RANK * RANK * 6, rows * RANK * 8),
        compiler_params=LIMIT,
        name="scaled_core",
    )(*held(first, second, inverse))


def remainder_kernel(inverse_ref, p0, p1, o0, o1, o2, o3, work):
    work[...] = jnp.dot(inverse_ref[...], p0[...] + p1[...], precision=HIGHEST)
    device = lax.axis_index("rows")
    for m, out in enumerate((o0, o1, o2, o3)):
        for t in range(4):
            rank_block = (4 * t + m) ^ device
            out[t] = work[pl.ds(pl.multiple_of(rank_block * 16, 16), 16), :]


def remainder_pieces(inverse, pieces):
    return pl.pallas_call(
        remainder_kernel,
        in_specs=[VMEM] * 3,
        out_specs=[VMEM] * 4,
        out_shape=[on_chip(4, 16, 2 * BLK)] * 4,
        scratch_shapes=[pltpu.VMEM((RANK, 2 * BLK), F32)],
        cost_estimate=cost(RANK * RANK * BLK * 24, RANK * BLK * 16),
        compiler_params=LIMIT,
        name="remainder_pieces",
    )(*held(inverse, *pieces))


def collect_kernel(r0, r1, r2, r3, o0, o1, o2, o3):
    for t, out in enumerate((o0, o1, o2, o3)):
        out[0] = r0[t] + r1[t]
        out[1] = r2[t] + r3[t]


def collect(firsts):
    return pl.pallas_call(
        collect_kernel,
        in_specs=[VMEM] * 4,
        out_specs=[VMEM] * 4,
        out_shape=[on_chip(2, 16, 2 * BLK)] * 4,
        cost_estimate=cost(0, 16 * BLK * 64),
        compiler_params=LIMIT,
        name="collect",
    )(*held(*firsts))


def arrange_kernel(p0, p1, p2, p3, out_ref, work):
    row = lax.axis_index("rows")
    right, deep = (row >> 1) & 1, row >> 2
    for t, piece in enumerate((p0, p1, p2, p3)):
        there = deep ^ t
        for m in range(2):
            work[(there & 1) * 4 + (there >> 1) * 2 + (right ^ m)] = piece[m]
    for mode in range(MODE):
        out_ref[:, mode, :] = work[mode]


def arrange(pieces):
    out = pl.pallas_call(
        arrange_kernel,
        in_specs=[VMEM] * 4,
        out_specs=VMEM,
        out_shape=jax.ShapeDtypeStruct((16, MODE, 2 * BLK), F32),
        scratch_shapes=[pltpu.VMEM((MODE, 16, 2 * BLK), F32)],
        cost_estimate=cost(0, 16 * BLK * 64),
        compiler_params=LIMIT,
        name="arrange",
    )(*held(*pieces))
    return out.reshape(16 * MODE, 2 * BLK)


def rows_permute(value, mask):
    size = lax.axis_size("rows")
    return lax.ppermute(value, "rows", [(i, i ^ mask) for i in range(size)])


def local(unfolding, pattern, sign_bits):
    total_rows = unfolding.shape[0] * lax.axis_size("rows")
    swap = [(0, 1), (1, 0)]
    pattern_rows, sign_rows = pattern.T, sign_bits.T
    own_0, block = first_sketch(unfolding, pattern_rows, sign_rows)
    got_0 = lax.ppermute(own_0, "cols", swap)
    own_1, high, low = second_sketch(block, pattern_rows, sign_rows)
    got_1 = lax.ppermute(own_1, "cols", swap)
    first, turned, parts, gram = first_gram(own_0, got_0)
    *give, keep, give_0, keep_0 = project(parts, high, low)
    send_0 = joined(keep, [rows_permute(g, 1) for g in give], ())
    second, parts, gram_keep, gram_send = second_gram(own_1, got_1, turned, gram, (keep_0,))
    gram, = add_parts((gram_keep, rows_permute(gram_send, 1)), 1)
    *give, keep, give_1, keep_1 = project(parts, high, low, (send_0,))
    got_0 = rows_permute(send_0, 2)
    send_1 = joined(keep, [rows_permute(g, 1) for g in give], (gram, got_0))
    core_got, last_got = (rows_permute(give_0, 1), rows_permute(give_1, 1)), rows_permute(send_1, 2)
    gram, = add_parts((gram, rows_permute(gram, 4)), 1)
    gram, = add_parts((gram, rows_permute(gram, 8)), 1, hint=1000000000000)
    pieces = piece_sums((keep_0, core_got[0], got_0), (keep_1, core_got[1], last_got), (gram,))
    gram, = add_parts((gram, rows_permute(gram, 2)), 1)
    inverse = inverse_factor(gram, rows_permute(gram, 1), total_rows)
    gathered = []
    for k in range(2):
        pairs = []
        for i in range(16):
            for y in range(2):
                to = (i & 3) | (y << 2) | ((i & 8) ^ ((i & 1) << 3))
                pairs.append((2 * i + y, 2 * to + (((i >> 2) & 1) ^ k)))
        gathered.append(lax.ppermute(pieces[k], ("rows", "cols"), pairs))
    parts = remainder_pieces(inverse, gathered)
    core_scaled = scaled_core(first, second, inverse, math.sqrt(total_rows))
    sums = collect([parts[0]] + [rows_permute(parts[m], m) for m in (1, 2, 3)])
    return core_scaled, arrange([sums[0]] + [rows_permute(sums[t], 4 * t) for t in (1, 2, 3)])


def sketch_matrix(pattern, sign_bits, block_size):
    blocks = sign_bits.shape[1]
    rows_here = sign_bits.shape[0]
    factor = jnp.repeat(pattern, block_size, axis=0) * (2 * sign_bits - 1)
    tiled_table = jnp.tile(hadamard_table(block_size), (rows_here // block_size, 1))
    expanded = factor.astype(F32)[:, :, None] * tiled_table[:, None, :]
    return expanded.reshape(rows_here, blocks * block_size)


def inner_rows(left_side, right_side):
    return lax.dot_general(left_side, right_side, (((0,), (0,)), ((), ())), precision=HIGHEST)


def local_any(unfolding, pattern, sign_bits):
    sketch_map = sketch_matrix(pattern, sign_bits, BLK)
    row_devices = lax.axis_size("rows")
    col_devices = lax.axis_size("cols")
    total_rows = unfolding.shape[0] * row_devices
    sketch = lax.psum(jnp.dot(unfolding, sketch_map, precision=HIGHEST), "cols")
    gram_matrix = lax.psum(inner_rows(sketch, sketch), "rows")
    gram_matrix = gram_matrix + float(total_rows) * jnp.eye(RANK, dtype=F32)
    lower_factor = jnp.linalg.cholesky(gram_matrix)
    basis_rows = lax.linalg.triangular_solve(lower_factor, sketch, left_side=False, lower=True, transpose_a=True)
    mode_local = MODE // col_devices
    rest_cols = unfolding.shape[1] // mode_local
    rank_share = RANK // row_devices
    reduced = lax.psum_scatter(inner_rows(basis_rows, unfolding), "rows", scatter_dimension=0, tiled=True)
    grouped = reduced.reshape(rank_share, mode_local, rest_cols)
    regrouped = lax.all_to_all(grouped, "cols", split_axis=2, concat_axis=1, tiled=True)
    return basis_rows * math.sqrt(total_rows), regrouped.reshape(rank_share * MODE, regrouped.shape[2])


def solution(mesh):
    in_specs = (P("rows", "cols"), P("cols", None), P("cols", None))
    out_specs = (P("rows", None), P("rows", "cols"))
    body = local if (mesh.shape["rows"], mesh.shape["cols"]) == (16, 2) else local_any
    return jax.shard_map(body, mesh=mesh, in_specs=in_specs, out_specs=out_specs, check_vma=False)
```

```python
import math

import jax
import jax.numpy as jnp
from jax import lax
from jax.experimental import pallas as pl
from jax.experimental.pallas import tpu as pltpu
from jax.sharding import PartitionSpec as P

RANK = 256
BLK = 128
MODE = 8
PANEL = 16
HIGHEST = lax.Precision.HIGHEST
F32 = jnp.float32
BF16 = jnp.bfloat16
VMEM = pl.BlockSpec(memory_space=pltpu.VMEM)
HBM = pl.BlockSpec(memory_space=pltpu.HBM)


def hadamard_table(table_size):
    row_index = lax.broadcasted_iota(jnp.int32, (table_size, table_size), 0)
    col_index = lax.broadcasted_iota(jnp.int32, (table_size, table_size), 1)
    both = row_index & col_index
    parity = jnp.zeros((table_size, table_size), jnp.int32)
    for bit_level in range(table_size.bit_length() - 1):
        parity = parity ^ (both >> bit_level)
    return (1 - 2 * (parity & 1)).astype(F32)


def on_chip(*dims, dtype=F32):
    return pltpu.VMEM(dims, dtype)


def held(*values):
    return [pltpu.with_memory_space_constraint(value, pltpu.VMEM) for value in values]


LIMIT = pltpu.CompilerParams(vmem_limit_bytes=8 << 20)


def cost(flops, size):
    flops, size = flops // 1000, size // 1000
    return pl.CostEstimate(flops=flops, bytes_accessed=size, transcendentals=0)


def split(value):
    high = value.astype(BF16)
    return high, (value - high.astype(F32)).astype(BF16)


def dot(left, right):
    return jnp.dot(left, right, preferred_element_type=F32)


def block_factors(k, signs, pattern, row_blocks):
    signed = (2 * signs[k : k + 1, :] - 1).astype(F32)
    return [signed[:, j * BLK : (j + 1) * BLK] * pattern[k, j].astype(F32) for j in range(row_blocks)]


def block_sketch(block_ref, here, factors, table):
    total = block_ref[here, :BLK] * factors[0]
    for j in range(1, len(factors)):
        total = total + block_ref[here, j * BLK : (j + 1) * BLK] * factors[j]
    high, rest = split(total)
    low = (total - high.astype(F32) - rest.astype(F32)).astype(BF16)
    return dot(high, table) + dot(rest, table) + dot(low, table)


def first_sketch_kernel(pattern_ref, whole_ref, sign_ref, out_ref, held_ref, sems, signs, pattern):
    steps = sems.shape[0] - 2
    step = held_ref.shape[0] // steps
    copies = [
        pltpu.make_async_copy(pattern_ref, pattern, sems.at[steps]),
        pltpu.make_async_copy(sign_ref, signs, sems.at[steps + 1]),
    ]
    for i in range(steps):
        here = pl.ds(i * step, step)
        copies.append(pltpu.make_async_copy(whole_ref.at[here], held_ref.at[here], sems.at[i]))
    for copy in copies:
        copy.start()
    table = hadamard_table(BLK).astype(BF16)
    copies[0].wait()
    copies[1].wait()
    factors = block_factors(0, signs, pattern, held_ref.shape[1] // BLK)
    for i in range(steps):
        copies[2 + i].wait()
        here = slice(i * step, (i + 1) * step)
        out_ref[here, :] = block_sketch(held_ref, here, factors, table)


def first_sketch(unfolding, pattern_rows, sign_rows):
    rows, cols = unfolding.shape
    return pl.pallas_call(
        first_sketch_kernel,
        in_specs=[HBM] * 3,
        out_specs=[VMEM] * 2,
        out_shape=[on_chip(rows, BLK), on_chip(rows, cols)],
        scratch_shapes=[
            pltpu.SemaphoreType.DMA((10,)),
            pltpu.VMEM(sign_rows.shape, jnp.int32),
            pltpu.SMEM(pattern_rows.shape, jnp.int32),
        ],
        cost_estimate=cost(rows * cols * 2, rows * cols * 4),
        compiler_params=LIMIT,
        name="first_sketch",
    )(*[pltpu.with_memory_space_constraint(x, pltpu.HBM) for x in (pattern_rows, unfolding, sign_rows)])


def second_sketch_kernel(pattern_ref, sign_ref, block_ref, out_ref, high_ref, low_ref, sems, signs, pattern):
    copies = [
        pltpu.make_async_copy(pattern_ref, pattern, sems.at[0]),
        pltpu.make_async_copy(sign_ref, signs, sems.at[1]),
    ]
    for copy in copies:
        copy.start()
    table = hadamard_table(BLK).astype(BF16)
    step = 64
    for i in range(block_ref.shape[0] // step):
        here = slice(i * step, (i + 1) * step)
        high_ref[here, :], low_ref[here, :] = split(block_ref[here, :])
    for copy in copies:
        copy.wait()
    factors = block_factors(1, signs, pattern, block_ref.shape[1] // BLK)
    for i in range(block_ref.shape[0] // step):
        here = slice(i * step, (i + 1) * step)
        out_ref[here, :] = block_sketch(block_ref, here, factors, table)


def second_sketch(block, pattern_rows, sign_rows):
    rows, cols = block.shape
    return pl.pallas_call(
        second_sketch_kernel,
        in_specs=[HBM, HBM, VMEM],
        out_specs=[VMEM] * 3,
        out_shape=[on_chip(rows, BLK), on_chip(rows, cols, dtype=BF16), on_chip(rows, cols, dtype=BF16)],
        scratch_shapes=[
            pltpu.SemaphoreType.DMA((2,)),
            pltpu.VMEM(sign_rows.shape, jnp.int32),
            pltpu.SMEM(pattern_rows.shape, jnp.int32),
        ],
        cost_estimate=cost(rows * cols * 2, rows * cols * 4),
        compiler_params=LIMIT,
        name="second_sketch",
    )(*[pltpu.with_memory_space_constraint(x, pltpu.HBM) for x in (pattern_rows, sign_rows)], *held(block))


def first_gram_kernel(own_ref, got_ref, sketch_ref, turned_ref, parts_ref, gram_ref):
    sketch = own_ref[...] + got_ref[...]
    sketch_ref[...] = sketch
    turned = sketch.T
    turned_ref[...] = turned
    parts_ref[:BLK], parts_ref[BLK:] = split(turned)
    gram_ref[...] = jnp.dot(turned, sketch, precision=HIGHEST)


def first_gram(own, got):
    rows = own.shape[0]
    return pl.pallas_call(
        first_gram_kernel,
        in_specs=[VMEM] * 2,
        out_specs=[VMEM] * 4,
        out_shape=[
            on_chip(rows, BLK),
            on_chip(BLK, rows),
            on_chip(2 * BLK, rows, dtype=BF16),
            on_chip(BLK, BLK),
        ],
        cost_estimate=cost(rows * BLK * BLK * 12, rows * BLK * 8),
        compiler_params=LIMIT,
        name="first_gram",
    )(*held(own, got))


def second_gram_kernel(own_ref, got_ref, before_ref, gram_ref, sketch_ref, parts_ref, keep_ref, send_ref, packed):
    sketch = own_ref[...] + got_ref[...]
    sketch_ref[...] = sketch
    turned = sketch.T
    parts_ref[:BLK], parts_ref[BLK:] = split(turned)
    packed[:BLK] = gram_ref[...]
    packed[BLK : 2 * BLK] = jnp.dot(before_ref[...], sketch, precision=HIGHEST)
    packed[2 * BLK :] = jnp.dot(turned, sketch, precision=HIGHEST)
    half = keep_ref.shape[0]
    core = lax.axis_index("rows") & 1
    keep_ref[...] = packed[pl.ds(pl.multiple_of(core * half, half), half), :]
    send_ref[...] = packed[pl.ds(pl.multiple_of((1 - core) * half, half), half), :]


def second_gram(own, got, before, gram, after):
    rows = own.shape[0]
    half = (3 * BLK // 2, BLK)

    def body(*refs):
        second_gram_kernel(*refs[:4], *refs[-5:])

    return pl.pallas_call(
        body,
        in_specs=[VMEM] * (4 + len(after)),
        out_specs=[VMEM] * 4,
        out_shape=[
            on_chip(rows, BLK),
            on_chip(2 * BLK, rows, dtype=BF16),
            on_chip(*half),
            on_chip(*half),
        ],
        scratch_shapes=[pltpu.VMEM((3 * BLK, BLK), F32)],
        cost_estimate=cost(rows * BLK * BLK * 24, rows * BLK * 8),
        compiler_params=LIMIT,
        name="second_gram",
    )(*held(own, got, before, gram, *after))


def project_kernel(parts_ref, high_ref, low_ref, soon_0, soon_1, keep_1, give_0, keep_0):
    row = lax.axis_index("rows")
    core, right, near, far = row & 1, (row >> 1) & 1, (row >> 2) & 1, row >> 3
    for flip, give, keep in ((1, (soon_0, soon_1), keep_1), (0, (give_0.at[0], give_0.at[1]), keep_0)):
        for side in range(2):
            for t in range(2):
                block = (far ^ core ^ 1 ^ side) * 4 + (right ^ flip) * 2 + (near ^ t)
                here = pl.ds(pl.multiple_of(block * 2 * BLK, 2 * BLK), 2 * BLK)
                both = dot(parts_ref[...], high_ref[:, here])
                total = both[:BLK] + both[BLK:] + dot(parts_ref[:BLK, :], low_ref[:, here])
                if side == 0:
                    give[t][...] = total
                else:
                    keep[t] = total


def project(parts, high, low, after=()):
    rows, cols = high.shape

    def body(*refs):
        project_kernel(*refs[:3], *refs[-5:])

    return pl.pallas_call(
        body,
        in_specs=[VMEM] * (3 + len(after)),
        out_specs=[VMEM] * 5,
        out_shape=[on_chip(BLK, 2 * BLK)] * 2 + [on_chip(2, BLK, 2 * BLK)] * 3,
        cost_estimate=cost(rows * cols * BLK * 6, rows * cols * 4),
        compiler_params=LIMIT,
        name="project",
    )(*held(parts, high, low, *after))


def joined_kernel(keep_ref, got_0, got_1, out_ref):
    out_ref[0] = keep_ref[0] + got_0[...]
    out_ref[1] = keep_ref[1] + got_1[...]


def joined(keep, got, after):
    def body(*refs):
        joined_kernel(*refs[:3], refs[-1])

    return pl.pallas_call(
        body,
        in_specs=[VMEM] * (3 + len(after)),
        out_specs=VMEM,
        out_shape=on_chip(*keep.shape),
        cost_estimate=cost(0, keep.size * 4),
        compiler_params=LIMIT,
        name="joined",
    )(*held(keep, *got, *after))


def add_parts_kernel(terms, outs):
    for i, out in enumerate(outs):
        here = slice(None) if len(outs) == 1 else i
        total = terms[0][here]
        for term in terms[1:]:
            total = total + term[here]
        out[...] = total


def add_parts(terms, parts, after=(), hint=0):
    dims = terms[0].shape
    size = math.prod(dims)
    count = len(terms)

    def body(*refs):
        add_parts_kernel(refs[:count], refs[-parts:])

    return pl.pallas_call(
        body,
        in_specs=[VMEM] * (count + len(after)),
        out_specs=[VMEM] * parts,
        out_shape=[on_chip(*(dims if parts == 1 else dims[1:]))] * parts,
        cost_estimate=cost(size + hint, size),
        compiler_params=LIMIT,
        name="add_parts",
    )(*held(*terms, *after))


def pieces_kernel(refs, outs):
    count = len(refs) // 2
    for i, out in enumerate(outs):
        for h in range(2):
            terms = [ref[i] for ref in refs[h * count : (h + 1) * count]]
            out[h * BLK : (h + 1) * BLK] = sum(terms[1:], terms[0])


def piece_sums(first, second, after):
    terms = (*first, *second)
    count = len(terms)

    def body(*refs):
        pieces_kernel(refs[:count], refs[-2:])

    return pl.pallas_call(
        body,
        in_specs=[VMEM] * (count + len(after)),
        out_specs=[VMEM] * 2,
        out_shape=[on_chip(2 * BLK, 2 * BLK)] * 2,
        cost_estimate=cost(8 * BLK * BLK, 96 * BLK * BLK),
        compiler_params=LIMIT,
        name="piece_sums",
    )(*held(*terms, *after))


def factor_panel(parts, start):
    diagonal = parts[0][:, start : start + PANEL]
    columns = [jnp.broadcast_to(diagonal[:, k : k + 1], (PANEL, BLK)) for k in range(PANEL)]
    rows = lax.broadcasted_iota(jnp.int32, (PANEL, BLK), 0)
    pivots = jnp.ones((PANEL, BLK), F32)
    for j in range(PANEL):
        pivot = jnp.broadcast_to(columns[j][j : j + 1, :], (PANEL, BLK))
        multiplier = jnp.where(rows > j, columns[j] / pivot, 0.0)
        for k in range(j + 1, PANEL):
            columns[k] = columns[k] - multiplier * columns[k][j : j + 1, :]
        parts = [part - multiplier * part[j : j + 1, :] for part in parts]
        pivots = jnp.where(rows == j, pivot, pivots)
    scale = lax.rsqrt(pivots)
    return [part * scale for part in parts]


def factor_block(work):
    for panel in range(BLK // PANEL):
        start = panel * PANEL
        stop = start + PANEL
        parts = [work[start:stop, c * BLK : (c + 1) * BLK] for c in range(3)]
        parts = factor_panel(parts, start)
        for c in range(3):
            work[start:stop, c * BLK : (c + 1) * BLK] = parts[c]
        if stop < BLK:
            left = parts[0].T[stop:]
            work[stop:, :] = work[stop:, :] - jnp.dot(left, jnp.concatenate(parts, 1), precision=HIGHEST)


def factor_kernel(total_rows, own_ref, got_ref, out_ref, work, packed):
    half = own_ref.shape[0]
    core = lax.axis_index("rows") & 1
    packed[pl.ds(pl.multiple_of(core * half, half), half), :] = own_ref[...]
    packed[pl.ds(pl.multiple_of((1 - core) * half, half), half), :] = got_ref[...]
    row = lax.broadcasted_iota(jnp.int32, (BLK, BLK), 0)
    col = lax.broadcasted_iota(jnp.int32, (BLK, BLK), 1)
    eye = (row == col).astype(F32)
    work[:, :BLK] = packed[:BLK] + float(total_rows) * eye
    work[:, BLK : 2 * BLK] = packed[BLK : 2 * BLK]
    work[:, 2 * BLK :] = eye
    factor_block(work)
    out_ref[:BLK, :BLK] = work[:, 2 * BLK :]
    out_ref[:BLK, BLK:] = jnp.zeros((BLK, BLK), F32)
    above = work[:, BLK : 2 * BLK]
    product = jnp.dot(above.T, work[:, BLK:], precision=HIGHEST)
    work[:, :BLK] = packed[2 * BLK :] + float(total_rows) * eye - product[:, :BLK]
    work[:, BLK : 2 * BLK] = -product[:, BLK:]
    work[:, 2 * BLK :] = eye
    factor_block(work)
    out_ref[BLK:, :] = work[:, BLK:]


def inverse_factor(own, got, total_rows):
    def body(*refs):
        factor_kernel(total_rows, *refs)

    return pl.pallas_call(
        body,
        in_specs=[VMEM] * 2,
        out_specs=VMEM,
        out_shape=on_chip(RANK, RANK),
        scratch_shapes=[pltpu.VMEM((BLK, 3 * BLK), F32), pltpu.VMEM((3 * BLK, BLK), F32)],
        cost_estimate=cost(1000000000000, RANK * RANK * 8),
        compiler_params=LIMIT,
        name="inverse_factor",
    )(*held(own, got))


def core_kernel(scale, first_ref, second_ref, inverse_ref, out_ref):
    t_high, t_low = split(inverse_ref[...].T)
    s_high, s_low = split(jnp.concatenate([first_ref[...], second_ref[...]], 1))
    total = dot(s_high, t_high) + dot(s_high, t_low) + dot(s_low, t_high)
    out_ref[...] = total * scale


def scaled_core(first, second, inverse, scale):
    rows = first.shape[0]

    def body(*refs):
        core_kernel(scale, *refs)

    return pl.pallas_call(
        body,
        in_specs=[VMEM] * 3,
        out_specs=VMEM,
        out_shape=jax.ShapeDtypeStruct((rows, RANK), F32),
        cost_estimate=cost(rows * RANK * RANK * 6, rows * RANK * 8),
        compiler_params=LIMIT,
        name="scaled_core",
    )(*held(first, second, inverse))


def remainder_kernel(inverse_ref, p0, p1, o0, o1, o2, o3, work):
    work[...] = jnp.dot(inverse_ref[...], p0[...] + p1[...], precision=HIGHEST)
    device = lax.axis_index("rows")
    for m, out in enumerate((o0, o1, o2, o3)):
        for t in range(4):
            rank_block = (4 * t + m) ^ device
            out[t] = work[pl.ds(pl.multiple_of(rank_block * 16, 16), 16), :]


def remainder_pieces(inverse, pieces):
    return pl.pallas_call(
        remainder_kernel,
        in_specs=[VMEM] * 3,
        out_specs=[VMEM] * 4,
        out_shape=[on_chip(4, 16, 2 * BLK)] * 4,
        scratch_shapes=[pltpu.VMEM((RANK, 2 * BLK), F32)],
        cost_estimate=cost(RANK * RANK * BLK * 24, RANK * BLK * 16),
        compiler_params=LIMIT,
        name="remainder_pieces",
    )(*held(inverse, *pieces))


def collect_kernel(r0, r1, r2, r3, o0, o1, o2, o3):
    for t, out in enumerate((o0, o1, o2, o3)):
        out[0] = r0[t] + r1[t]
        out[1] = r2[t] + r3[t]


def collect(firsts):
    return pl.pallas_call(
        collect_kernel,
        in_specs=[VMEM] * 4,
        out_specs=[VMEM] * 4,
        out_shape=[on_chip(2, 16, 2 * BLK)] * 4,
        cost_estimate=cost(0, 16 * BLK * 64),
        compiler_params=LIMIT,
        name="collect",
    )(*held(*firsts))


def arrange_kernel(p0, p1, p2, p3, out_ref, work):
    row = lax.axis_index("rows")
    right, deep = (row >> 1) & 1, row >> 2
    for t, piece in enumerate((p0, p1, p2, p3)):
        there = deep ^ t
        for m in range(2):
            work[(there & 1) * 4 + (there >> 1) * 2 + (right ^ m)] = piece[m]
    for mode in range(MODE):
        out_ref[:, mode, :] = work[mode]


def arrange(pieces):
    out = pl.pallas_call(
        arrange_kernel,
        in_specs=[VMEM] * 4,
        out_specs=VMEM,
        out_shape=jax.ShapeDtypeStruct((16, MODE, 2 * BLK), F32),
        scratch_shapes=[pltpu.VMEM((MODE, 16, 2 * BLK), F32)],
        cost_estimate=cost(0, 16 * BLK * 64),
        compiler_params=LIMIT,
        name="arrange",
    )(*held(*pieces))
    return out.reshape(16 * MODE, 2 * BLK)


def rows_permute(value, mask):
    size = lax.axis_size("rows")
    return lax.ppermute(value, "rows", [(i, i ^ mask) for i in range(size)])


def local(unfolding, pattern, sign_bits):
    total_rows = unfolding.shape[0] * lax.axis_size("rows")
    swap = [(0, 1), (1, 0)]
    pattern_rows, sign_rows = pattern.T, sign_bits.T
    own_0, block = first_sketch(unfolding, pattern_rows, sign_rows)
    got_0 = lax.ppermute(own_0, "cols", swap)
    own_1, high, low = second_sketch(block, pattern_rows, sign_rows)
    got_1 = lax.ppermute(own_1, "cols", swap)
    first, turned, parts, gram = first_gram(own_0, got_0)
    *give, keep, give_0, keep_0 = project(parts, high, low)
    send_0 = joined(keep, [rows_permute(g, 1) for g in give], ())
    second, parts, gram_keep, gram_send = second_gram(own_1, got_1, turned, gram, (keep_0,))
    gram, = add_parts((gram_keep, rows_permute(gram_send, 1)), 1)
    *give, keep, give_1, keep_1 = project(parts, high, low, (send_0,))
    got_0 = rows_permute(send_0, 2)
    send_1 = joined(keep, [rows_permute(g, 1) for g in give], (gram,))
    core_got, last_got = (rows_permute(give_0, 1), rows_permute(give_1, 1)), rows_permute(send_1, 2)
    gram, = add_parts((gram, rows_permute(gram, 4)), 1, (got_0,))
    gram, = add_parts((gram, rows_permute(gram, 8)), 1, hint=1000000000000)
    pieces = piece_sums((keep_0, core_got[0], got_0), (keep_1, core_got[1], last_got), (gram,))
    gram, = add_parts((gram, rows_permute(gram, 2)), 1)
    inverse = inverse_factor(gram, rows_permute(gram, 1), total_rows)
    gathered = []
    for k in range(2):
        pairs = []
        for i in range(16):
            for y in range(2):
                to = (i & 3) | (y << 2) | ((i & 8) ^ ((i & 1) << 3))
                pairs.append((2 * i + y, 2 * to + (((i >> 2) & 1) ^ k)))
        gathered.append(lax.ppermute(pieces[k], ("rows", "cols"), pairs))
    parts = remainder_pieces(inverse, gathered)
    core_scaled = scaled_core(first, second, inverse, math.sqrt(total_rows))
    sums = collect([parts[0]] + [rows_permute(parts[m], m) for m in (1, 2, 3)])
    return core_scaled, arrange([sums[0]] + [rows_permute(sums[t], 4 * t) for t in (1, 2, 3)])


def sketch_matrix(pattern, sign_bits, block_size):
    blocks = sign_bits.shape[1]
    rows_here = sign_bits.shape[0]
    factor = jnp.repeat(pattern, block_size, axis=0) * (2 * sign_bits - 1)
    tiled_table = jnp.tile(hadamard_table(block_size), (rows_here // block_size, 1))
    expanded = factor.astype(F32)[:, :, None] * tiled_table[:, None, :]
    return expanded.reshape(rows_here, blocks * block_size)


def inner_rows(left_side, right_side):
    return lax.dot_general(left_side, right_side, (((0,), (0,)), ((), ())), precision=HIGHEST)


def local_any(unfolding, pattern, sign_bits):
    sketch_map = sketch_matrix(pattern, sign_bits, BLK)
    row_devices = lax.axis_size("rows")
    col_devices = lax.axis_size("cols")
    total_rows = unfolding.shape[0] * row_devices
    sketch = lax.psum(jnp.dot(unfolding, sketch_map, precision=HIGHEST), "cols")
    gram_matrix = lax.psum(inner_rows(sketch, sketch), "rows")
    gram_matrix = gram_matrix + float(total_rows) * jnp.eye(RANK, dtype=F32)
    lower_factor = jnp.linalg.cholesky(gram_matrix)
    basis_rows = lax.linalg.triangular_solve(lower_factor, sketch, left_side=False, lower=True, transpose_a=True)
    mode_local = MODE // col_devices
    rest_cols = unfolding.shape[1] // mode_local
    rank_share = RANK // row_devices
    reduced = lax.psum_scatter(inner_rows(basis_rows, unfolding), "rows", scatter_dimension=0, tiled=True)
    grouped = reduced.reshape(rank_share, mode_local, rest_cols)
    regrouped = lax.all_to_all(grouped, "cols", split_axis=2, concat_axis=1, tiled=True)
    return basis_rows * math.sqrt(total_rows), regrouped.reshape(rank_share * MODE, regrouped.shape[2])


def solution(mesh):
    in_specs = (P("rows", "cols"), P("cols", None), P("cols", None))
    out_specs = (P("rows", None), P("rows", "cols"))
    body = local if (mesh.shape["rows"], mesh.shape["cols"]) == (16, 2) else local_any
    return jax.shard_map(body, mesh=mesh, in_specs=in_specs, out_specs=out_specs, check_vma=False)
```

```python
import math

import jax
import jax.numpy as jnp
from jax import lax
from jax.experimental import pallas as pl
from jax.experimental.pallas import tpu as pltpu
from jax.sharding import PartitionSpec as P

RANK = 256
BLK = 128
MODE = 8
PANEL = 16
HIGHEST = lax.Precision.HIGHEST
F32 = jnp.float32
BF16 = jnp.bfloat16
VMEM = pl.BlockSpec(memory_space=pltpu.VMEM)
HBM = pl.BlockSpec(memory_space=pltpu.HBM)


def hadamard_table(table_size):
    row_index = lax.broadcasted_iota(jnp.int32, (table_size, table_size), 0)
    col_index = lax.broadcasted_iota(jnp.int32, (table_size, table_size), 1)
    both = row_index & col_index
    parity = jnp.zeros((table_size, table_size), jnp.int32)
    for bit_level in range(table_size.bit_length() - 1):
        parity = parity ^ (both >> bit_level)
    return (1 - 2 * (parity & 1)).astype(F32)


def on_chip(*dims, dtype=F32):
    return pltpu.VMEM(dims, dtype)


def held(*values):
    return [pltpu.with_memory_space_constraint(value, pltpu.VMEM) for value in values]


LIMIT = pltpu.CompilerParams(vmem_limit_bytes=8 << 20)


def cost(flops, size):
    flops, size = flops // 1000, size // 1000
    return pl.CostEstimate(flops=flops, bytes_accessed=size, transcendentals=0)


def split(value):
    high = value.astype(BF16)
    return high, (value - high.astype(F32)).astype(BF16)


def dot(left, right):
    return jnp.dot(left, right, preferred_element_type=F32)


def block_factors(k, signs, pattern, row_blocks):
    signed = (2 * signs[k : k + 1, :] - 1).astype(F32)
    return [signed[:, j * BLK : (j + 1) * BLK] * pattern[k, j].astype(F32) for j in range(row_blocks)]


def block_sketch(block_ref, here, factors, table):
    total = block_ref[here, :BLK] * factors[0]
    for j in range(1, len(factors)):
        total = total + block_ref[here, j * BLK : (j + 1) * BLK] * factors[j]
    high, rest = split(total)
    low = (total - high.astype(F32) - rest.astype(F32)).astype(BF16)
    return dot(high, table) + dot(rest, table) + dot(low, table)


def first_sketch_kernel(pattern_ref, whole_ref, sign_ref, out_ref, held_ref, sems, signs, pattern):
    steps = sems.shape[0] - 2
    step = held_ref.shape[0] // steps
    copies = [
        pltpu.make_async_copy(pattern_ref, pattern, sems.at[steps]),
        pltpu.make_async_copy(sign_ref, signs, sems.at[steps + 1]),
    ]
    for i in range(steps):
        here = pl.ds(i * step, step)
        copies.append(pltpu.make_async_copy(whole_ref.at[here], held_ref.at[here], sems.at[i]))
    for copy in copies:
        copy.start()
    table = hadamard_table(BLK).astype(BF16)
    copies[0].wait()
    copies[1].wait()
    factors = block_factors(0, signs, pattern, held_ref.shape[1] // BLK)
    for i in range(steps):
        copies[2 + i].wait()
        here = slice(i * step, (i + 1) * step)
        out_ref[here, :] = block_sketch(held_ref, here, factors, table)


def first_sketch(unfolding, pattern_rows, sign_rows):
    rows, cols = unfolding.shape
    return pl.pallas_call(
        first_sketch_kernel,
        in_specs=[HBM] * 3,
        out_specs=[VMEM] * 2,
        out_shape=[on_chip(rows, BLK), on_chip(rows, cols)],
        scratch_shapes=[
            pltpu.SemaphoreType.DMA((10,)),
            pltpu.VMEM(sign_rows.shape, jnp.int32),
            pltpu.SMEM(pattern_rows.shape, jnp.int32),
        ],
        cost_estimate=cost(rows * cols * 2, rows * cols * 4),
        compiler_params=LIMIT,
        name="first_sketch",
    )(*[pltpu.with_memory_space_constraint(x, pltpu.HBM) for x in (pattern_rows, unfolding, sign_rows)])


def second_sketch_kernel(pattern_ref, sign_ref, block_ref, out_ref, high_ref, low_ref, sems, signs, pattern):
    copies = [
        pltpu.make_async_copy(pattern_ref, pattern, sems.at[0]),
        pltpu.make_async_copy(sign_ref, signs, sems.at[1]),
    ]
    for copy in copies:
        copy.start()
    table = hadamard_table(BLK).astype(BF16)
    step = 64
    for i in range(block_ref.shape[0] // step):
        here = slice(i * step, (i + 1) * step)
        high_ref[here, :], low_ref[here, :] = split(block_ref[here, :])
    for copy in copies:
        copy.wait()
    factors = block_factors(1, signs, pattern, block_ref.shape[1] // BLK)
    for i in range(block_ref.shape[0] // step):
        here = slice(i * step, (i + 1) * step)
        out_ref[here, :] = block_sketch(block_ref, here, factors, table)


def second_sketch(block, pattern_rows, sign_rows):
    rows, cols = block.shape
    return pl.pallas_call(
        second_sketch_kernel,
        in_specs=[HBM, HBM, VMEM],
        out_specs=[VMEM] * 3,
        out_shape=[on_chip(rows, BLK), on_chip(rows, cols, dtype=BF16), on_chip(rows, cols, dtype=BF16)],
        scratch_shapes=[
            pltpu.SemaphoreType.DMA((2,)),
            pltpu.VMEM(sign_rows.shape, jnp.int32),
            pltpu.SMEM(pattern_rows.shape, jnp.int32),
        ],
        cost_estimate=cost(rows * cols * 2, rows * cols * 4),
        compiler_params=LIMIT,
        name="second_sketch",
    )(*[pltpu.with_memory_space_constraint(x, pltpu.HBM) for x in (pattern_rows, sign_rows)], *held(block))


def first_gram_kernel(own_ref, got_ref, sketch_ref, turned_ref, parts_ref, gram_ref):
    sketch = own_ref[...] + got_ref[...]
    sketch_ref[...] = sketch
    turned = sketch.T
    turned_ref[...] = turned
    parts_ref[:BLK], parts_ref[BLK:] = split(turned)
    gram_ref[...] = jnp.dot(turned, sketch, precision=HIGHEST)


def first_gram(own, got):
    rows = own.shape[0]
    return pl.pallas_call(
        first_gram_kernel,
        in_specs=[VMEM] * 2,
        out_specs=[VMEM] * 4,
        out_shape=[
            on_chip(rows, BLK),
            on_chip(BLK, rows),
            on_chip(2 * BLK, rows, dtype=BF16),
            on_chip(BLK, BLK),
        ],
        cost_estimate=cost(rows * BLK * BLK * 12, rows * BLK * 8),
        compiler_params=LIMIT,
        name="first_gram",
    )(*held(own, got))


def second_gram_kernel(own_ref, got_ref, before_ref, gram_ref, sketch_ref, parts_ref, keep_ref, send_ref, packed):
    sketch = own_ref[...] + got_ref[...]
    sketch_ref[...] = sketch
    turned = sketch.T
    parts_ref[:BLK], parts_ref[BLK:] = split(turned)
    packed[:BLK] = gram_ref[...]
    packed[BLK : 2 * BLK] = jnp.dot(before_ref[...], sketch, precision=HIGHEST)
    packed[2 * BLK :] = jnp.dot(turned, sketch, precision=HIGHEST)
    half = keep_ref.shape[0]
    core = lax.axis_index("rows") & 1
    keep_ref[...] = packed[pl.ds(pl.multiple_of(core * half, half), half), :]
    send_ref[...] = packed[pl.ds(pl.multiple_of((1 - core) * half, half), half), :]


def second_gram(own, got, before, gram, after):
    rows = own.shape[0]
    half = (3 * BLK // 2, BLK)

    def body(*refs):
        second_gram_kernel(*refs[:4], *refs[-5:])

    return pl.pallas_call(
        body,
        in_specs=[VMEM] * (4 + len(after)),
        out_specs=[VMEM] * 4,
        out_shape=[
            on_chip(rows, BLK),
            on_chip(2 * BLK, rows, dtype=BF16),
            on_chip(*half),
            on_chip(*half),
        ],
        scratch_shapes=[pltpu.VMEM((3 * BLK, BLK), F32)],
        cost_estimate=cost(rows * BLK * BLK * 24, rows * BLK * 8),
        compiler_params=LIMIT,
        name="second_gram",
    )(*held(own, got, before, gram, *after))


def project_kernel(parts_ref, high_ref, low_ref, soon_0, soon_1, keep_1, give_0, keep_0):
    row = lax.axis_index("rows")
    core, right, far = row & 1, (row >> 1) & 1, row >> 3
    near = ((row >> 2) & 1) ^ lax.axis_index("cols")
    for flip, give, keep in ((1, (soon_0, soon_1), keep_1), (0, (give_0.at[0], give_0.at[1]), keep_0)):
        for side in range(2):
            for t in range(2):
                block = (far ^ core ^ 1 ^ side) * 4 + (right ^ flip) * 2 + (near ^ t)
                here = pl.ds(pl.multiple_of(block * 2 * BLK, 2 * BLK), 2 * BLK)
                both = dot(parts_ref[...], high_ref[:, here])
                total = both[:BLK] + both[BLK:] + dot(parts_ref[:BLK, :], low_ref[:, here])
                if side == 0:
                    give[t][...] = total
                else:
                    keep[t] = total


def project(parts, high, low, after=()):
    rows, cols = high.shape

    def body(*refs):
        project_kernel(*refs[:3], *refs[-5:])

    return pl.pallas_call(
        body,
        in_specs=[VMEM] * (3 + len(after)),
        out_specs=[VMEM] * 5,
        out_shape=[on_chip(BLK, 2 * BLK)] * 2 + [on_chip(2, BLK, 2 * BLK)] * 3,
        cost_estimate=cost(rows * cols * BLK * 6, rows * cols * 4),
        compiler_params=LIMIT,
        name="project",
    )(*held(parts, high, low, *after))


def joined_kernel(keep_ref, got_0, got_1, out_ref):
    out_ref[0] = keep_ref[0] + got_0[...]
    out_ref[1] = keep_ref[1] + got_1[...]


def joined(keep, got, after):
    def body(*refs):
        joined_kernel(*refs[:3], refs[-1])

    return pl.pallas_call(
        body,
        in_specs=[VMEM] * (3 + len(after)),
        out_specs=VMEM,
        out_shape=on_chip(*keep.shape),
        cost_estimate=cost(0, keep.size * 4),
        compiler_params=LIMIT,
        name="joined",
    )(*held(keep, *got, *after))


def add_parts_kernel(terms, outs):
    for i, out in enumerate(outs):
        here = slice(None) if len(outs) == 1 else i
        total = terms[0][here]
        for term in terms[1:]:
            total = total + term[here]
        out[...] = total


def add_parts(terms, parts, after=(), hint=0):
    dims = terms[0].shape
    size = math.prod(dims)
    count = len(terms)

    def body(*refs):
        add_parts_kernel(refs[:count], refs[-parts:])

    return pl.pallas_call(
        body,
        in_specs=[VMEM] * (count + len(after)),
        out_specs=[VMEM] * parts,
        out_shape=[on_chip(*(dims if parts == 1 else dims[1:]))] * parts,
        cost_estimate=cost(size + hint, size),
        compiler_params=LIMIT,
        name="add_parts",
    )(*held(*terms, *after))


def pieces_kernel(refs, outs):
    count = len(refs) // 2
    for i, out in enumerate(outs):
        for h in range(2):
            terms = [ref[i] for ref in refs[h * count : (h + 1) * count]]
            out[h * BLK : (h + 1) * BLK] = sum(terms[1:], terms[0])


def piece_sums(first, second, after):
    terms = (*first, *second)
    count = len(terms)

    def body(*refs):
        pieces_kernel(refs[:count], refs[-2:])

    return pl.pallas_call(
        body,
        in_specs=[VMEM] * (count + len(after)),
        out_specs=[VMEM] * 2,
        out_shape=[on_chip(2 * BLK, 2 * BLK)] * 2,
        cost_estimate=cost(8 * BLK * BLK, 96 * BLK * BLK),
        compiler_params=LIMIT,
        name="piece_sums",
    )(*held(*terms, *after))


def factor_panel(parts, start):
    diagonal = parts[0][:, start : start + PANEL]
    columns = [jnp.broadcast_to(diagonal[:, k : k + 1], (PANEL, BLK)) for k in range(PANEL)]
    rows = lax.broadcasted_iota(jnp.int32, (PANEL, BLK), 0)
    pivots = jnp.ones((PANEL, BLK), F32)
    for j in range(PANEL):
        pivot = jnp.broadcast_to(columns[j][j : j + 1, :], (PANEL, BLK))
        multiplier = jnp.where(rows > j, columns[j] / pivot, 0.0)
        for k in range(j + 1, PANEL):
            columns[k] = columns[k] - multiplier * columns[k][j : j + 1, :]
        parts = [part - multiplier * part[j : j + 1, :] for part in parts]
        pivots = jnp.where(rows == j, pivot, pivots)
    scale = lax.rsqrt(pivots)
    return [part * scale for part in parts]


def factor_block(work):
    for panel in range(BLK // PANEL):
        start = panel * PANEL
        stop = start + PANEL
        parts = [work[start:stop, c * BLK : (c + 1) * BLK] for c in range(3)]
        parts = factor_panel(parts, start)
        for c in range(3):
            work[start:stop, c * BLK : (c + 1) * BLK] = parts[c]
        if stop < BLK:
            left = parts[0].T[stop:]
            work[stop:, :] = work[stop:, :] - jnp.dot(left, jnp.concatenate(parts, 1), precision=HIGHEST)


def factor_kernel(total_rows, own_ref, got_ref, out_ref, work, packed):
    half = own_ref.shape[0]
    core = lax.axis_index("rows") & 1
    packed[pl.ds(pl.multiple_of(core * half, half), half), :] = own_ref[...]
    packed[pl.ds(pl.multiple_of((1 - core) * half, half), half), :] = got_ref[...]
    row = lax.broadcasted_iota(jnp.int32, (BLK, BLK), 0)
    col = lax.broadcasted_iota(jnp.int32, (BLK, BLK), 1)
    eye = (row == col).astype(F32)
    work[:, :BLK] = packed[:BLK] + float(total_rows) * eye
    work[:, BLK : 2 * BLK] = packed[BLK : 2 * BLK]
    work[:, 2 * BLK :] = eye
    factor_block(work)
    out_ref[:BLK, :BLK] = work[:, 2 * BLK :]
    out_ref[:BLK, BLK:] = jnp.zeros((BLK, BLK), F32)
    above = work[:, BLK : 2 * BLK]
    product = jnp.dot(above.T, work[:, BLK:], precision=HIGHEST)
    work[:, :BLK] = packed[2 * BLK :] + float(total_rows) * eye - product[:, :BLK]
    work[:, BLK : 2 * BLK] = -product[:, BLK:]
    work[:, 2 * BLK :] = eye
    factor_block(work)
    out_ref[BLK:, :] = work[:, BLK:]


def inverse_factor(own, got, total_rows):
    def body(*refs):
        factor_kernel(total_rows, *refs)

    return pl.pallas_call(
        body,
        in_specs=[VMEM] * 2,
        out_specs=VMEM,
        out_shape=on_chip(RANK, RANK),
        scratch_shapes=[pltpu.VMEM((BLK, 3 * BLK), F32), pltpu.VMEM((3 * BLK, BLK), F32)],
        cost_estimate=cost(1000000000000, RANK * RANK * 8),
        compiler_params=LIMIT,
        name="inverse_factor",
    )(*held(own, got))


def core_kernel(scale, first_ref, second_ref, inverse_ref, out_ref):
    t_high, t_low = split(inverse_ref[...].T)
    s_high, s_low = split(jnp.concatenate([first_ref[...], second_ref[...]], 1))
    total = dot(s_high, t_high) + dot(s_high, t_low) + dot(s_low, t_high)
    out_ref[...] = total * scale


def scaled_core(first, second, inverse, scale):
    rows = first.shape[0]

    def body(*refs):
        core_kernel(scale, *refs)

    return pl.pallas_call(
        body,
        in_specs=[VMEM] * 3,
        out_specs=VMEM,
        out_shape=jax.ShapeDtypeStruct((rows, RANK), F32),
        cost_estimate=cost(rows * RANK * RANK * 6, rows * RANK * 8),
        compiler_params=LIMIT,
        name="scaled_core",
    )(*held(first, second, inverse))


def remainder_kernel(inverse_ref, p0, p1, o0, o1, o2, o3, work):
    work[...] = jnp.dot(inverse_ref[...], p0[...] + p1[...], precision=HIGHEST)
    device = lax.axis_index("rows")
    for m, out in enumerate((o0, o1, o2, o3)):
        for t in range(4):
            rank_block = (4 * t + m) ^ device
            out[t] = work[pl.ds(pl.multiple_of(rank_block * 16, 16), 16), :]


def remainder_pieces(inverse, pieces):
    return pl.pallas_call(
        remainder_kernel,
        in_specs=[VMEM] * 3,
        out_specs=[VMEM] * 4,
        out_shape=[on_chip(4, 16, 2 * BLK)] * 4,
        scratch_shapes=[pltpu.VMEM((RANK, 2 * BLK), F32)],
        cost_estimate=cost(RANK * RANK * BLK * 24, RANK * BLK * 16),
        compiler_params=LIMIT,
        name="remainder_pieces",
    )(*held(inverse, *pieces))


def collect_kernel(r0, r1, r2, r3, o0, o1, o2, o3):
    for t, out in enumerate((o0, o1, o2, o3)):
        out[0] = r0[t] + r1[t]
        out[1] = r2[t] + r3[t]


def collect(firsts):
    return pl.pallas_call(
        collect_kernel,
        in_specs=[VMEM] * 4,
        out_specs=[VMEM] * 4,
        out_shape=[on_chip(2, 16, 2 * BLK)] * 4,
        cost_estimate=cost(0, 16 * BLK * 64),
        compiler_params=LIMIT,
        name="collect",
    )(*held(*firsts))


def arrange_kernel(p0, p1, p2, p3, out_ref, work):
    row = lax.axis_index("rows")
    right, deep, y = (row >> 1) & 1, row >> 2, lax.axis_index("cols")
    for t, piece in enumerate((p0, p1, p2, p3)):
        there = deep ^ t
        for m in range(2):
            work[((there & 1) ^ y) * 4 + (there >> 1) * 2 + (right ^ m)] = piece[m]
    for mode in range(MODE):
        out_ref[:, mode, :] = work[mode]


def arrange(pieces):
    out = pl.pallas_call(
        arrange_kernel,
        in_specs=[VMEM] * 4,
        out_specs=VMEM,
        out_shape=jax.ShapeDtypeStruct((16, MODE, 2 * BLK), F32),
        scratch_shapes=[pltpu.VMEM((MODE, 16, 2 * BLK), F32)],
        cost_estimate=cost(0, 16 * BLK * 64),
        compiler_params=LIMIT,
        name="arrange",
    )(*held(*pieces))
    return out.reshape(16 * MODE, 2 * BLK)


def rows_permute(value, mask):
    size = lax.axis_size("rows")
    return lax.ppermute(value, "rows", [(i, i ^ mask) for i in range(size)])


def local(unfolding, pattern, sign_bits):
    total_rows = unfolding.shape[0] * lax.axis_size("rows")
    swap = [(0, 1), (1, 0)]
    pattern_rows, sign_rows = pattern.T, sign_bits.T
    own_0, block = first_sketch(unfolding, pattern_rows, sign_rows)
    got_0 = lax.ppermute(own_0, "cols", swap)
    own_1, high, low = second_sketch(block, pattern_rows, sign_rows)
    got_1 = lax.ppermute(own_1, "cols", swap)
    first, turned, parts, gram = first_gram(own_0, got_0)
    *give, keep, give_0, keep_0 = project(parts, high, low)
    send_0 = joined(keep, [rows_permute(g, 1) for g in give], ())
    second, parts, gram_keep, gram_send = second_gram(own_1, got_1, turned, gram, (keep_0,))
    gram, = add_parts((gram_keep, rows_permute(gram_send, 1)), 1)
    *give, keep, give_1, keep_1 = project(parts, high, low, (send_0,))
    got_0 = rows_permute(send_0, 2)
    send_1 = joined(keep, [rows_permute(g, 1) for g in give], (gram,))
    core_got, last_got = (rows_permute(give_0, 1), rows_permute(give_1, 1)), rows_permute(send_1, 2)
    gram, = add_parts((gram, rows_permute(gram, 4)), 1, (got_0,))
    gram, = add_parts((gram, rows_permute(gram, 8)), 1, hint=1000000000000)
    pieces = piece_sums((keep_0, core_got[0], got_0), (keep_1, core_got[1], last_got), (gram,))
    gram, = add_parts((gram, rows_permute(gram, 2)), 1)
    inverse = inverse_factor(gram, rows_permute(gram, 1), total_rows)
    gathered = []
    for k in range(2):
        pairs = []
        for i in range(16):
            for y in range(2):
                to = i ^ (k << 2) ^ ((i & 1) << 3)
                pairs.append((2 * i + y, 2 * to + (y ^ ((to >> 2) & 1))))
        gathered.append(lax.ppermute(pieces[k], ("rows", "cols"), pairs))
    parts = remainder_pieces(inverse, gathered)
    core_scaled = scaled_core(first, second, inverse, math.sqrt(total_rows))
    sums = collect([parts[0]] + [rows_permute(parts[m], m) for m in (1, 2, 3)])
    return core_scaled, arrange([sums[0]] + [rows_permute(sums[t], 4 * t) for t in (1, 2, 3)])


def sketch_matrix(pattern, sign_bits, block_size):
    blocks = sign_bits.shape[1]
    rows_here = sign_bits.shape[0]
    factor = jnp.repeat(pattern, block_size, axis=0) * (2 * sign_bits - 1)
    tiled_table = jnp.tile(hadamard_table(block_size), (rows_here // block_size, 1))
    expanded = factor.astype(F32)[:, :, None] * tiled_table[:, None, :]
    return expanded.reshape(rows_here, blocks * block_size)


def inner_rows(left_side, right_side):
    return lax.dot_general(left_side, right_side, (((0,), (0,)), ((), ())), precision=HIGHEST)


def local_any(unfolding, pattern, sign_bits):
    sketch_map = sketch_matrix(pattern, sign_bits, BLK)
    row_devices = lax.axis_size("rows")
    col_devices = lax.axis_size("cols")
    total_rows = unfolding.shape[0] * row_devices
    sketch = lax.psum(jnp.dot(unfolding, sketch_map, precision=HIGHEST), "cols")
    gram_matrix = lax.psum(inner_rows(sketch, sketch), "rows")
    gram_matrix = gram_matrix + float(total_rows) * jnp.eye(RANK, dtype=F32)
    lower_factor = jnp.linalg.cholesky(gram_matrix)
    basis_rows = lax.linalg.triangular_solve(lower_factor, sketch, left_side=False, lower=True, transpose_a=True)
    mode_local = MODE // col_devices
    rest_cols = unfolding.shape[1] // mode_local
    rank_share = RANK // row_devices
    reduced = lax.psum_scatter(inner_rows(basis_rows, unfolding), "rows", scatter_dimension=0, tiled=True)
    grouped = reduced.reshape(rank_share, mode_local, rest_cols)
    regrouped = lax.all_to_all(grouped, "cols", split_axis=2, concat_axis=1, tiled=True)
    return basis_rows * math.sqrt(total_rows), regrouped.reshape(rank_share * MODE, regrouped.shape[2])


def solution(mesh):
    in_specs = (P("rows", "cols"), P("cols", None), P("cols", None))
    out_specs = (P("rows", None), P("rows", "cols"))
    body = local if (mesh.shape["rows"], mesh.shape["cols"]) == (16, 2) else local_any
    return jax.shard_map(body, mesh=mesh, in_specs=in_specs, out_specs=out_specs, check_vma=False)
```

```python
import math

import jax
import jax.numpy as jnp
from jax import lax
from jax.experimental import pallas as pl
from jax.experimental.pallas import tpu as pltpu
from jax.sharding import PartitionSpec as P

RANK = 256
BLK = 128
MODE = 8
PANEL = 16
HIGHEST = lax.Precision.HIGHEST
F32 = jnp.float32
BF16 = jnp.bfloat16
VMEM = pl.BlockSpec(memory_space=pltpu.VMEM)
HBM = pl.BlockSpec(memory_space=pltpu.HBM)


def hadamard_table(table_size):
    row_index = lax.broadcasted_iota(jnp.int32, (table_size, table_size), 0)
    col_index = lax.broadcasted_iota(jnp.int32, (table_size, table_size), 1)
    both = row_index & col_index
    parity = jnp.zeros((table_size, table_size), jnp.int32)
    for bit_level in range(table_size.bit_length() - 1):
        parity = parity ^ (both >> bit_level)
    return (1 - 2 * (parity & 1)).astype(F32)


def on_chip(*dims, dtype=F32):
    return pltpu.VMEM(dims, dtype)


def held(*values):
    return [pltpu.with_memory_space_constraint(value, pltpu.VMEM) for value in values]


LIMIT = pltpu.CompilerParams(vmem_limit_bytes=8 << 20)


def cost(flops, size):
    flops, size = flops // 1000, size // 1000
    return pl.CostEstimate(flops=flops, bytes_accessed=size, transcendentals=0)


def split(value):
    high = value.astype(BF16)
    return high, (value - high.astype(F32)).astype(BF16)


def dot(left, right):
    return jnp.dot(left, right, preferred_element_type=F32)


def block_factors(k, signs, pattern, row_blocks):
    signed = (2 * signs[k : k + 1, :] - 1).astype(F32)
    return [signed[:, j * BLK : (j + 1) * BLK] * pattern[k, j].astype(F32) for j in range(row_blocks)]


def block_sketch(block_ref, here, factors, table):
    total = block_ref[here, :BLK] * factors[0]
    for j in range(1, len(factors)):
        total = total + block_ref[here, j * BLK : (j + 1) * BLK] * factors[j]
    high, rest = split(total)
    low = (total - high.astype(F32) - rest.astype(F32)).astype(BF16)
    return dot(high, table) + dot(rest, table) + dot(low, table)


def first_sketch_kernel(pattern_ref, whole_ref, sign_ref, out_ref, held_ref, sems, signs, pattern):
    steps = sems.shape[0] - 2
    step = held_ref.shape[0] // steps
    copies = [
        pltpu.make_async_copy(pattern_ref, pattern, sems.at[steps]),
        pltpu.make_async_copy(sign_ref, signs, sems.at[steps + 1]),
    ]
    for i in range(steps):
        here = pl.ds(i * step, step)
        copies.append(pltpu.make_async_copy(whole_ref.at[here], held_ref.at[here], sems.at[i]))
    for copy in copies:
        copy.start()
    table = hadamard_table(BLK).astype(BF16)
    copies[0].wait()
    copies[1].wait()
    factors = block_factors(0, signs, pattern, held_ref.shape[1] // BLK)
    for i in range(steps):
        copies[2 + i].wait()
        here = slice(i * step, (i + 1) * step)
        out_ref[here, :] = block_sketch(held_ref, here, factors, table)


def first_sketch(unfolding, pattern_rows, sign_rows):
    rows, cols = unfolding.shape
    return pl.pallas_call(
        first_sketch_kernel,
        in_specs=[HBM] * 3,
        out_specs=[VMEM] * 2,
        out_shape=[on_chip(rows, BLK), on_chip(rows, cols)],
        scratch_shapes=[
            pltpu.SemaphoreType.DMA((10,)),
            pltpu.VMEM(sign_rows.shape, jnp.int32),
            pltpu.SMEM(pattern_rows.shape, jnp.int32),
        ],
        cost_estimate=cost(rows * cols * 2, rows * cols * 4),
        compiler_params=LIMIT,
        name="first_sketch",
    )(*[pltpu.with_memory_space_constraint(x, pltpu.HBM) for x in (pattern_rows, unfolding, sign_rows)])


def second_sketch_kernel(pattern_ref, sign_ref, block_ref, out_ref, high_ref, low_ref, sems, signs, pattern):
    copies = [
        pltpu.make_async_copy(pattern_ref, pattern, sems.at[0]),
        pltpu.make_async_copy(sign_ref, signs, sems.at[1]),
    ]
    for copy in copies:
        copy.start()
    table = hadamard_table(BLK).astype(BF16)
    step = 64
    for i in range(block_ref.shape[0] // step):
        here = slice(i * step, (i + 1) * step)
        high_ref[here, :], low_ref[here, :] = split(block_ref[here, :])
    for copy in copies:
        copy.wait()
    factors = block_factors(1, signs, pattern, block_ref.shape[1] // BLK)
    for i in range(block_ref.shape[0] // step):
        here = slice(i * step, (i + 1) * step)
        out_ref[here, :] = block_sketch(block_ref, here, factors, table)


def second_sketch(block, pattern_rows, sign_rows):
    rows, cols = block.shape
    return pl.pallas_call(
        second_sketch_kernel,
        in_specs=[HBM, HBM, VMEM],
        out_specs=[VMEM] * 3,
        out_shape=[on_chip(rows, BLK), on_chip(rows, cols, dtype=BF16), on_chip(rows, cols, dtype=BF16)],
        scratch_shapes=[
            pltpu.SemaphoreType.DMA((2,)),
            pltpu.VMEM(sign_rows.shape, jnp.int32),
            pltpu.SMEM(pattern_rows.shape, jnp.int32),
        ],
        cost_estimate=cost(rows * cols * 2, rows * cols * 4),
        compiler_params=LIMIT,
        name="second_sketch",
    )(*[pltpu.with_memory_space_constraint(x, pltpu.HBM) for x in (pattern_rows, sign_rows)], *held(block))


def first_gram_kernel(own_ref, got_ref, sketch_ref, turned_ref, parts_ref, gram_ref):
    sketch = own_ref[...] + got_ref[...]
    sketch_ref[...] = sketch
    turned = sketch.T
    turned_ref[...] = turned
    parts_ref[:BLK], parts_ref[BLK:] = split(turned)
    gram_ref[...] = jnp.dot(turned, sketch, precision=HIGHEST)


def first_gram(own, got):
    rows = own.shape[0]
    return pl.pallas_call(
        first_gram_kernel,
        in_specs=[VMEM] * 2,
        out_specs=[VMEM] * 4,
        out_shape=[
            on_chip(rows, BLK),
            on_chip(BLK, rows),
            on_chip(2 * BLK, rows, dtype=BF16),
            on_chip(BLK, BLK),
        ],
        cost_estimate=cost(rows * BLK * BLK * 12, rows * BLK * 8),
        compiler_params=LIMIT,
        name="first_gram",
    )(*held(own, got))


def second_gram_kernel(own_ref, got_ref, before_ref, gram_ref, sketch_ref, parts_ref, keep_ref, send_ref, packed):
    sketch = own_ref[...] + got_ref[...]
    sketch_ref[...] = sketch
    turned = sketch.T
    parts_ref[:BLK], parts_ref[BLK:] = split(turned)
    packed[:BLK] = gram_ref[...]
    packed[BLK : 2 * BLK] = jnp.dot(before_ref[...], sketch, precision=HIGHEST)
    packed[2 * BLK :] = jnp.dot(turned, sketch, precision=HIGHEST)
    half = keep_ref.shape[0]
    core = lax.axis_index("rows") & 1
    keep_ref[...] = packed[pl.ds(pl.multiple_of(core * half, half), half), :]
    send_ref[...] = packed[pl.ds(pl.multiple_of((1 - core) * half, half), half), :]


def second_gram(own, got, before, gram, after):
    rows = own.shape[0]
    half = (3 * BLK // 2, BLK)

    def body(*refs):
        second_gram_kernel(*refs[:4], *refs[-5:])

    return pl.pallas_call(
        body,
        in_specs=[VMEM] * (4 + len(after)),
        out_specs=[VMEM] * 4,
        out_shape=[
            on_chip(rows, BLK),
            on_chip(2 * BLK, rows, dtype=BF16),
            on_chip(*half),
            on_chip(*half),
        ],
        scratch_shapes=[pltpu.VMEM((3 * BLK, BLK), F32)],
        cost_estimate=cost(rows * BLK * BLK * 24, rows * BLK * 8),
        compiler_params=LIMIT,
        name="second_gram",
    )(*held(own, got, before, gram, *after))


def project_kernel(parts_ref, high_ref, low_ref, soon_0, soon_1, keep_1, give_0, keep_0):
    row = lax.axis_index("rows")
    core, right, far = row & 1, (row >> 1) & 1, row >> 3
    near = ((row >> 2) & 1) ^ lax.axis_index("cols")
    for flip, give, keep in ((1, (soon_0, soon_1), keep_1), (0, (give_0.at[0], give_0.at[1]), keep_0)):
        for side in range(2):
            for t in range(2):
                block = (far ^ core ^ 1 ^ side) * 4 + (right ^ flip) * 2 + (near ^ t)
                here = pl.ds(pl.multiple_of(block * 2 * BLK, 2 * BLK), 2 * BLK)
                both = dot(parts_ref[...], high_ref[:, here])
                total = both[:BLK] + both[BLK:] + dot(parts_ref[:BLK, :], low_ref[:, here])
                if side == 0:
                    give[t][...] = total
                else:
                    keep[t] = total


def project(parts, high, low, after=()):
    rows, cols = high.shape

    def body(*refs):
        project_kernel(*refs[:3], *refs[-5:])

    return pl.pallas_call(
        body,
        in_specs=[VMEM] * (3 + len(after)),
        out_specs=[VMEM] * 5,
        out_shape=[on_chip(BLK, 2 * BLK)] * 2 + [on_chip(2, BLK, 2 * BLK)] * 3,
        cost_estimate=cost(rows * cols * BLK * 6, rows * cols * 4),
        compiler_params=LIMIT,
        name="project",
    )(*held(parts, high, low, *after))


def joined_kernel(keep_ref, got_0, got_1, out_ref):
    out_ref[0] = keep_ref[0] + got_0[...]
    out_ref[1] = keep_ref[1] + got_1[...]


def joined(keep, got, after):
    def body(*refs):
        joined_kernel(*refs[:3], refs[-1])

    return pl.pallas_call(
        body,
        in_specs=[VMEM] * (3 + len(after)),
        out_specs=VMEM,
        out_shape=on_chip(*keep.shape),
        cost_estimate=cost(0, keep.size * 4),
        compiler_params=LIMIT,
        name="joined",
    )(*held(keep, *got, *after))


def add_parts_kernel(terms, outs):
    for i, out in enumerate(outs):
        here = slice(None) if len(outs) == 1 else i
        total = terms[0][here]
        for term in terms[1:]:
            total = total + term[here]
        out[...] = total


def add_parts(terms, parts, after=(), hint=0):
    dims = terms[0].shape
    size = math.prod(dims)
    count = len(terms)

    def body(*refs):
        add_parts_kernel(refs[:count], refs[-parts:])

    return pl.pallas_call(
        body,
        in_specs=[VMEM] * (count + len(after)),
        out_specs=[VMEM] * parts,
        out_shape=[on_chip(*(dims if parts == 1 else dims[1:]))] * parts,
        cost_estimate=cost(size + hint, size),
        compiler_params=LIMIT,
        name="add_parts",
    )(*held(*terms, *after))


def pieces_kernel(refs, outs):
    count = len(refs) // 2
    for i, out in enumerate(outs):
        for h in range(2):
            terms = [ref[i] for ref in refs[h * count : (h + 1) * count]]
            out[h * BLK : (h + 1) * BLK] = sum(terms[1:], terms[0])


def piece_sums(first, second, after):
    terms = (*first, *second)
    count = len(terms)

    def body(*refs):
        pieces_kernel(refs[:count], refs[-2:])

    return pl.pallas_call(
        body,
        in_specs=[VMEM] * (count + len(after)),
        out_specs=[VMEM] * 2,
        out_shape=[on_chip(2 * BLK, 2 * BLK)] * 2,
        cost_estimate=cost(8 * BLK * BLK, 96 * BLK * BLK),
        compiler_params=LIMIT,
        name="piece_sums",
    )(*held(*terms, *after))


def factor_panel(parts, start):
    diagonal = parts[0][:, start : start + PANEL]
    columns = [jnp.broadcast_to(diagonal[:, k : k + 1], (PANEL, BLK)) for k in range(PANEL)]
    rows = lax.broadcasted_iota(jnp.int32, (PANEL, BLK), 0)
    pivots = jnp.ones((PANEL, BLK), F32)
    for j in range(PANEL):
        pivot = jnp.broadcast_to(columns[j][j : j + 1, :], (PANEL, BLK))
        multiplier = jnp.where(rows > j, columns[j] / pivot, 0.0)
        for k in range(j + 1, PANEL):
            columns[k] = columns[k] - multiplier * columns[k][j : j + 1, :]
        parts = [part - multiplier * part[j : j + 1, :] for part in parts]
        pivots = jnp.where(rows == j, pivot, pivots)
    scale = lax.rsqrt(pivots)
    return [part * scale for part in parts]


def factor_block(work):
    for panel in range(BLK // PANEL):
        start = panel * PANEL
        stop = start + PANEL
        parts = [work[start:stop, c * BLK : (c + 1) * BLK] for c in range(3)]
        parts = factor_panel(parts, start)
        for c in range(3):
            work[start:stop, c * BLK : (c + 1) * BLK] = parts[c]
        if stop < BLK:
            left, whole = parts[0].T, jnp.concatenate(parts, 1)
            after = min(stop + PANEL, BLK)
            work[stop:after, :] = work[stop:after, :] - jnp.dot(left[stop:after], whole, precision=HIGHEST)
            if after < BLK:
                work[after:, :] = work[after:, :] - jnp.dot(left[after:], whole, precision=HIGHEST)


def factor_kernel(total_rows, own_ref, got_ref, out_ref, work, packed):
    half = own_ref.shape[0]
    core = lax.axis_index("rows") & 1
    packed[pl.ds(pl.multiple_of(core * half, half), half), :] = own_ref[...]
    packed[pl.ds(pl.multiple_of((1 - core) * half, half), half), :] = got_ref[...]
    row = lax.broadcasted_iota(jnp.int32, (BLK, BLK), 0)
    col = lax.broadcasted_iota(jnp.int32, (BLK, BLK), 1)
    eye = (row == col).astype(F32)
    work[:, :BLK] = packed[:BLK] + float(total_rows) * eye
    work[:, BLK : 2 * BLK] = packed[BLK : 2 * BLK]
    work[:, 2 * BLK :] = eye
    factor_block(work)
    out_ref[:BLK, :BLK] = work[:, 2 * BLK :]
    out_ref[:BLK, BLK:] = jnp.zeros((BLK, BLK), F32)
    above = work[:, BLK : 2 * BLK]
    product = jnp.dot(above.T, work[:, BLK:], precision=HIGHEST)
    work[:, :BLK] = packed[2 * BLK :] + float(total_rows) * eye - product[:, :BLK]
    work[:, BLK : 2 * BLK] = -product[:, BLK:]
    work[:, 2 * BLK :] = eye
    factor_block(work)
    out_ref[BLK:, :] = work[:, BLK:]


def inverse_factor(own, got, total_rows):
    def body(*refs):
        factor_kernel(total_rows, *refs)

    return pl.pallas_call(
        body,
        in_specs=[VMEM] * 2,
        out_specs=VMEM,
        out_shape=on_chip(RANK, RANK),
        scratch_shapes=[pltpu.VMEM((BLK, 3 * BLK), F32), pltpu.VMEM((3 * BLK, BLK), F32)],
        cost_estimate=cost(1000000000000, RANK * RANK * 8),
        compiler_params=LIMIT,
        name="inverse_factor",
    )(*held(own, got))


def core_kernel(scale, first_ref, second_ref, inverse_ref, out_ref):
    t_high, t_low = split(inverse_ref[...].T)
    s_high, s_low = split(jnp.concatenate([first_ref[...], second_ref[...]], 1))
    total = dot(s_high, t_high) + dot(s_high, t_low) + dot(s_low, t_high)
    out_ref[...] = total * scale


def scaled_core(first, second, inverse, scale):
    rows = first.shape[0]

    def body(*refs):
        core_kernel(scale, *refs)

    return pl.pallas_call(
        body,
        in_specs=[VMEM] * 3,
        out_specs=VMEM,
        out_shape=jax.ShapeDtypeStruct((rows, RANK), F32),
        cost_estimate=cost(rows * RANK * RANK * 6, rows * RANK * 8),
        compiler_params=LIMIT,
        name="scaled_core",
    )(*held(first, second, inverse))


def remainder_kernel(inverse_ref, p0, p1, o0, o1, o2, o3, work):
    work[...] = jnp.dot(inverse_ref[...], p0[...] + p1[...], precision=HIGHEST)
    device = lax.axis_index("rows")
    for m, out in enumerate((o0, o1, o2, o3)):
        for t in range(4):
            rank_block = (4 * t + m) ^ device
            out[t] = work[pl.ds(pl.multiple_of(rank_block * 16, 16), 16), :]


def remainder_pieces(inverse, pieces):
    return pl.pallas_call(
        remainder_kernel,
        in_specs=[VMEM] * 3,
        out_specs=[VMEM] * 4,
        out_shape=[on_chip(4, 16, 2 * BLK)] * 4,
        scratch_shapes=[pltpu.VMEM((RANK, 2 * BLK), F32)],
        cost_estimate=cost(RANK * RANK * BLK * 24, RANK * BLK * 16),
        compiler_params=LIMIT,
        name="remainder_pieces",
    )(*held(inverse, *pieces))


def collect_kernel(r0, r1, r2, r3, o0, o1, o2, o3):
    for t, out in enumerate((o0, o1, o2, o3)):
        out[0] = r0[t] + r1[t]
        out[1] = r2[t] + r3[t]


def collect(firsts):
    return pl.pallas_call(
        collect_kernel,
        in_specs=[VMEM] * 4,
        out_specs=[VMEM] * 4,
        out_shape=[on_chip(2, 16, 2 * BLK)] * 4,
        cost_estimate=cost(0, 16 * BLK * 64),
        compiler_params=LIMIT,
        name="collect",
    )(*held(*firsts))


def arrange_kernel(p0, p1, p2, p3, out_ref, work):
    row = lax.axis_index("rows")
    right, deep, y = (row >> 1) & 1, row >> 2, lax.axis_index("cols")
    for t, piece in enumerate((p0, p1, p2, p3)):
        there = deep ^ t
        for m in range(2):
            work[((there & 1) ^ y) * 4 + (there >> 1) * 2 + (right ^ m)] = piece[m]
    for mode in range(MODE):
        out_ref[:, mode, :] = work[mode]


def arrange(pieces):
    out = pl.pallas_call(
        arrange_kernel,
        in_specs=[VMEM] * 4,
        out_specs=VMEM,
        out_shape=jax.ShapeDtypeStruct((16, MODE, 2 * BLK), F32),
        scratch_shapes=[pltpu.VMEM((MODE, 16, 2 * BLK), F32)],
        cost_estimate=cost(0, 16 * BLK * 64),
        compiler_params=LIMIT,
        name="arrange",
    )(*held(*pieces))
    return out.reshape(16 * MODE, 2 * BLK)


def rows_permute(value, mask):
    size = lax.axis_size("rows")
    return lax.ppermute(value, "rows", [(i, i ^ mask) for i in range(size)])


def local(unfolding, pattern, sign_bits):
    total_rows = unfolding.shape[0] * lax.axis_size("rows")
    swap = [(0, 1), (1, 0)]
    pattern_rows, sign_rows = pattern.T, sign_bits.T
    own_0, block = first_sketch(unfolding, pattern_rows, sign_rows)
    got_0 = lax.ppermute(own_0, "cols", swap)
    own_1, high, low = second_sketch(block, pattern_rows, sign_rows)
    got_1 = lax.ppermute(own_1, "cols", swap)
    first, turned, parts, gram = first_gram(own_0, got_0)
    *give, keep, give_0, keep_0 = project(parts, high, low)
    send_0 = joined(keep, [rows_permute(g, 1) for g in give], ())
    second, parts, gram_keep, gram_send = second_gram(own_1, got_1, turned, gram, (keep_0,))
    gram, = add_parts((gram_keep, rows_permute(gram_send, 1)), 1)
    *give, keep, give_1, keep_1 = project(parts, high, low, (send_0,))
    got_0 = rows_permute(send_0, 2)
    send_1 = joined(keep, [rows_permute(g, 1) for g in give], (gram,))
    core_got, last_got = (rows_permute(give_0, 1), rows_permute(give_1, 1)), rows_permute(send_1, 2)
    gram, = add_parts((gram, rows_permute(gram, 4)), 1, (got_0,))
    gram, = add_parts((gram, rows_permute(gram, 8)), 1, hint=1000000000000)
    pieces = piece_sums((keep_0, core_got[0], got_0), (keep_1, core_got[1], last_got), (gram,))
    gram, = add_parts((gram, rows_permute(gram, 2)), 1)
    inverse = inverse_factor(gram, rows_permute(gram, 1), total_rows)
    gathered = []
    for k in range(2):
        pairs = []
        for i in range(16):
            for y in range(2):
                to = i ^ (k << 2) ^ ((i & 1) << 3)
                pairs.append((2 * i + y, 2 * to + (y ^ ((to >> 2) & 1))))
        gathered.append(lax.ppermute(pieces[k], ("rows", "cols"), pairs))
    parts = remainder_pieces(inverse, gathered)
    core_scaled = scaled_core(first, second, inverse, math.sqrt(total_rows))
    sums = collect([parts[0]] + [rows_permute(parts[m], m) for m in (1, 2, 3)])
    return core_scaled, arrange([sums[0]] + [rows_permute(sums[t], 4 * t) for t in (1, 2, 3)])


def sketch_matrix(pattern, sign_bits, block_size):
    blocks = sign_bits.shape[1]
    rows_here = sign_bits.shape[0]
    factor = jnp.repeat(pattern, block_size, axis=0) * (2 * sign_bits - 1)
    tiled_table = jnp.tile(hadamard_table(block_size), (rows_here // block_size, 1))
    expanded = factor.astype(F32)[:, :, None] * tiled_table[:, None, :]
    return expanded.reshape(rows_here, blocks * block_size)


def inner_rows(left_side, right_side):
    return lax.dot_general(left_side, right_side, (((0,), (0,)), ((), ())), precision=HIGHEST)


def local_any(unfolding, pattern, sign_bits):
    sketch_map = sketch_matrix(pattern, sign_bits, BLK)
    row_devices = lax.axis_size("rows")
    col_devices = lax.axis_size("cols")
    total_rows = unfolding.shape[0] * row_devices
    sketch = lax.psum(jnp.dot(unfolding, sketch_map, precision=HIGHEST), "cols")
    gram_matrix = lax.psum(inner_rows(sketch, sketch), "rows")
    gram_matrix = gram_matrix + float(total_rows) * jnp.eye(RANK, dtype=F32)
    lower_factor = jnp.linalg.cholesky(gram_matrix)
    basis_rows = lax.linalg.triangular_solve(lower_factor, sketch, left_side=False, lower=True, transpose_a=True)
    mode_local = MODE // col_devices
    rest_cols = unfolding.shape[1] // mode_local
    rank_share = RANK // row_devices
    reduced = lax.psum_scatter(inner_rows(basis_rows, unfolding), "rows", scatter_dimension=0, tiled=True)
    grouped = reduced.reshape(rank_share, mode_local, rest_cols)
    regrouped = lax.all_to_all(grouped, "cols", split_axis=2, concat_axis=1, tiled=True)
    return basis_rows * math.sqrt(total_rows), regrouped.reshape(rank_share * MODE, regrouped.shape[2])


def solution(mesh):
    in_specs = (P("rows", "cols"), P("cols", None), P("cols", None))
    out_specs = (P("rows", None), P("rows", "cols"))
    body = local if (mesh.shape["rows"], mesh.shape["cols"]) == (16, 2) else local_any
    return jax.shard_map(body, mesh=mesh, in_specs=in_specs, out_specs=out_specs, check_vma=False)
```

```python
import math

import jax
import jax.numpy as jnp
from jax import lax
from jax.experimental import pallas as pl
from jax.experimental.pallas import tpu as pltpu
from jax.sharding import PartitionSpec as P

RANK = 256
BLK = 128
MODE = 8
PANEL = 16
HIGHEST = lax.Precision.HIGHEST
F32 = jnp.float32
BF16 = jnp.bfloat16
VMEM = pl.BlockSpec(memory_space=pltpu.VMEM)
HBM = pl.BlockSpec(memory_space=pltpu.HBM)


def hadamard_table(table_size):
    row_index = lax.broadcasted_iota(jnp.int32, (table_size, table_size), 0)
    col_index = lax.broadcasted_iota(jnp.int32, (table_size, table_size), 1)
    both = row_index & col_index
    parity = jnp.zeros((table_size, table_size), jnp.int32)
    for bit_level in range(table_size.bit_length() - 1):
        parity = parity ^ (both >> bit_level)
    return (1 - 2 * (parity & 1)).astype(F32)


def on_chip(*dims, dtype=F32):
    return pltpu.VMEM(dims, dtype)


def held(*values):
    return [pltpu.with_memory_space_constraint(value, pltpu.VMEM) for value in values]


LIMIT = pltpu.CompilerParams(vmem_limit_bytes=8 << 20)


def cost(flops, size):
    flops, size = flops // 1000, size // 1000
    return pl.CostEstimate(flops=flops, bytes_accessed=size, transcendentals=0)


def split(value):
    high = value.astype(BF16)
    return high, (value - high.astype(F32)).astype(BF16)


def dot(left, right):
    return jnp.dot(left, right, preferred_element_type=F32)


def block_factors(k, signs, pattern, row_blocks):
    signed = (2 * signs[k : k + 1, :] - 1).astype(F32)
    return [signed[:, j * BLK : (j + 1) * BLK] * pattern[k, j].astype(F32) for j in range(row_blocks)]


def block_sketch(block_ref, here, factors, table):
    total = block_ref[here, :BLK] * factors[0]
    for j in range(1, len(factors)):
        total = total + block_ref[here, j * BLK : (j + 1) * BLK] * factors[j]
    high, rest = split(total)
    low = (total - high.astype(F32) - rest.astype(F32)).astype(BF16)
    return dot(high, table) + dot(rest, table) + dot(low, table)


def first_sketch_kernel(pattern_ref, whole_ref, sign_ref, out_ref, held_ref, sems, signs, pattern):
    steps = sems.shape[0] - 2
    step = held_ref.shape[0] // steps
    copies = [
        pltpu.make_async_copy(pattern_ref, pattern, sems.at[steps]),
        pltpu.make_async_copy(sign_ref, signs, sems.at[steps + 1]),
    ]
    for i in range(steps):
        here = pl.ds(i * step, step)
        copies.append(pltpu.make_async_copy(whole_ref.at[here], held_ref.at[here], sems.at[i]))
    for copy in copies:
        copy.start()
    table = hadamard_table(BLK).astype(BF16)
    copies[0].wait()
    copies[1].wait()
    factors = block_factors(0, signs, pattern, held_ref.shape[1] // BLK)
    for i in range(steps):
        copies[2 + i].wait()
        here = slice(i * step, (i + 1) * step)
        out_ref[here, :] = block_sketch(held_ref, here, factors, table)


def first_sketch(unfolding, pattern_rows, sign_rows):
    rows, cols = unfolding.shape
    return pl.pallas_call(
        first_sketch_kernel,
        in_specs=[HBM] * 3,
        out_specs=[VMEM] * 2,
        out_shape=[on_chip(rows, BLK), on_chip(rows, cols)],
        scratch_shapes=[
            pltpu.SemaphoreType.DMA((10,)),
            pltpu.VMEM(sign_rows.shape, jnp.int32),
            pltpu.SMEM(pattern_rows.shape, jnp.int32),
        ],
        cost_estimate=cost(rows * cols * 2, rows * cols * 4),
        compiler_params=LIMIT,
        name="first_sketch",
    )(*[pltpu.with_memory_space_constraint(x, pltpu.HBM) for x in (pattern_rows, unfolding, sign_rows)])


def second_sketch_kernel(pattern_ref, sign_ref, block_ref, out_ref, high_ref, low_ref, sems, signs, pattern):
    copies = [
        pltpu.make_async_copy(pattern_ref, pattern, sems.at[0]),
        pltpu.make_async_copy(sign_ref, signs, sems.at[1]),
    ]
    for copy in copies:
        copy.start()
    table = hadamard_table(BLK).astype(BF16)
    step = 64
    for i in range(block_ref.shape[0] // step):
        here = slice(i * step, (i + 1) * step)
        high_ref[here, :], low_ref[here, :] = split(block_ref[here, :])
    for copy in copies:
        copy.wait()
    factors = block_factors(1, signs, pattern, block_ref.shape[1] // BLK)
    for i in range(block_ref.shape[0] // step):
        here = slice(i * step, (i + 1) * step)
        out_ref[here, :] = block_sketch(block_ref, here, factors, table)


def second_sketch(block, pattern_rows, sign_rows):
    rows, cols = block.shape
    return pl.pallas_call(
        second_sketch_kernel,
        in_specs=[HBM, HBM, VMEM],
        out_specs=[VMEM] * 3,
        out_shape=[on_chip(rows, BLK), on_chip(rows, cols, dtype=BF16), on_chip(rows, cols, dtype=BF16)],
        scratch_shapes=[
            pltpu.SemaphoreType.DMA((2,)),
            pltpu.VMEM(sign_rows.shape, jnp.int32),
            pltpu.SMEM(pattern_rows.shape, jnp.int32),
        ],
        cost_estimate=cost(rows * cols * 2, rows * cols * 4),
        compiler_params=LIMIT,
        name="second_sketch",
    )(*[pltpu.with_memory_space_constraint(x, pltpu.HBM) for x in (pattern_rows, sign_rows)], *held(block))


def first_gram_kernel(own_ref, got_ref, sketch_ref, turned_ref, parts_ref, gram_ref):
    sketch = own_ref[...] + got_ref[...]
    sketch_ref[...] = sketch
    turned = sketch.T
    turned_ref[...] = turned
    parts_ref[:BLK], parts_ref[BLK:] = split(turned)
    gram_ref[...] = jnp.dot(turned, sketch, precision=HIGHEST)


def first_gram(own, got):
    rows = own.shape[0]
    return pl.pallas_call(
        first_gram_kernel,
        in_specs=[VMEM] * 2,
        out_specs=[VMEM] * 4,
        out_shape=[
            on_chip(rows, BLK),
            on_chip(BLK, rows),
            on_chip(2 * BLK, rows, dtype=BF16),
            on_chip(BLK, BLK),
        ],
        cost_estimate=cost(rows * BLK * BLK * 12, rows * BLK * 8),
        compiler_params=LIMIT,
        name="first_gram",
    )(*held(own, got))


def second_gram_kernel(own_ref, got_ref, before_ref, gram_ref, sketch_ref, parts_ref, keep_ref, send_ref, packed):
    sketch = own_ref[...] + got_ref[...]
    sketch_ref[...] = sketch
    turned = sketch.T
    parts_ref[:BLK], parts_ref[BLK:] = split(turned)
    packed[:BLK] = gram_ref[...]
    packed[BLK : 2 * BLK] = jnp.dot(before_ref[...], sketch, precision=HIGHEST)
    packed[2 * BLK :] = jnp.dot(turned, sketch, precision=HIGHEST)
    half = keep_ref.shape[0]
    core = lax.axis_index("rows") & 1
    keep_ref[...] = packed[pl.ds(pl.multiple_of(core * half, half), half), :]
    send_ref[...] = packed[pl.ds(pl.multiple_of((1 - core) * half, half), half), :]


def second_gram(own, got, before, gram, after):
    rows = own.shape[0]
    half = (3 * BLK // 2, BLK)

    def body(*refs):
        second_gram_kernel(*refs[:4], *refs[-5:])

    return pl.pallas_call(
        body,
        in_specs=[VMEM] * (4 + len(after)),
        out_specs=[VMEM] * 4,
        out_shape=[
            on_chip(rows, BLK),
            on_chip(2 * BLK, rows, dtype=BF16),
            on_chip(*half),
            on_chip(*half),
        ],
        scratch_shapes=[pltpu.VMEM((3 * BLK, BLK), F32)],
        cost_estimate=cost(rows * BLK * BLK * 24, rows * BLK * 8),
        compiler_params=LIMIT,
        name="second_gram",
    )(*held(own, got, before, gram, *after))


def project_kernel(parts_ref, high_ref, low_ref, soon_0, soon_1, keep_1, give_0, keep_0):
    row = lax.axis_index("rows")
    core, right, far = row & 1, (row >> 1) & 1, row >> 3
    near = ((row >> 2) & 1) ^ lax.axis_index("cols")
    for flip, give, keep in ((1, (soon_0, soon_1), keep_1), (0, (give_0.at[0], give_0.at[1]), keep_0)):
        for side in range(2):
            for t in range(2):
                block = (far ^ core ^ 1 ^ side) * 4 + (right ^ flip) * 2 + (near ^ t)
                here = pl.ds(pl.multiple_of(block * 2 * BLK, 2 * BLK), 2 * BLK)
                both = dot(parts_ref[...], high_ref[:, here])
                total = both[:BLK] + both[BLK:] + dot(parts_ref[:BLK, :], low_ref[:, here])
                if side == 0:
                    give[t][...] = total
                else:
                    keep[t] = total


def project(parts, high, low, after=()):
    rows, cols = high.shape

    def body(*refs):
        project_kernel(*refs[:3], *refs[-5:])

    return pl.pallas_call(
        body,
        in_specs=[VMEM] * (3 + len(after)),
        out_specs=[VMEM] * 5,
        out_shape=[on_chip(BLK, 2 * BLK)] * 2 + [on_chip(2, BLK, 2 * BLK)] * 3,
        cost_estimate=cost(rows * cols * BLK * 6, rows * cols * 4),
        compiler_params=LIMIT,
        name="project",
    )(*held(parts, high, low, *after))


def joined_kernel(keep_ref, got_0, got_1, out_ref):
    out_ref[0] = keep_ref[0] + got_0[...]
    out_ref[1] = keep_ref[1] + got_1[...]


def joined(keep, got, after):
    def body(*refs):
        joined_kernel(*refs[:3], refs[-1])

    return pl.pallas_call(
        body,
        in_specs=[VMEM] * (3 + len(after)),
        out_specs=VMEM,
        out_shape=on_chip(*keep.shape),
        cost_estimate=cost(0, keep.size * 4),
        compiler_params=LIMIT,
        name="joined",
    )(*held(keep, *got, *after))


def add_parts_kernel(terms, outs):
    for i, out in enumerate(outs):
        here = slice(None) if len(outs) == 1 else i
        total = terms[0][here]
        for term in terms[1:]:
            total = total + term[here]
        out[...] = total


def add_parts(terms, parts, after=(), hint=0):
    dims = terms[0].shape
    size = math.prod(dims)
    count = len(terms)

    def body(*refs):
        add_parts_kernel(refs[:count], refs[-parts:])

    return pl.pallas_call(
        body,
        in_specs=[VMEM] * (count + len(after)),
        out_specs=[VMEM] * parts,
        out_shape=[on_chip(*(dims if parts == 1 else dims[1:]))] * parts,
        cost_estimate=cost(size + hint, size),
        compiler_params=LIMIT,
        name="add_parts",
    )(*held(*terms, *after))


def pieces_kernel(refs, outs):
    count = len(refs) // 2
    for i, out in enumerate(outs):
        for h in range(2):
            terms = [ref[i] for ref in refs[h * count : (h + 1) * count]]
            out[h * BLK : (h + 1) * BLK] = sum(terms[1:], terms[0])


def piece_sums(first, second, after):
    terms = (*first, *second)
    count = len(terms)

    def body(*refs):
        pieces_kernel(refs[:count], refs[-2:])

    return pl.pallas_call(
        body,
        in_specs=[VMEM] * (count + len(after)),
        out_specs=[VMEM] * 2,
        out_shape=[on_chip(2 * BLK, 2 * BLK)] * 2,
        cost_estimate=cost(8 * BLK * BLK, 96 * BLK * BLK),
        compiler_params=LIMIT,
        name="piece_sums",
    )(*held(*terms, *after))


def factor_panel(parts, start):
    diagonal = parts[0][:, start : start + PANEL]
    columns = [jnp.broadcast_to(diagonal[:, k : k + 1], (PANEL, BLK)) for k in range(PANEL)]
    rows = lax.broadcasted_iota(jnp.int32, (PANEL, BLK), 0)
    pivots = jnp.ones((PANEL, BLK), F32)
    for j in range(PANEL):
        pivot = jnp.broadcast_to(columns[j][j : j + 1, :], (PANEL, BLK))
        multiplier = jnp.where(rows > j, columns[j] / pivot, 0.0)
        for k in range(j + 1, PANEL):
            columns[k] = columns[k] - multiplier * columns[k][j : j + 1, :]
        parts = [part - multiplier * part[j : j + 1, :] for part in parts]
        pivots = jnp.where(rows == j, pivot, pivots)
    scale = lax.rsqrt(pivots)
    return [part * scale for part in parts]


def factor_block(work):
    for panel in range(BLK // PANEL):
        start = panel * PANEL
        stop = start + PANEL
        parts = [work[start:stop, c * BLK : (c + 1) * BLK] for c in range(3)]
        parts = factor_panel(parts, start)
        for c in range(3):
            work[start:stop, c * BLK : (c + 1) * BLK] = parts[c]
        if stop < BLK:
            left, whole = parts[0].T, jnp.concatenate(parts, 1)
            after = min(stop + PANEL, BLK)
            work[stop:after, :] = work[stop:after, :] - jnp.dot(left[stop:after], whole, precision=HIGHEST)
            if after < BLK:
                work[after:, :] = work[after:, :] - jnp.dot(left[after:], whole, precision=HIGHEST)


def factor_kernel(total_rows, own_ref, got_ref, out_ref, work, packed):
    half = own_ref.shape[0]
    core = lax.axis_index("rows") & 1
    packed[pl.ds(pl.multiple_of(core * half, half), half), :] = own_ref[...]
    packed[pl.ds(pl.multiple_of((1 - core) * half, half), half), :] = got_ref[...]
    row = lax.broadcasted_iota(jnp.int32, (BLK, BLK), 0)
    col = lax.broadcasted_iota(jnp.int32, (BLK, BLK), 1)
    eye = (row == col).astype(F32)
    work[:, :BLK] = packed[:BLK] + float(total_rows) * eye
    work[:, BLK : 2 * BLK] = packed[BLK : 2 * BLK]
    work[:, 2 * BLK :] = eye
    factor_block(work)
    out_ref[:BLK, :BLK] = work[:, 2 * BLK :]
    out_ref[:BLK, BLK:] = jnp.zeros((BLK, BLK), F32)
    above = work[:, BLK : 2 * BLK]
    product = jnp.dot(above.T, work[:, BLK:], precision=HIGHEST)
    work[:, :BLK] = packed[2 * BLK :] + float(total_rows) * eye - product[:, :BLK]
    work[:, BLK : 2 * BLK] = -product[:, BLK:]
    work[:, 2 * BLK :] = eye
    factor_block(work)
    out_ref[BLK:, :] = work[:, BLK:]


def inverse_factor(own, got, total_rows):
    def body(*refs):
        factor_kernel(total_rows, *refs)

    return pl.pallas_call(
        body,
        in_specs=[VMEM] * 2,
        out_specs=VMEM,
        out_shape=on_chip(RANK, RANK),
        scratch_shapes=[pltpu.VMEM((BLK, 3 * BLK), F32), pltpu.VMEM((3 * BLK, BLK), F32)],
        cost_estimate=cost(1000000000000, RANK * RANK * 8),
        compiler_params=LIMIT,
        name="inverse_factor",
    )(*held(own, got))


def core_kernel(scale, first_ref, second_ref, inverse_ref, out_ref):
    t_high, t_low = split(inverse_ref[...].T)
    s_high, s_low = split(jnp.concatenate([first_ref[...], second_ref[...]], 1))
    total = dot(s_high, t_high) + dot(s_high, t_low) + dot(s_low, t_high)
    out_ref[...] = total * scale


def scaled_core(first, second, inverse, scale):
    rows = first.shape[0]

    def body(*refs):
        core_kernel(scale, *refs)

    return pl.pallas_call(
        body,
        in_specs=[VMEM] * 3,
        out_specs=VMEM,
        out_shape=jax.ShapeDtypeStruct((rows, RANK), F32),
        cost_estimate=cost(rows * RANK * RANK * 6, rows * RANK * 8),
        compiler_params=LIMIT,
        name="scaled_core",
    )(*held(first, second, inverse))


def remainder_kernel(inverse_ref, p0, p1, o0, o1, o2, o3, work):
    work[...] = jnp.dot(inverse_ref[...], p0[...] + p1[...], precision=HIGHEST)
    row = lax.axis_index("rows")
    for m, out in enumerate((o0, o1, o2, o3)):
        to = (row & 3) ^ m
        for j in range(4):
            deep = (row >> 2) ^ (((to & 1) << 1) | (j >> 1))
            rank_block = (deep << 2) | (to ^ (j & 1))
            out[j] = work[pl.ds(pl.multiple_of(rank_block * 16, 16), 16), :]


def remainder_pieces(inverse, pieces):
    return pl.pallas_call(
        remainder_kernel,
        in_specs=[VMEM] * 3,
        out_specs=[VMEM] * 4,
        out_shape=[on_chip(4, 16, 2 * BLK)] * 4,
        scratch_shapes=[pltpu.VMEM((RANK, 2 * BLK), F32)],
        cost_estimate=cost(RANK * RANK * BLK * 24, RANK * BLK * 16),
        compiler_params=LIMIT,
        name="remainder_pieces",
    )(*held(inverse, *pieces))


def collect_kernel(r0, r1, r2, r3, o0, o1):
    for t, out in enumerate((o0, o1)):
        for j in range(2):
            out[j, 0] = r0[2 * t + j] + r1[2 * t + j]
            out[j, 1] = r2[2 * t + j] + r3[2 * t + j]


def collect(firsts):
    return pl.pallas_call(
        collect_kernel,
        in_specs=[VMEM] * 4,
        out_specs=[VMEM] * 2,
        out_shape=[on_chip(2, 2, 16, 2 * BLK)] * 2,
        cost_estimate=cost(0, 16 * BLK * 64),
        compiler_params=LIMIT,
        name="collect",
    )(*held(*firsts))


def share_kernel(p0, p1, out):
    out[0] = p0[1]
    out[1] = p1[1]


def share(pieces):
    return pl.pallas_call(
        share_kernel,
        in_specs=[VMEM] * 2,
        out_specs=VMEM,
        out_shape=on_chip(2, 2, 16, 2 * BLK),
        cost_estimate=cost(0, 16 * BLK * 64),
        compiler_params=LIMIT,
        name="share",
    )(*held(*pieces))


def arrange_kernel(p0, p1, shared, out_ref, work):
    row = lax.axis_index("rows")
    core, right, deep, y = row & 1, (row >> 1) & 1, row >> 2, lax.axis_index("cols")
    for t, ours in enumerate((p0, p1)):
        for other in range(2):
            there = deep ^ (((core ^ other) << 1) | t)
            piece = shared.at[t] if other else ours.at[0]
            for m in range(2):
                work[((there & 1) ^ y) * 4 + (there >> 1) * 2 + (right ^ m)] = piece[m]
    for mode in range(MODE):
        out_ref[:, mode, :] = work[mode]


def arrange(pieces):
    out = pl.pallas_call(
        arrange_kernel,
        in_specs=[VMEM] * 3,
        out_specs=VMEM,
        out_shape=jax.ShapeDtypeStruct((16, MODE, 2 * BLK), F32),
        scratch_shapes=[pltpu.VMEM((MODE, 16, 2 * BLK), F32)],
        cost_estimate=cost(0, 16 * BLK * 64),
        compiler_params=LIMIT,
        name="arrange",
    )(*held(*pieces))
    return out.reshape(16 * MODE, 2 * BLK)


def rows_permute(value, mask):
    size = lax.axis_size("rows")
    return lax.ppermute(value, "rows", [(i, i ^ mask) for i in range(size)])


def local(unfolding, pattern, sign_bits):
    total_rows = unfolding.shape[0] * lax.axis_size("rows")
    swap = [(0, 1), (1, 0)]
    pattern_rows, sign_rows = pattern.T, sign_bits.T
    own_0, block = first_sketch(unfolding, pattern_rows, sign_rows)
    got_0 = lax.ppermute(own_0, "cols", swap)
    own_1, high, low = second_sketch(block, pattern_rows, sign_rows)
    got_1 = lax.ppermute(own_1, "cols", swap)
    first, turned, parts, gram = first_gram(own_0, got_0)
    *give, keep, give_0, keep_0 = project(parts, high, low)
    send_0 = joined(keep, [rows_permute(g, 1) for g in give], ())
    second, parts, gram_keep, gram_send = second_gram(own_1, got_1, turned, gram, (keep_0,))
    gram, = add_parts((gram_keep, rows_permute(gram_send, 1)), 1)
    *give, keep, give_1, keep_1 = project(parts, high, low, (send_0,))
    got_0 = rows_permute(send_0, 2)
    send_1 = joined(keep, [rows_permute(g, 1) for g in give], (gram,))
    core_got, last_got = (rows_permute(give_0, 1), rows_permute(give_1, 1)), rows_permute(send_1, 2)
    gram, = add_parts((gram, rows_permute(gram, 4)), 1, (got_0,))
    gram, = add_parts((gram, rows_permute(gram, 8)), 1, hint=1000000000000)
    pieces = piece_sums((keep_0, core_got[0], got_0), (keep_1, core_got[1], last_got), (gram,))
    gram, = add_parts((gram, rows_permute(gram, 2)), 1)
    inverse = inverse_factor(gram, rows_permute(gram, 1), total_rows)
    gathered = []
    for k in range(2):
        pairs = []
        for i in range(16):
            for y in range(2):
                to = i ^ (k << 2) ^ ((i & 1) << 3)
                pairs.append((2 * i + y, 2 * to + (y ^ ((to >> 2) & 1))))
        gathered.append(lax.ppermute(pieces[k], ("rows", "cols"), pairs))
    parts = remainder_pieces(inverse, gathered)
    core_scaled = scaled_core(first, second, inverse, math.sqrt(total_rows))
    sums = collect([parts[0]] + [rows_permute(parts[m], m) for m in (1, 2, 3)])
    passed = []
    for t in range(2):
        pairs = [(i, i ^ (t << 2) ^ ((i & 1) << 3)) for i in range(16)]
        passed.append(lax.ppermute(sums[t], "rows", pairs))
    return core_scaled, arrange([*passed, rows_permute(share(passed), 1)])


def sketch_matrix(pattern, sign_bits, block_size):
    blocks = sign_bits.shape[1]
    rows_here = sign_bits.shape[0]
    factor = jnp.repeat(pattern, block_size, axis=0) * (2 * sign_bits - 1)
    tiled_table = jnp.tile(hadamard_table(block_size), (rows_here // block_size, 1))
    expanded = factor.astype(F32)[:, :, None] * tiled_table[:, None, :]
    return expanded.reshape(rows_here, blocks * block_size)


def inner_rows(left_side, right_side):
    return lax.dot_general(left_side, right_side, (((0,), (0,)), ((), ())), precision=HIGHEST)


def local_any(unfolding, pattern, sign_bits):
    sketch_map = sketch_matrix(pattern, sign_bits, BLK)
    row_devices = lax.axis_size("rows")
    col_devices = lax.axis_size("cols")
    total_rows = unfolding.shape[0] * row_devices
    sketch = lax.psum(jnp.dot(unfolding, sketch_map, precision=HIGHEST), "cols")
    gram_matrix = lax.psum(inner_rows(sketch, sketch), "rows")
    gram_matrix = gram_matrix + float(total_rows) * jnp.eye(RANK, dtype=F32)
    lower_factor = jnp.linalg.cholesky(gram_matrix)
    basis_rows = lax.linalg.triangular_solve(lower_factor, sketch, left_side=False, lower=True, transpose_a=True)
    mode_local = MODE // col_devices
    rest_cols = unfolding.shape[1] // mode_local
    rank_share = RANK // row_devices
    reduced = lax.psum_scatter(inner_rows(basis_rows, unfolding), "rows", scatter_dimension=0, tiled=True)
    grouped = reduced.reshape(rank_share, mode_local, rest_cols)
    regrouped = lax.all_to_all(grouped, "cols", split_axis=2, concat_axis=1, tiled=True)
    return basis_rows * math.sqrt(total_rows), regrouped.reshape(rank_share * MODE, regrouped.shape[2])


def solution(mesh):
    in_specs = (P("rows", "cols"), P("cols", None), P("cols", None))
    out_specs = (P("rows", None), P("rows", "cols"))
    body = local if (mesh.shape["rows"], mesh.shape["cols"]) == (16, 2) else local_any
    return jax.shard_map(body, mesh=mesh, in_specs=in_specs, out_specs=out_specs, check_vma=False)
```

```python
import math

import jax
import jax.numpy as jnp
from jax import lax
from jax.experimental import pallas as pl
from jax.experimental.pallas import tpu as pltpu
from jax.sharding import PartitionSpec as P

RANK = 256
BLK = 128
MODE = 8
PANEL = 16
HIGHEST = lax.Precision.HIGHEST
F32 = jnp.float32
BF16 = jnp.bfloat16
VMEM = pl.BlockSpec(memory_space=pltpu.VMEM)
HBM = pl.BlockSpec(memory_space=pltpu.HBM)


def hadamard_table(table_size):
    row_index = lax.broadcasted_iota(jnp.int32, (table_size, table_size), 0)
    col_index = lax.broadcasted_iota(jnp.int32, (table_size, table_size), 1)
    both = row_index & col_index
    parity = jnp.zeros((table_size, table_size), jnp.int32)
    for bit_level in range(table_size.bit_length() - 1):
        parity = parity ^ (both >> bit_level)
    return (1 - 2 * (parity & 1)).astype(F32)


def on_chip(*dims, dtype=F32):
    return pltpu.VMEM(dims, dtype)


def held(*values):
    return [pltpu.with_memory_space_constraint(value, pltpu.VMEM) for value in values]


LIMIT = pltpu.CompilerParams(vmem_limit_bytes=8 << 20)


def cost(flops, size):
    flops, size = flops // 1000, size // 1000
    return pl.CostEstimate(flops=flops, bytes_accessed=size, transcendentals=0)


def split(value):
    high = value.astype(BF16)
    return high, (value - high.astype(F32)).astype(BF16)


def dot(left, right):
    return jnp.dot(left, right, preferred_element_type=F32)


def block_factors(k, signs, pattern, row_blocks):
    signed = (2 * signs[k : k + 1, :] - 1).astype(F32)
    return [signed[:, j * BLK : (j + 1) * BLK] * pattern[k, j].astype(F32) for j in range(row_blocks)]


def block_sketch(block_ref, here, factors, table):
    total = block_ref[here, :BLK] * factors[0]
    for j in range(1, len(factors)):
        total = total + block_ref[here, j * BLK : (j + 1) * BLK] * factors[j]
    high, rest = split(total)
    low = (total - high.astype(F32) - rest.astype(F32)).astype(BF16)
    return dot(high, table) + dot(rest, table) + dot(low, table)


def first_sketch_kernel(pattern_ref, whole_ref, sign_ref, out_ref, held_ref, sems, signs, pattern):
    steps = sems.shape[0] - 2
    step = held_ref.shape[0] // steps
    copies = [
        pltpu.make_async_copy(pattern_ref, pattern, sems.at[steps]),
        pltpu.make_async_copy(sign_ref, signs, sems.at[steps + 1]),
    ]
    for i in range(steps):
        here = pl.ds(i * step, step)
        copies.append(pltpu.make_async_copy(whole_ref.at[here], held_ref.at[here], sems.at[i]))
    for copy in copies:
        copy.start()
    table = hadamard_table(BLK).astype(BF16)
    copies[0].wait()
    copies[1].wait()
    factors = block_factors(0, signs, pattern, held_ref.shape[1] // BLK)
    for i in range(steps):
        copies[2 + i].wait()
        here = slice(i * step, (i + 1) * step)
        out_ref[here, :] = block_sketch(held_ref, here, factors, table)


def first_sketch(unfolding, pattern_rows, sign_rows):
    rows, cols = unfolding.shape
    return pl.pallas_call(
        first_sketch_kernel,
        in_specs=[HBM] * 3,
        out_specs=[VMEM] * 2,
        out_shape=[on_chip(rows, BLK), on_chip(rows, cols)],
        scratch_shapes=[
            pltpu.SemaphoreType.DMA((10,)),
            pltpu.VMEM(sign_rows.shape, jnp.int32),
            pltpu.SMEM(pattern_rows.shape, jnp.int32),
        ],
        cost_estimate=cost(rows * cols * 2, rows * cols * 4),
        compiler_params=LIMIT,
        name="first_sketch",
    )(*[pltpu.with_memory_space_constraint(x, pltpu.HBM) for x in (pattern_rows, unfolding, sign_rows)])


def second_sketch_kernel(pattern_ref, sign_ref, block_ref, out_ref, high_ref, low_ref, sems, signs, pattern):
    copies = [
        pltpu.make_async_copy(pattern_ref, pattern, sems.at[0]),
        pltpu.make_async_copy(sign_ref, signs, sems.at[1]),
    ]
    for copy in copies:
        copy.start()
    table = hadamard_table(BLK).astype(BF16)
    step = 64
    for i in range(block_ref.shape[0] // step):
        here = slice(i * step, (i + 1) * step)
        high_ref[here, :], low_ref[here, :] = split(block_ref[here, :])
    for copy in copies:
        copy.wait()
    factors = block_factors(1, signs, pattern, block_ref.shape[1] // BLK)
    for i in range(block_ref.shape[0] // step):
        here = slice(i * step, (i + 1) * step)
        out_ref[here, :] = block_sketch(block_ref, here, factors, table)


def second_sketch(block, pattern_rows, sign_rows):
    rows, cols = block.shape
    return pl.pallas_call(
        second_sketch_kernel,
        in_specs=[HBM, HBM, VMEM],
        out_specs=[VMEM] * 3,
        out_shape=[on_chip(rows, BLK), on_chip(rows, cols, dtype=BF16), on_chip(rows, cols, dtype=BF16)],
        scratch_shapes=[
            pltpu.SemaphoreType.DMA((2,)),
            pltpu.VMEM(sign_rows.shape, jnp.int32),
            pltpu.SMEM(pattern_rows.shape, jnp.int32),
        ],
        cost_estimate=cost(rows * cols * 2, rows * cols * 4),
        compiler_params=LIMIT,
        name="second_sketch",
    )(*[pltpu.with_memory_space_constraint(x, pltpu.HBM) for x in (pattern_rows, sign_rows)], *held(block))


def first_gram_kernel(own_ref, got_ref, sketch_ref, turned_ref, parts_ref, gram_ref):
    sketch = own_ref[...] + got_ref[...]
    sketch_ref[...] = sketch
    turned = sketch.T
    turned_ref[...] = turned
    parts_ref[:BLK], parts_ref[BLK:] = split(turned)
    gram_ref[...] = jnp.dot(turned, sketch, precision=HIGHEST)


def first_gram(own, got):
    rows = own.shape[0]
    return pl.pallas_call(
        first_gram_kernel,
        in_specs=[VMEM] * 2,
        out_specs=[VMEM] * 4,
        out_shape=[
            on_chip(rows, BLK),
            on_chip(BLK, rows),
            on_chip(2 * BLK, rows, dtype=BF16),
            on_chip(BLK, BLK),
        ],
        cost_estimate=cost(rows * BLK * BLK * 12, rows * BLK * 8),
        compiler_params=LIMIT,
        name="first_gram",
    )(*held(own, got))


def second_gram_kernel(own_ref, got_ref, before_ref, gram_ref, sketch_ref, parts_ref, keep_ref, send_ref, packed):
    sketch = own_ref[...] + got_ref[...]
    sketch_ref[...] = sketch
    turned = sketch.T
    parts_ref[:BLK], parts_ref[BLK:] = split(turned)
    packed[:BLK] = gram_ref[...]
    packed[BLK : 2 * BLK] = jnp.dot(before_ref[...], sketch, precision=HIGHEST)
    packed[2 * BLK :] = jnp.dot(turned, sketch, precision=HIGHEST)
    half = keep_ref.shape[0]
    core = lax.axis_index("rows") & 1
    keep_ref[...] = packed[pl.ds(pl.multiple_of(core * half, half), half), :]
    send_ref[...] = packed[pl.ds(pl.multiple_of((1 - core) * half, half), half), :]


def second_gram(own, got, before, gram, after):
    rows = own.shape[0]
    half = (3 * BLK // 2, BLK)

    def body(*refs):
        second_gram_kernel(*refs[:4], *refs[-5:])

    return pl.pallas_call(
        body,
        in_specs=[VMEM] * (4 + len(after)),
        out_specs=[VMEM] * 4,
        out_shape=[
            on_chip(rows, BLK),
            on_chip(2 * BLK, rows, dtype=BF16),
            on_chip(*half),
            on_chip(*half),
        ],
        scratch_shapes=[pltpu.VMEM((3 * BLK, BLK), F32)],
        cost_estimate=cost(rows * BLK * BLK * 24, rows * BLK * 8),
        compiler_params=LIMIT,
        name="second_gram",
    )(*held(own, got, before, gram, *after))


def project_kernel(parts_ref, high_ref, low_ref, soon_0, soon_1, keep_1, give_0, keep_0):
    row = lax.axis_index("rows")
    core, right, far = row & 1, (row >> 1) & 1, row >> 3
    near = ((row >> 2) & 1) ^ lax.axis_index("cols")
    for flip, give, keep in ((1, (soon_0, soon_1), keep_1), (0, (give_0.at[0], give_0.at[1]), keep_0)):
        for side in range(2):
            for t in range(2):
                block = (far ^ core ^ 1 ^ side) * 4 + (right ^ flip) * 2 + (near ^ t)
                here = pl.ds(pl.multiple_of(block * 2 * BLK, 2 * BLK), 2 * BLK)
                both = dot(parts_ref[...], high_ref[:, here])
                total = both[:BLK] + both[BLK:] + dot(parts_ref[:BLK, :], low_ref[:, here])
                if side == 0:
                    give[t][...] = total
                else:
                    keep[t] = total


def project(parts, high, low, after=()):
    rows, cols = high.shape

    def body(*refs):
        project_kernel(*refs[:3], *refs[-5:])

    return pl.pallas_call(
        body,
        in_specs=[VMEM] * (3 + len(after)),
        out_specs=[VMEM] * 5,
        out_shape=[on_chip(BLK, 2 * BLK)] * 2 + [on_chip(2, BLK, 2 * BLK)] * 3,
        cost_estimate=cost(rows * cols * BLK * 6, rows * cols * 4),
        compiler_params=LIMIT,
        name="project",
    )(*held(parts, high, low, *after))


def joined_kernel(keep_ref, got_0, got_1, out_ref):
    out_ref[0] = keep_ref[0] + got_0[...]
    out_ref[1] = keep_ref[1] + got_1[...]


def joined(keep, got, after):
    def body(*refs):
        joined_kernel(*refs[:3], refs[-1])

    return pl.pallas_call(
        body,
        in_specs=[VMEM] * (3 + len(after)),
        out_specs=VMEM,
        out_shape=on_chip(*keep.shape),
        cost_estimate=cost(0, keep.size * 4),
        compiler_params=LIMIT,
        name="joined",
    )(*held(keep, *got, *after))


def add_parts_kernel(terms, outs):
    for i, out in enumerate(outs):
        here = slice(None) if len(outs) == 1 else i
        total = terms[0][here]
        for term in terms[1:]:
            total = total + term[here]
        out[...] = total


def add_parts(terms, parts, after=(), hint=0):
    dims = terms[0].shape
    size = math.prod(dims)
    count = len(terms)

    def body(*refs):
        add_parts_kernel(refs[:count], refs[-parts:])

    return pl.pallas_call(
        body,
        in_specs=[VMEM] * (count + len(after)),
        out_specs=[VMEM] * parts,
        out_shape=[on_chip(*(dims if parts == 1 else dims[1:]))] * parts,
        cost_estimate=cost(size + hint, size),
        compiler_params=LIMIT,
        name="add_parts",
    )(*held(*terms, *after))


def pieces_kernel(refs, outs):
    count = len(refs) // 2
    for i, out in enumerate(outs):
        for h in range(2):
            terms = [ref[i] for ref in refs[h * count : (h + 1) * count]]
            out[h * BLK : (h + 1) * BLK] = sum(terms[1:], terms[0])


def piece_sums(first, second, after):
    terms = (*first, *second)
    count = len(terms)

    def body(*refs):
        pieces_kernel(refs[:count], refs[-2:])

    return pl.pallas_call(
        body,
        in_specs=[VMEM] * (count + len(after)),
        out_specs=[VMEM] * 2,
        out_shape=[on_chip(2 * BLK, 2 * BLK)] * 2,
        cost_estimate=cost(8 * BLK * BLK, 96 * BLK * BLK),
        compiler_params=LIMIT,
        name="piece_sums",
    )(*held(*terms, *after))


def factor_panel(parts, start):
    diagonal = parts[0][:, start : start + PANEL]
    columns = [jnp.broadcast_to(diagonal[:, k : k + 1], (PANEL, BLK)) for k in range(PANEL)]
    rows = lax.broadcasted_iota(jnp.int32, (PANEL, BLK), 0)
    pivots = jnp.ones((PANEL, BLK), F32)
    for j in range(PANEL):
        pivot = jnp.broadcast_to(columns[j][j : j + 1, :], (PANEL, BLK))
        multiplier = jnp.where(rows > j, columns[j] / pivot, 0.0)
        for k in range(j + 1, PANEL):
            columns[k] = columns[k] - multiplier * columns[k][j : j + 1, :]
        parts = [part - multiplier * part[j : j + 1, :] for part in parts]
        pivots = jnp.where(rows == j, pivot, pivots)
    scale = lax.rsqrt(pivots)
    return [part * scale for part in parts]


def factor_block(work):
    for panel in range(BLK // PANEL):
        start = panel * PANEL
        stop = start + PANEL
        parts = [work[start:stop, c * BLK : (c + 1) * BLK] for c in range(3)]
        parts = factor_panel(parts, start)
        for c in range(3):
            work[start:stop, c * BLK : (c + 1) * BLK] = parts[c]
        if stop < BLK:
            left, whole = parts[0].T, jnp.concatenate(parts, 1)
            after = min(stop + PANEL, BLK)
            work[stop:after, :] = work[stop:after, :] - jnp.dot(left[stop:after], whole, precision=HIGHEST)
            if after < BLK:
                work[after:, :] = work[after:, :] - jnp.dot(left[after:], whole, precision=HIGHEST)


def factor_kernel(total_rows, own_ref, got_ref, out_ref, work, packed):
    half = own_ref.shape[0]
    core = lax.axis_index("rows") & 1
    packed[pl.ds(pl.multiple_of(core * half, half), half), :] = own_ref[...]
    packed[pl.ds(pl.multiple_of((1 - core) * half, half), half), :] = got_ref[...]
    row = lax.broadcasted_iota(jnp.int32, (BLK, BLK), 0)
    col = lax.broadcasted_iota(jnp.int32, (BLK, BLK), 1)
    eye = (row == col).astype(F32)
    work[:, :BLK] = packed[:BLK] + float(total_rows) * eye
    work[:, BLK : 2 * BLK] = packed[BLK : 2 * BLK]
    work[:, 2 * BLK :] = eye
    factor_block(work)
    out_ref[:BLK, :BLK] = work[:, 2 * BLK :]
    out_ref[:BLK, BLK:] = jnp.zeros((BLK, BLK), F32)
    above = work[:, BLK : 2 * BLK]
    product = jnp.dot(above.T, work[:, BLK:], precision=HIGHEST)
    work[:, :BLK] = packed[2 * BLK :] + float(total_rows) * eye - product[:, :BLK]
    work[:, BLK : 2 * BLK] = -product[:, BLK:]
    work[:, 2 * BLK :] = eye
    factor_block(work)
    out_ref[BLK:, :] = work[:, BLK:]


def inverse_factor(own, got, total_rows):
    def body(*refs):
        factor_kernel(total_rows, *refs)

    return pl.pallas_call(
        body,
        in_specs=[VMEM] * 2,
        out_specs=VMEM,
        out_shape=on_chip(RANK, RANK),
        scratch_shapes=[pltpu.VMEM((BLK, 3 * BLK), F32), pltpu.VMEM((3 * BLK, BLK), F32)],
        cost_estimate=cost(1000000000000, RANK * RANK * 8),
        compiler_params=LIMIT,
        name="inverse_factor",
    )(*held(own, got))


def core_kernel(scale, first_ref, second_ref, inverse_ref, out_ref, done_ref):
    t_high, t_low = split(inverse_ref[...].T)
    s_high, s_low = split(jnp.concatenate([first_ref[...], second_ref[...]], 1))
    total = dot(s_high, t_high) + dot(s_high, t_low) + dot(s_low, t_high)
    out_ref[...] = total * scale
    done_ref[...] = total[:8, :BLK]


def scaled_core(first, second, inverse, scale):
    rows = first.shape[0]

    def body(*refs):
        core_kernel(scale, *refs)

    return pl.pallas_call(
        body,
        in_specs=[VMEM] * 3,
        out_specs=[VMEM] * 2,
        out_shape=[jax.ShapeDtypeStruct((rows, RANK), F32), on_chip(8, BLK)],
        cost_estimate=cost(rows * RANK * RANK * 6, rows * RANK * 8),
        compiler_params=LIMIT,
        name="scaled_core",
    )(*held(first, second, inverse))


def remainder_kernel(inverse_ref, p0, p1, o0, o1, o2, o3, work):
    work[...] = jnp.dot(inverse_ref[...], p0[...] + p1[...], precision=HIGHEST)
    row = lax.axis_index("rows")
    for m, out in enumerate((o0, o1, o2, o3)):
        to = (row & 3) ^ m
        for j in range(4):
            deep = (row >> 2) ^ (((to & 1) << 1) | (j >> 1))
            rank_block = (deep << 2) | (to ^ (j & 1))
            out[j] = work[pl.ds(pl.multiple_of(rank_block * 16, 16), 16), :]


def remainder_pieces(inverse, pieces):
    return pl.pallas_call(
        remainder_kernel,
        in_specs=[VMEM] * 3,
        out_specs=[VMEM] * 4,
        out_shape=[on_chip(4, 16, 2 * BLK)] * 4,
        scratch_shapes=[pltpu.VMEM((RANK, 2 * BLK), F32)],
        cost_estimate=cost(RANK * RANK * BLK * 24, RANK * BLK * 16),
        compiler_params=LIMIT,
        name="remainder_pieces",
    )(*held(inverse, *pieces))


def collect_kernel(r0, r1, r2, r3, o0, o1):
    for t, out in enumerate((o0, o1)):
        for j in range(2):
            out[j, 0] = r0[2 * t + j] + r1[2 * t + j]
            out[j, 1] = r2[2 * t + j] + r3[2 * t + j]


def collect(firsts):
    return pl.pallas_call(
        collect_kernel,
        in_specs=[VMEM] * 4,
        out_specs=[VMEM] * 2,
        out_shape=[on_chip(2, 2, 16, 2 * BLK)] * 2,
        cost_estimate=cost(0, 16 * BLK * 64),
        compiler_params=LIMIT,
        name="collect",
    )(*held(*firsts))


def share_kernel(p0, p1, after, out):
    out[0] = p0[1]
    out[1] = p1[1]


def share(pieces, after):
    return pl.pallas_call(
        share_kernel,
        in_specs=[VMEM] * 3,
        out_specs=VMEM,
        out_shape=on_chip(2, 2, 16, 2 * BLK),
        cost_estimate=cost(0, 16 * BLK * 64),
        compiler_params=LIMIT,
        name="share",
    )(*held(*pieces, after))


def arrange_kernel(p0, p1, shared, out_ref, work):
    row = lax.axis_index("rows")
    core, right, deep, y = row & 1, (row >> 1) & 1, row >> 2, lax.axis_index("cols")
    for t, ours in enumerate((p0, p1)):
        for other in range(2):
            there = deep ^ (((core ^ other) << 1) | t)
            piece = shared.at[t] if other else ours.at[0]
            for m in range(2):
                work[((there & 1) ^ y) * 4 + (there >> 1) * 2 + (right ^ m)] = piece[m]
    for mode in range(MODE):
        out_ref[:, mode, :] = work[mode]


def arrange(pieces):
    out = pl.pallas_call(
        arrange_kernel,
        in_specs=[VMEM] * 3,
        out_specs=VMEM,
        out_shape=jax.ShapeDtypeStruct((16, MODE, 2 * BLK), F32),
        scratch_shapes=[pltpu.VMEM((MODE, 16, 2 * BLK), F32)],
        cost_estimate=cost(0, 16 * BLK * 64),
        compiler_params=LIMIT,
        name="arrange",
    )(*held(*pieces))
    return out.reshape(16 * MODE, 2 * BLK)


def rows_permute(value, mask):
    size = lax.axis_size("rows")
    return lax.ppermute(value, "rows", [(i, i ^ mask) for i in range(size)])


def local(unfolding, pattern, sign_bits):
    total_rows = unfolding.shape[0] * lax.axis_size("rows")
    swap = [(0, 1), (1, 0)]
    pattern_rows, sign_rows = pattern.T, sign_bits.T
    own_0, block = first_sketch(unfolding, pattern_rows, sign_rows)
    got_0 = lax.ppermute(own_0, "cols", swap)
    own_1, high, low = second_sketch(block, pattern_rows, sign_rows)
    got_1 = lax.ppermute(own_1, "cols", swap)
    first, turned, parts, gram = first_gram(own_0, got_0)
    *give, keep, give_0, keep_0 = project(parts, high, low)
    send_0 = joined(keep, [rows_permute(g, 1) for g in give], ())
    second, parts, gram_keep, gram_send = second_gram(own_1, got_1, turned, gram, (keep_0,))
    gram, = add_parts((gram_keep, rows_permute(gram_send, 1)), 1)
    *give, keep, give_1, keep_1 = project(parts, high, low, (send_0,))
    got_0 = rows_permute(send_0, 2)
    send_1 = joined(keep, [rows_permute(g, 1) for g in give], (gram,))
    core_got, last_got = (rows_permute(give_0, 1), rows_permute(give_1, 1)), rows_permute(send_1, 2)
    gram, = add_parts((gram, rows_permute(gram, 4)), 1, (got_0,))
    gram, = add_parts((gram, rows_permute(gram, 8)), 1, hint=1000000000000)
    pieces = piece_sums((keep_0, core_got[0], got_0), (keep_1, core_got[1], last_got), (gram,))
    gram, = add_parts((gram, rows_permute(gram, 2)), 1)
    inverse = inverse_factor(gram, rows_permute(gram, 1), total_rows)
    gathered = []
    for k in range(2):
        pairs = []
        for i in range(16):
            for y in range(2):
                to = i ^ (k << 2) ^ ((i & 1) << 3)
                pairs.append((2 * i + y, 2 * to + (y ^ ((to >> 2) & 1))))
        gathered.append(lax.ppermute(pieces[k], ("rows", "cols"), pairs))
    parts = remainder_pieces(inverse, gathered)
    core_scaled, scaled = scaled_core(first, second, inverse, math.sqrt(total_rows))
    sums = collect([parts[0]] + [rows_permute(parts[m], m) for m in (1, 2, 3)])
    passed = []
    for t in range(2):
        pairs = [(i, i ^ (t << 2) ^ ((i & 1) << 3)) for i in range(16)]
        passed.append(lax.ppermute(sums[t], "rows", pairs))
    return core_scaled, arrange([*passed, rows_permute(share(passed, scaled), 1)])


def sketch_matrix(pattern, sign_bits, block_size):
    blocks = sign_bits.shape[1]
    rows_here = sign_bits.shape[0]
    factor = jnp.repeat(pattern, block_size, axis=0) * (2 * sign_bits - 1)
    tiled_table = jnp.tile(hadamard_table(block_size), (rows_here // block_size, 1))
    expanded = factor.astype(F32)[:, :, None] * tiled_table[:, None, :]
    return expanded.reshape(rows_here, blocks * block_size)


def inner_rows(left_side, right_side):
    return lax.dot_general(left_side, right_side, (((0,), (0,)), ((), ())), precision=HIGHEST)


def local_any(unfolding, pattern, sign_bits):
    sketch_map = sketch_matrix(pattern, sign_bits, BLK)
    row_devices = lax.axis_size("rows")
    col_devices = lax.axis_size("cols")
    total_rows = unfolding.shape[0] * row_devices
    sketch = lax.psum(jnp.dot(unfolding, sketch_map, precision=HIGHEST), "cols")
    gram_matrix = lax.psum(inner_rows(sketch, sketch), "rows")
    gram_matrix = gram_matrix + float(total_rows) * jnp.eye(RANK, dtype=F32)
    lower_factor = jnp.linalg.cholesky(gram_matrix)
    basis_rows = lax.linalg.triangular_solve(lower_factor, sketch, left_side=False, lower=True, transpose_a=True)
    mode_local = MODE // col_devices
    rest_cols = unfolding.shape[1] // mode_local
    rank_share = RANK // row_devices
    reduced = lax.psum_scatter(inner_rows(basis_rows, unfolding), "rows", scatter_dimension=0, tiled=True)
    grouped = reduced.reshape(rank_share, mode_local, rest_cols)
    regrouped = lax.all_to_all(grouped, "cols", split_axis=2, concat_axis=1, tiled=True)
    return basis_rows * math.sqrt(total_rows), regrouped.reshape(rank_share * MODE, regrouped.shape[2])


def solution(mesh):
    in_specs = (P("rows", "cols"), P("cols", None), P("cols", None))
    out_specs = (P("rows", None), P("rows", "cols"))
    body = local if (mesh.shape["rows"], mesh.shape["cols"]) == (16, 2) else local_any
    return jax.shard_map(body, mesh=mesh, in_specs=in_specs, out_specs=out_specs, check_vma=False)
```

```python
import math

import jax
import jax.numpy as jnp
from jax import lax
from jax.experimental import pallas as pl
from jax.experimental.pallas import tpu as pltpu
from jax.sharding import PartitionSpec as P

RANK = 256
BLK = 128
MODE = 8
PANEL = 16
HIGHEST = lax.Precision.HIGHEST
F32 = jnp.float32
BF16 = jnp.bfloat16
VMEM = pl.BlockSpec(memory_space=pltpu.VMEM)
HBM = pl.BlockSpec(memory_space=pltpu.HBM)


def hadamard_table(table_size):
    row_index = lax.broadcasted_iota(jnp.int32, (table_size, table_size), 0)
    col_index = lax.broadcasted_iota(jnp.int32, (table_size, table_size), 1)
    both = row_index & col_index
    parity = jnp.zeros((table_size, table_size), jnp.int32)
    for bit_level in range(table_size.bit_length() - 1):
        parity = parity ^ (both >> bit_level)
    return (1 - 2 * (parity & 1)).astype(F32)


def on_chip(*dims, dtype=F32):
    return pltpu.VMEM(dims, dtype)


def held(*values):
    return [pltpu.with_memory_space_constraint(value, pltpu.VMEM) for value in values]


LIMIT = pltpu.CompilerParams(vmem_limit_bytes=8 << 20)


def cost(flops, size):
    flops, size = flops // 1000, size // 1000
    return pl.CostEstimate(flops=flops, bytes_accessed=size, transcendentals=0)


def split(value):
    high = value.astype(BF16)
    return high, (value - high.astype(F32)).astype(BF16)


def dot(left, right):
    return jnp.dot(left, right, preferred_element_type=F32)


def block_factors(k, signs, pattern, row_blocks):
    signed = (2 * signs[k : k + 1, :] - 1).astype(F32)
    return [signed[:, j * BLK : (j + 1) * BLK] * pattern[k, j].astype(F32) for j in range(row_blocks)]


def block_sketch(block_ref, here, factors, table):
    total = block_ref[here, :BLK] * factors[0]
    for j in range(1, len(factors)):
        total = total + block_ref[here, j * BLK : (j + 1) * BLK] * factors[j]
    high, rest = split(total)
    low = (total - high.astype(F32) - rest.astype(F32)).astype(BF16)
    return dot(high, table) + dot(rest, table) + dot(low, table)


def first_sketch_kernel(pattern_ref, whole_ref, sign_ref, out_ref, held_ref, sems, signs, pattern):
    steps = sems.shape[0] - 2
    step = held_ref.shape[0] // steps
    copies = [
        pltpu.make_async_copy(pattern_ref, pattern, sems.at[steps]),
        pltpu.make_async_copy(sign_ref, signs, sems.at[steps + 1]),
    ]
    for i in range(steps):
        here = pl.ds(i * step, step)
        copies.append(pltpu.make_async_copy(whole_ref.at[here], held_ref.at[here], sems.at[i]))
    for copy in copies:
        copy.start()
    table = hadamard_table(BLK).astype(BF16)
    copies[0].wait()
    copies[1].wait()
    factors = block_factors(0, signs, pattern, held_ref.shape[1] // BLK)
    for i in range(steps):
        copies[2 + i].wait()
        here = slice(i * step, (i + 1) * step)
        out_ref[here, :] = block_sketch(held_ref, here, factors, table)


def first_sketch(unfolding, pattern_rows, sign_rows):
    rows, cols = unfolding.shape
    return pl.pallas_call(
        first_sketch_kernel,
        in_specs=[HBM] * 3,
        out_specs=[VMEM] * 2,
        out_shape=[on_chip(rows, BLK), on_chip(rows, cols)],
        scratch_shapes=[
            pltpu.SemaphoreType.DMA((18,)),
            pltpu.VMEM(sign_rows.shape, jnp.int32),
            pltpu.SMEM(pattern_rows.shape, jnp.int32),
        ],
        cost_estimate=cost(rows * cols * 2, rows * cols * 4),
        compiler_params=LIMIT,
        name="first_sketch",
    )(*[pltpu.with_memory_space_constraint(x, pltpu.HBM) for x in (pattern_rows, unfolding, sign_rows)])


def second_sketch_kernel(pattern_ref, sign_ref, block_ref, out_ref, high_ref, low_ref, sems, signs, pattern):
    copies = [
        pltpu.make_async_copy(pattern_ref, pattern, sems.at[0]),
        pltpu.make_async_copy(sign_ref, signs, sems.at[1]),
    ]
    for copy in copies:
        copy.start()
    table = hadamard_table(BLK).astype(BF16)
    step = 64
    for i in range(block_ref.shape[0] // step):
        here = slice(i * step, (i + 1) * step)
        high_ref[here, :], low_ref[here, :] = split(block_ref[here, :])
    for copy in copies:
        copy.wait()
    factors = block_factors(1, signs, pattern, block_ref.shape[1] // BLK)
    for i in range(block_ref.shape[0] // step):
        here = slice(i * step, (i + 1) * step)
        out_ref[here, :] = block_sketch(block_ref, here, factors, table)


def second_sketch(block, pattern_rows, sign_rows):
    rows, cols = block.shape
    return pl.pallas_call(
        second_sketch_kernel,
        in_specs=[HBM, HBM, VMEM],
        out_specs=[VMEM] * 3,
        out_shape=[on_chip(rows, BLK), on_chip(rows, cols, dtype=BF16), on_chip(rows, cols, dtype=BF16)],
        scratch_shapes=[
            pltpu.SemaphoreType.DMA((2,)),
            pltpu.VMEM(sign_rows.shape, jnp.int32),
            pltpu.SMEM(pattern_rows.shape, jnp.int32),
        ],
        cost_estimate=cost(rows * cols * 2, rows * cols * 4),
        compiler_params=LIMIT,
        name="second_sketch",
    )(*[pltpu.with_memory_space_constraint(x, pltpu.HBM) for x in (pattern_rows, sign_rows)], *held(block))


def first_gram_kernel(own_ref, got_ref, sketch_ref, turned_ref, parts_ref, gram_ref):
    sketch = own_ref[...] + got_ref[...]
    sketch_ref[...] = sketch
    turned = sketch.T
    turned_ref[...] = turned
    parts_ref[:BLK], parts_ref[BLK:] = split(turned)
    gram_ref[...] = jnp.dot(turned, sketch, precision=HIGHEST)


def first_gram(own, got):
    rows = own.shape[0]
    return pl.pallas_call(
        first_gram_kernel,
        in_specs=[VMEM] * 2,
        out_specs=[VMEM] * 4,
        out_shape=[
            on_chip(rows, BLK),
            on_chip(BLK, rows),
            on_chip(2 * BLK, rows, dtype=BF16),
            on_chip(BLK, BLK),
        ],
        cost_estimate=cost(rows * BLK * BLK * 12, rows * BLK * 8),
        compiler_params=LIMIT,
        name="first_gram",
    )(*held(own, got))


def second_gram_kernel(own_ref, got_ref, before_ref, gram_ref, sketch_ref, parts_ref, keep_ref, send_ref, packed):
    sketch = own_ref[...] + got_ref[...]
    sketch_ref[...] = sketch
    turned = sketch.T
    parts_ref[:BLK], parts_ref[BLK:] = split(turned)
    packed[:BLK] = gram_ref[...]
    packed[BLK : 2 * BLK] = jnp.dot(before_ref[...], sketch, precision=HIGHEST)
    packed[2 * BLK :] = jnp.dot(turned, sketch, precision=HIGHEST)
    half = keep_ref.shape[0]
    core = lax.axis_index("rows") & 1
    keep_ref[...] = packed[pl.ds(pl.multiple_of(core * half, half), half), :]
    send_ref[...] = packed[pl.ds(pl.multiple_of((1 - core) * half, half), half), :]


def second_gram(own, got, before, gram, after):
    rows = own.shape[0]
    half = (3 * BLK // 2, BLK)

    def body(*refs):
        second_gram_kernel(*refs[:4], *refs[-5:])

    return pl.pallas_call(
        body,
        in_specs=[VMEM] * (4 + len(after)),
        out_specs=[VMEM] * 4,
        out_shape=[
            on_chip(rows, BLK),
            on_chip(2 * BLK, rows, dtype=BF16),
            on_chip(*half),
            on_chip(*half),
        ],
        scratch_shapes=[pltpu.VMEM((3 * BLK, BLK), F32)],
        cost_estimate=cost(rows * BLK * BLK * 24, rows * BLK * 8),
        compiler_params=LIMIT,
        name="second_gram",
    )(*held(own, got, before, gram, *after))


def project_kernel(parts_ref, high_ref, low_ref, soon_0, soon_1, keep_1, give_0, keep_0):
    row = lax.axis_index("rows")
    core, right, far = row & 1, (row >> 1) & 1, row >> 3
    near = ((row >> 2) & 1) ^ lax.axis_index("cols")
    for flip, give, keep in ((1, (soon_0, soon_1), keep_1), (0, (give_0.at[0], give_0.at[1]), keep_0)):
        for side in range(2):
            for t in range(2):
                block = (far ^ core ^ 1 ^ side) * 4 + (right ^ flip) * 2 + (near ^ t)
                here = pl.ds(pl.multiple_of(block * 2 * BLK, 2 * BLK), 2 * BLK)
                both = dot(parts_ref[...], high_ref[:, here])
                total = both[:BLK] + both[BLK:] + dot(parts_ref[:BLK, :], low_ref[:, here])
                if side == 0:
                    give[t][...] = total
                else:
                    keep[t] = total


def project(parts, high, low, after=()):
    rows, cols = high.shape

    def body(*refs):
        project_kernel(*refs[:3], *refs[-5:])

    return pl.pallas_call(
        body,
        in_specs=[VMEM] * (3 + len(after)),
        out_specs=[VMEM] * 5,
        out_shape=[on_chip(BLK, 2 * BLK)] * 2 + [on_chip(2, BLK, 2 * BLK)] * 3,
        cost_estimate=cost(rows * cols * BLK * 6, rows * cols * 4),
        compiler_params=LIMIT,
        name="project",
    )(*held(parts, high, low, *after))


def joined_kernel(keep_ref, got_0, got_1, out_ref):
    out_ref[0] = keep_ref[0] + got_0[...]
    out_ref[1] = keep_ref[1] + got_1[...]


def joined(keep, got, after):
    def body(*refs):
        joined_kernel(*refs[:3], refs[-1])

    return pl.pallas_call(
        body,
        in_specs=[VMEM] * (3 + len(after)),
        out_specs=VMEM,
        out_shape=on_chip(*keep.shape),
        cost_estimate=cost(0, keep.size * 4),
        compiler_params=LIMIT,
        name="joined",
    )(*held(keep, *got, *after))


def add_parts_kernel(terms, outs):
    for i, out in enumerate(outs):
        here = slice(None) if len(outs) == 1 else i
        total = terms[0][here]
        for term in terms[1:]:
            total = total + term[here]
        out[...] = total


def add_parts(terms, parts, after=(), hint=0):
    dims = terms[0].shape
    size = math.prod(dims)
    count = len(terms)

    def body(*refs):
        add_parts_kernel(refs[:count], refs[-parts:])

    return pl.pallas_call(
        body,
        in_specs=[VMEM] * (count + len(after)),
        out_specs=[VMEM] * parts,
        out_shape=[on_chip(*(dims if parts == 1 else dims[1:]))] * parts,
        cost_estimate=cost(size + hint, size),
        compiler_params=LIMIT,
        name="add_parts",
    )(*held(*terms, *after))


def pieces_kernel(refs, outs):
    count = len(refs) // 2
    for i, out in enumerate(outs):
        for h in range(2):
            terms = [ref[i] for ref in refs[h * count : (h + 1) * count]]
            out[h * BLK : (h + 1) * BLK] = sum(terms[1:], terms[0])


def piece_sums(first, second, after):
    terms = (*first, *second)
    count = len(terms)

    def body(*refs):
        pieces_kernel(refs[:count], refs[-2:])

    return pl.pallas_call(
        body,
        in_specs=[VMEM] * (count + len(after)),
        out_specs=[VMEM] * 2,
        out_shape=[on_chip(2 * BLK, 2 * BLK)] * 2,
        cost_estimate=cost(8 * BLK * BLK, 96 * BLK * BLK),
        compiler_params=LIMIT,
        name="piece_sums",
    )(*held(*terms, *after))


def factor_panel(parts, start):
    diagonal = parts[0][:, start : start + PANEL]
    columns = [jnp.broadcast_to(diagonal[:, k : k + 1], (PANEL, BLK)) for k in range(PANEL)]
    rows = lax.broadcasted_iota(jnp.int32, (PANEL, BLK), 0)
    pivots = jnp.ones((PANEL, BLK), F32)
    for j in range(PANEL):
        pivot = jnp.broadcast_to(columns[j][j : j + 1, :], (PANEL, BLK))
        multiplier = jnp.where(rows > j, columns[j] / pivot, 0.0)
        for k in range(j + 1, PANEL):
            columns[k] = columns[k] - multiplier * columns[k][j : j + 1, :]
        parts = [part - multiplier * part[j : j + 1, :] for part in parts]
        pivots = jnp.where(rows == j, pivot, pivots)
    scale = lax.rsqrt(pivots)
    return [part * scale for part in parts]


def factor_block(work):
    for panel in range(BLK // PANEL):
        start = panel * PANEL
        stop = start + PANEL
        parts = [work[start:stop, c * BLK : (c + 1) * BLK] for c in range(3)]
        parts = factor_panel(parts, start)
        for c in range(3):
            work[start:stop, c * BLK : (c + 1) * BLK] = parts[c]
        if stop < BLK:
            left, whole = parts[0].T, jnp.concatenate(parts, 1)
            after = min(stop + PANEL, BLK)
            work[stop:after, :] = work[stop:after, :] - jnp.dot(left[stop:after], whole, precision=HIGHEST)
            if after < BLK:
                work[after:, :] = work[after:, :] - jnp.dot(left[after:], whole, precision=HIGHEST)


def factor_kernel(total_rows, own_ref, got_ref, out_ref, work, packed):
    half = own_ref.shape[0]
    core = lax.axis_index("rows") & 1
    packed[pl.ds(pl.multiple_of(core * half, half), half), :] = own_ref[...]
    packed[pl.ds(pl.multiple_of((1 - core) * half, half), half), :] = got_ref[...]
    row = lax.broadcasted_iota(jnp.int32, (BLK, BLK), 0)
    col = lax.broadcasted_iota(jnp.int32, (BLK, BLK), 1)
    eye = (row == col).astype(F32)
    work[:, :BLK] = packed[:BLK] + float(total_rows) * eye
    work[:, BLK : 2 * BLK] = packed[BLK : 2 * BLK]
    work[:, 2 * BLK :] = eye
    factor_block(work)
    out_ref[:BLK, :BLK] = work[:, 2 * BLK :]
    out_ref[:BLK, BLK:] = jnp.zeros((BLK, BLK), F32)
    above = work[:, BLK : 2 * BLK]
    product = jnp.dot(above.T, work[:, BLK:], precision=HIGHEST)
    work[:, :BLK] = packed[2 * BLK :] + float(total_rows) * eye - product[:, :BLK]
    work[:, BLK : 2 * BLK] = -product[:, BLK:]
    work[:, 2 * BLK :] = eye
    factor_block(work)
    out_ref[BLK:, :] = work[:, BLK:]


def inverse_factor(own, got, total_rows):
    def body(*refs):
        factor_kernel(total_rows, *refs)

    return pl.pallas_call(
        body,
        in_specs=[VMEM] * 2,
        out_specs=VMEM,
        out_shape=on_chip(RANK, RANK),
        scratch_shapes=[pltpu.VMEM((BLK, 3 * BLK), F32), pltpu.VMEM((3 * BLK, BLK), F32)],
        cost_estimate=cost(1000000000000, RANK * RANK * 8),
        compiler_params=LIMIT,
        name="inverse_factor",
    )(*held(own, got))


def core_kernel(scale, first_ref, second_ref, inverse_ref, out_ref, done_ref):
    t_high, t_low = split(inverse_ref[...].T)
    s_high, s_low = split(jnp.concatenate([first_ref[...], second_ref[...]], 1))
    total = dot(s_high, t_high) + dot(s_high, t_low) + dot(s_low, t_high)
    out_ref[...] = total * scale
    done_ref[...] = total[:8, :BLK]


def scaled_core(first, second, inverse, scale):
    rows = first.shape[0]

    def body(*refs):
        core_kernel(scale, *refs)

    return pl.pallas_call(
        body,
        in_specs=[VMEM] * 3,
        out_specs=[VMEM] * 2,
        out_shape=[jax.ShapeDtypeStruct((rows, RANK), F32), on_chip(8, BLK)],
        cost_estimate=cost(rows * RANK * RANK * 6, rows * RANK * 8),
        compiler_params=LIMIT,
        name="scaled_core",
    )(*held(first, second, inverse))


def remainder_kernel(inverse_ref, p0, p1, o0, o1, o2, o3, work):
    work[...] = jnp.dot(inverse_ref[...], p0[...] + p1[...], precision=HIGHEST)
    row = lax.axis_index("rows")
    for m, out in enumerate((o0, o1, o2, o3)):
        to = (row & 3) ^ m
        for j in range(4):
            deep = (row >> 2) ^ (((to & 1) << 1) | (j >> 1))
            rank_block = (deep << 2) | (to ^ (j & 1))
            out[j] = work[pl.ds(pl.multiple_of(rank_block * 16, 16), 16), :]


def remainder_pieces(inverse, pieces):
    return pl.pallas_call(
        remainder_kernel,
        in_specs=[VMEM] * 3,
        out_specs=[VMEM] * 4,
        out_shape=[on_chip(4, 16, 2 * BLK)] * 4,
        scratch_shapes=[pltpu.VMEM((RANK, 2 * BLK), F32)],
        cost_estimate=cost(RANK * RANK * BLK * 24, RANK * BLK * 16),
        compiler_params=LIMIT,
        name="remainder_pieces",
    )(*held(inverse, *pieces))


def collect_kernel(r0, r1, r2, r3, o0, o1):
    for t, out in enumerate((o0, o1)):
        for j in range(2):
            out[j, 0] = r0[2 * t + j] + r1[2 * t + j]
            out[j, 1] = r2[2 * t + j] + r3[2 * t + j]


def collect(firsts):
    return pl.pallas_call(
        collect_kernel,
        in_specs=[VMEM] * 4,
        out_specs=[VMEM] * 2,
        out_shape=[on_chip(2, 2, 16, 2 * BLK)] * 2,
        cost_estimate=cost(0, 16 * BLK * 64),
        compiler_params=LIMIT,
        name="collect",
    )(*held(*firsts))


def share_kernel(p0, p1, after, out):
    out[0] = p0[1]
    out[1] = p1[1]


def share(pieces, after):
    return pl.pallas_call(
        share_kernel,
        in_specs=[VMEM] * 3,
        out_specs=VMEM,
        out_shape=on_chip(2, 2, 16, 2 * BLK),
        cost_estimate=cost(0, 16 * BLK * 64),
        compiler_params=LIMIT,
        name="share",
    )(*held(*pieces, after))


def arrange_kernel(p0, p1, shared, out_ref, work):
    row = lax.axis_index("rows")
    core, right, deep, y = row & 1, (row >> 1) & 1, row >> 2, lax.axis_index("cols")
    for t, ours in enumerate((p0, p1)):
        for other in range(2):
            there = deep ^ (((core ^ other) << 1) | t)
            piece = shared.at[t] if other else ours.at[0]
            for m in range(2):
                work[((there & 1) ^ y) * 4 + (there >> 1) * 2 + (right ^ m)] = piece[m]
    for mode in range(MODE):
        out_ref[:, mode, :] = work[mode]


def arrange(pieces):
    out = pl.pallas_call(
        arrange_kernel,
        in_specs=[VMEM] * 3,
        out_specs=VMEM,
        out_shape=jax.ShapeDtypeStruct((16, MODE, 2 * BLK), F32),
        scratch_shapes=[pltpu.VMEM((MODE, 16, 2 * BLK), F32)],
        cost_estimate=cost(0, 16 * BLK * 64),
        compiler_params=LIMIT,
        name="arrange",
    )(*held(*pieces))
    return out.reshape(16 * MODE, 2 * BLK)


def rows_permute(value, mask):
    size = lax.axis_size("rows")
    return lax.ppermute(value, "rows", [(i, i ^ mask) for i in range(size)])


def local(unfolding, pattern, sign_bits):
    total_rows = unfolding.shape[0] * lax.axis_size("rows")
    swap = [(0, 1), (1, 0)]
    pattern_rows, sign_rows = pattern.T, sign_bits.T
    own_0, block = first_sketch(unfolding, pattern_rows, sign_rows)
    got_0 = lax.ppermute(own_0, "cols", swap)
    own_1, high, low = second_sketch(block, pattern_rows, sign_rows)
    got_1 = lax.ppermute(own_1, "cols", swap)
    first, turned, parts, gram = first_gram(own_0, got_0)
    *give, keep, give_0, keep_0 = project(parts, high, low)
    send_0 = joined(keep, [rows_permute(g, 1) for g in give], ())
    second, parts, gram_keep, gram_send = second_gram(own_1, got_1, turned, gram, (keep_0,))
    gram, = add_parts((gram_keep, rows_permute(gram_send, 1)), 1)
    *give, keep, give_1, keep_1 = project(parts, high, low, (send_0,))
    got_0 = rows_permute(send_0, 2)
    send_1 = joined(keep, [rows_permute(g, 1) for g in give], (gram,))
    core_got, last_got = (rows_permute(give_0, 1), rows_permute(give_1, 1)), rows_permute(send_1, 2)
    gram, = add_parts((gram, rows_permute(gram, 4)), 1, (got_0,))
    gram, = add_parts((gram, rows_permute(gram, 8)), 1, hint=1000000000000)
    pieces = piece_sums((keep_0, core_got[0], got_0), (keep_1, core_got[1], last_got), (gram,))
    gram, = add_parts((gram, rows_permute(gram, 2)), 1)
    inverse = inverse_factor(gram, rows_permute(gram, 1), total_rows)
    gathered = []
    for k in range(2):
        pairs = []
        for i in range(16):
            for y in range(2):
                to = i ^ (k << 2) ^ ((i & 1) << 3)
                pairs.append((2 * i + y, 2 * to + (y ^ ((to >> 2) & 1))))
        gathered.append(lax.ppermute(pieces[k], ("rows", "cols"), pairs))
    parts = remainder_pieces(inverse, gathered)
    core_scaled, scaled = scaled_core(first, second, inverse, math.sqrt(total_rows))
    sums = collect([parts[0]] + [rows_permute(parts[m], m) for m in (1, 2, 3)])
    passed = []
    for t in range(2):
        pairs = [(i, i ^ (t << 2) ^ ((i & 1) << 3)) for i in range(16)]
        passed.append(lax.ppermute(sums[t], "rows", pairs))
    return core_scaled, arrange([*passed, rows_permute(share(passed, scaled), 1)])


def sketch_matrix(pattern, sign_bits, block_size):
    blocks = sign_bits.shape[1]
    rows_here = sign_bits.shape[0]
    factor = jnp.repeat(pattern, block_size, axis=0) * (2 * sign_bits - 1)
    tiled_table = jnp.tile(hadamard_table(block_size), (rows_here // block_size, 1))
    expanded = factor.astype(F32)[:, :, None] * tiled_table[:, None, :]
    return expanded.reshape(rows_here, blocks * block_size)


def inner_rows(left_side, right_side):
    return lax.dot_general(left_side, right_side, (((0,), (0,)), ((), ())), precision=HIGHEST)


def local_any(unfolding, pattern, sign_bits):
    sketch_map = sketch_matrix(pattern, sign_bits, BLK)
    row_devices = lax.axis_size("rows")
    col_devices = lax.axis_size("cols")
    total_rows = unfolding.shape[0] * row_devices
    sketch = lax.psum(jnp.dot(unfolding, sketch_map, precision=HIGHEST), "cols")
    gram_matrix = lax.psum(inner_rows(sketch, sketch), "rows")
    gram_matrix = gram_matrix + float(total_rows) * jnp.eye(RANK, dtype=F32)
    lower_factor = jnp.linalg.cholesky(gram_matrix)
    basis_rows = lax.linalg.triangular_solve(lower_factor, sketch, left_side=False, lower=True, transpose_a=True)
    mode_local = MODE // col_devices
    rest_cols = unfolding.shape[1] // mode_local
    rank_share = RANK // row_devices
    reduced = lax.psum_scatter(inner_rows(basis_rows, unfolding), "rows", scatter_dimension=0, tiled=True)
    grouped = reduced.reshape(rank_share, mode_local, rest_cols)
    regrouped = lax.all_to_all(grouped, "cols", split_axis=2, concat_axis=1, tiled=True)
    return basis_rows * math.sqrt(total_rows), regrouped.reshape(rank_share * MODE, regrouped.shape[2])


def solution(mesh):
    in_specs = (P("rows", "cols"), P("cols", None), P("cols", None))
    out_specs = (P("rows", None), P("rows", "cols"))
    body = local if (mesh.shape["rows"], mesh.shape["cols"]) == (16, 2) else local_any
    return jax.shard_map(body, mesh=mesh, in_specs=in_specs, out_specs=out_specs, check_vma=False)
```
